128 devices in a mesh: req: 8 (over y, core), tok: 16 (over x, z).
Axes of the slice: x: 4, y: 4, z: 4, core: 2. Of those that a mesh axis runs over, the one named last changes fastest.
Arguments:
- layer_input: bfloat16 [16384, 2048], P(('req', 'tok')), may hold values from -12 to 12
- q_in: bfloat16 [16384, 2048], P(('req', 'tok')), may hold values from -10 to 10
- k_in: bfloat16 [16384, 2048], P(('req', 'tok')), may hold values from -10 to 10
- v_in: bfloat16 [16384, 2048], P(('req', 'tok')), may hold values from -6 to 6
- segment_ids: int32 [8, 2048], P('req'), may hold values from 0 to 3, never falling along the last dimension, each value on 1 to 1024 neighbouring positions
- lambda_parts: float32 [4, 128], replicated, may hold values from -0.8 to 0.8
- out_weight: bfloat16 [2048, 2048], replicated, may hold values from -0.125 to 0.125
- ffn_gain: float32 [2048], replicated, may hold values from 0.1 to 1.9
- gate_weight: bfloat16 [2048, 5632], P(None, 'req'), may hold values from -0.125 to 0.125
- up_weight: bfloat16 [2048, 5632], P(None, 'req'), may hold values from -0.125 to 0.125
- down_weight: bfloat16 [5632, 2048], P('req'), may hold values from -0.078125 to 0.078125
- next_gain: float32 [2048], replicated, may hold values from 0.1 to 1.9
- qkv_weight: bfloat16 [2048, 6144], P(None, 'req'), may hold values from -0.125 to 0.125
- page_owner: int32 [8, 256], P('req'), may hold values from 0 to 15, as said below
- page_slot: int32 [8, 256], P('req'), may hold values from 0 to 15, as said below
Outputs:
- layer_output: bfloat16 [16384, 2048], P(('req', 'tok'))
- q_next: bfloat16 [16384, 2048], P(('req', 'tok'))
- page_cache: bfloat16 [2048, 8, 4096], P(('req', 'tok'))
The draws below stay inside these ranges and needn't reach their ends.
Inputs may be any that keep to these rules, and one draw needn't show every extreme that they name: `segment_ids`: segment numbers never fall along a group; each of the 4 prompts of a group has 1 to 1024 tokens, one exactly 1024. `page_owner`: the 16 pages of each device name every device of its request group as owner exactly once. `page_slot`: within a request group every pair of owner and slot is named by exactly one page.
All inputs are finite; a program needn't handle non-finite values.
Results may differ from the reference program's by a relative error of at most 0.017.
Values may be sent and summed in bfloat16 or wider, within the bound.
A program may use at most 192 MiB of HBM per device.

```python
import math
import jax
import jax.numpy as jnp
import numpy as np
from jax import lax

D = 2048
HEADS = 8
HD = 128
FF = 5632
PAGE = 8
SEGS = 4
QW = 2048
GROUP = 2048
TOKENS = 16384
PAGES_DEV = 16
NPAGES = 2048
REQS = 8
PEERS = 16
CPAGES = 256
N_REQ = 8
N_TOK = 16


def query_key(key):
    query_draw = jnp.clip(jax.random.normal(jax.random.fold_in(key, 1), (TOKENS, QW), jnp.float32), -6.0, 6.0)
    key_draw = jnp.clip(jax.random.normal(jax.random.fold_in(key, 2), (TOKENS, QW), jnp.float32), -6.0, 6.0)
    return (query_draw, key_draw)


def draw_q_in(key, part):
    return query_key(key)[0].astype(jnp.bfloat16)


def draw_k_in(key, part):
    return query_key(key)[1].astype(jnp.bfloat16)


def draw_layer_input(key, part):
    columns = 0.3 * jnp.exp(jax.random.uniform(jax.random.fold_in(key, 6), (D,), jnp.float32, 0.0, math.log(10.0)))
    values = jax.random.normal(jax.random.fold_in(key, 7), (TOKENS, D), jnp.float32)
    return jnp.clip(values * columns[None, :], -12.0, 12.0).astype(jnp.bfloat16)


def page_tables(key):
    owner_keys = jax.random.split(jax.random.fold_in(key, 11), REQS * PEERS)
    page_perm = jax.vmap(lambda sub_key: jax.random.permutation(sub_key, PAGES_DEV))(owner_keys).reshape(REQS, PEERS, PAGES_DEV)
    owner_table = page_perm % PEERS
    rank_index = page_perm // PEERS
    slot_keys = jax.random.split(jax.random.fold_in(key, 12), REQS * PEERS)
    slot_perm = jax.vmap(lambda sub_key: jax.random.permutation(sub_key, PAGES_DEV))(slot_keys).reshape(REQS, PEERS, PAGES_DEV)
    sources = jnp.arange(PEERS)[None, :, None]
    group_index = jnp.arange(REQS)[:, None, None]
    position = sources * (PAGES_DEV // PEERS) + rank_index
    slot_table = slot_perm[group_index, owner_table, position]
    return (owner_table.reshape(REQS, CPAGES).astype(jnp.int32), slot_table.reshape(REQS, CPAGES).astype(jnp.int32))


def draw_page_owner(key, part):
    return page_tables(key)[0]


def draw_page_slot(key, part):
    return page_tables(key)[1]


def steps_of(own_key, dims, pieces, smallest, high):
    loudness = 1.0
    for dim, shards_of in pieces:
        steps = jax.random.uniform(jax.random.fold_in(jax.random.fold_in(own_key, 6), dim), (shards_of,), jnp.float32, smallest / len(pieces), high / len(pieces))
        loudness = loudness * jnp.repeat(jnp.exp(steps), dims[dim] // shards_of).reshape((-1,) + (1,) * (len(dims) - 1 - dim))
    return loudness


def length_profile(amount, total, reach, slope):
    portions = [(1 << 20) // math.isqrt(grade ** slope) + 1 for grade in range(2, amount + 1)]
    spare, given = total - reach - (amount - 1), [1] * (amount - 1)
    while spare > 0:
        free = [i for i in range(amount - 1) if given[i] < reach]
        pool, left = sum([portions[i] for i in free]), spare
        for i in free:
            addition = min(reach - given[i], max(1, left * portions[i] // pool), spare)
            given[i] = given[i] + addition
            spare = spare - addition
    return np.array([reach] + given)


def uneven_parts(stream_key, count, total, most, slope):
    if count == 2:
        one = jax.random.randint(stream_key, (), max(1, total - most), min(most, total - 1) + 1)
        return jnp.stack([one, total - one])
    sizes = jnp.asarray(length_profile(count, total, most, slope), jnp.int32)
    couples = (count - 1) // 2
    donor, receiver = sizes[1:1 + 2 * couples:2], sizes[2:2 + 2 * couples:2]
    margin = jnp.minimum(donor - 1, most - receiver)
    passed = jax.random.randint(jax.random.fold_in(stream_key, 1), (couples,), 0, 1 << 20) % (margin + 1)
    sizes = sizes.at[1:1 + 2 * couples:2].set(donor - passed).at[2:2 + 2 * couples:2].set(receiver + passed)
    return sizes[jax.random.permutation(jax.random.fold_in(stream_key, 2), count)]


def scatter_about(key, dims, deviation, limit, shards=(), kind=jnp.bfloat16):
    result = jax.random.normal(key, dims, jnp.float32) * deviation
    if len(shards) > 0:
        result = steps_of(key, dims, shards, -0.22, 0.18) * result
    return jnp.clip(result, min=-limit, max=limit).astype(kind)


def setup_inputs(seed: int = 0) -> dict:
    keys = jax.random.split(jax.random.key(seed), 16)
    return {
        "layer_input": draw_layer_input(jax.random.fold_in(keys[15], 71), 0),
        "q_in": draw_q_in(jax.random.fold_in(keys[15], 71), 0),
        "k_in": draw_k_in(jax.random.fold_in(keys[15], 71), 0),
        "v_in": scatter_about(keys[3], (TOKENS, QW), 1.0, 6.0, ((0, 128),)),
        "segment_ids": jax.vmap(lambda own: jnp.searchsorted(jnp.cumsum(uneven_parts(own, SEGS, GROUP, GROUP // 2, 2)), jnp.arange(GROUP), side="right"))(jax.random.split(keys[4], REQS)).reshape((REQS, GROUP)).astype(jnp.int32),
        "lambda_parts": scatter_about(keys[5], (4, HD), 0.2, 0.8, (), jnp.float32),
        "out_weight": scatter_about(keys[6], (QW, D), QW ** -0.5, 0.125),
        "ffn_gain": jnp.clip(1.0 + 0.18 * jax.random.normal(keys[7], (D,), jnp.float32), 0.1, 1.9),
        "gate_weight": scatter_about(keys[8], (D, FF), D ** -0.5, 0.125, ((1, 8),)),
        "up_weight": scatter_about(keys[9], (D, FF), D ** -0.5, 0.125, ((1, 8),)),
        "down_weight": scatter_about(keys[10], (FF, D), FF ** -0.5, 0.078125, ((0, 8),)),
        "next_gain": jnp.clip(1.0 + 0.18 * jax.random.normal(keys[11], (D,), jnp.float32), 0.1, 1.9),
        "qkv_weight": scatter_about(keys[12], (D, 3 * QW), D ** -0.5, 0.125, ((1, 8),)),
        "page_owner": draw_page_owner(jax.random.fold_in(keys[15], 71), 0),
        "page_slot": draw_page_slot(jax.random.fold_in(keys[15], 71), 0),
    }


NEG_FILL = -1e+30
LAMBDA_INIT = 0.2
EPSILON = 1e-05

def rms_rows(values):
    return values * lax.rsqrt(lax.optimization_barrier(jnp.mean(values * values, axis=-1, keepdims=True)) + EPSILON)

def lambda_value(lambda_parts):
    first_term = jnp.exp(jnp.sum(lambda_parts[0] * lambda_parts[1]))
    second_term = jnp.exp(jnp.sum(lambda_parts[2] * lambda_parts[3]))
    return first_term - second_term + LAMBDA_INIT

def group_attention(query_rows, key_rows, value_rows, seg_row, lambda_mix):
    places = jnp.arange(GROUP)
    visible = (seg_row[:, None] == seg_row[None, :]) & (places[None, :] <= places[:, None])
    score_scale = 1.0 / math.sqrt(HD)

    def one_head(head_index):
        query_head = lax.dynamic_slice_in_dim(query_rows, head_index * 2 * HD, 2 * HD, 1)
        key_head = lax.dynamic_slice_in_dim(key_rows, head_index * 2 * HD, 2 * HD, 1)
        value_head = lax.dynamic_slice_in_dim(value_rows, head_index * 2 * HD, 2 * HD, 1)
        map_outputs = []
        for map_index in range(2):
            query_map = query_head[:, map_index * HD:(map_index + 1) * HD]
            key_map = key_head[:, map_index * HD:(map_index + 1) * HD]
            scores = jnp.dot(query_map, key_map.T, preferred_element_type=jnp.float32) * score_scale
            scores = jnp.where(visible, scores, NEG_FILL)
            row_max = lax.optimization_barrier(jnp.max(scores, axis=1, keepdims=True))
            weights = jnp.where(visible, jnp.exp(scores - row_max), 0.0)
            totals = lax.optimization_barrier(jnp.sum(weights, axis=1, keepdims=True))
            map_out = jnp.dot(weights.astype(jnp.bfloat16), value_head, preferred_element_type=jnp.float32) / totals
            map_outputs.append(map_out)
        difference = map_outputs[0] - lambda_mix * map_outputs[1]
        return rms_rows(difference) * (1.0 - LAMBDA_INIT)
    head_outputs = lax.map(one_head, jnp.arange(HEADS))
    return jnp.transpose(head_outputs, (1, 0, 2)).reshape(GROUP, QW).astype(jnp.bfloat16)

def reference(layer_input, q_in, k_in, v_in, segment_ids, lambda_parts, out_weight, ffn_gain, gate_weight, up_weight, down_weight, next_gain, qkv_weight, page_owner, page_slot):
    lambda_mix = lambda_value(lambda_parts)
    query_groups = q_in.reshape(N_REQ, GROUP, QW)
    key_groups = k_in.reshape(N_REQ, GROUP, QW)
    value_groups = v_in.reshape(N_REQ, GROUP, QW)

    def per_group(group_items):
        return group_attention(group_items[0], group_items[1], group_items[2], group_items[3], lambda_mix)
    attention = lax.map(per_group, (query_groups, key_groups, value_groups, segment_ids)).reshape(TOKENS, QW)
    residual_mid = (layer_input.astype(jnp.float32) + jnp.dot(attention, out_weight, preferred_element_type=jnp.float32)).astype(jnp.bfloat16)

    def feed_forward(row_block):
        normed = (rms_rows(row_block.astype(jnp.float32)) * ffn_gain).astype(jnp.bfloat16)
        gate_proj = jnp.dot(normed, gate_weight, preferred_element_type=jnp.float32)
        up_proj = jnp.dot(normed, up_weight, preferred_element_type=jnp.float32)
        hidden = (jax.nn.silu(gate_proj) * up_proj).astype(jnp.bfloat16)
        ffn_out = jnp.dot(hidden, down_weight, preferred_element_type=jnp.float32)
        return (row_block.astype(jnp.float32) + ffn_out).astype(jnp.bfloat16)
    layer_output = lax.map(feed_forward, residual_mid.reshape(N_REQ, GROUP, D)).reshape(TOKENS, D)
    next_normed = (rms_rows(layer_output.astype(jnp.float32)) * next_gain).astype(jnp.bfloat16)
    projected = jnp.dot(next_normed, qkv_weight, preferred_element_type=jnp.float32).astype(jnp.bfloat16)
    q_next = projected[:, :QW]
    key_values = projected[:, QW:].reshape(NPAGES, PAGE, 2 * QW)
    group_index = jnp.arange(N_REQ, dtype=jnp.int32)[:, None]
    targets = ((group_index * N_TOK + page_owner) * PAGES_DEV + page_slot).reshape(NPAGES).astype(jnp.int32)
    page_cache = jnp.zeros((NPAGES, PAGE, 2 * QW), jnp.bfloat16).at[targets].set(key_values)
    return (layer_output, q_next, page_cache)
```

```python
import math

import jax
import jax.numpy as jnp
from jax import lax
from jax.sharding import PartitionSpec as P

HEADS = 8
PAGE = 8


NEG_FILL = -1e30
LAMBDA_INIT = 0.2
EPSILON = 1e-05
MAX_SEG = 1024


def rms_rows(values):
    return values * lax.rsqrt(jnp.mean(values * values, axis=-1, keepdims=True) + EPSILON)


def lambda_value(lambda_parts):
    first_term = jnp.exp(jnp.sum(lambda_parts[0] * lambda_parts[1]))
    second_term = jnp.exp(jnp.sum(lambda_parts[2] * lambda_parts[3]))
    return first_term - second_term + LAMBDA_INIT


def body(
    layer_input,
    q_in,
    k_in,
    v_in,
    segment_ids,
    lambda_parts,
    out_weight,
    ffn_gain,
    gate_weight,
    up_weight,
    down_weight,
    next_gain,
    qkv_weight,
    page_owner,
    page_slot,
):
    row_count = q_in.shape[0]
    feat_width = q_in.shape[1]
    head_dim = feat_width // (2 * HEADS)
    peer_count = lax.axis_size("tok")
    tok_place = lax.axis_index("tok")
    seg_row = segment_ids[0]
    first_row = tok_place * row_count
    query_places = first_row + jnp.arange(row_count)
    query_segs = lax.dynamic_slice_in_dim(seg_row, first_row, row_count)
    lambda_mix = lambda_value(lambda_parts)
    score_scale = 1.0 / math.sqrt(head_dim)
    query_split = q_in.reshape(row_count, HEADS, 2, head_dim)
    run_max = jnp.full((HEADS, 2, row_count), NEG_FILL, jnp.float32)
    back = -(-(MAX_SEG - 1) // row_count)
    own_kv = jnp.concatenate([k_in, v_in], axis=1)
    pieces = []
    for shift in range(back, 0, -1):
        pairs = [(src_i, src_i + shift) for src_i in range(peer_count - shift)]
        pieces.append(lax.ppermute(own_kv, "tok", perm=pairs))
    pieces.append(own_kv)
    window = jnp.concatenate(pieces, axis=0)
    piece_len = window.shape[0]
    key_rows = window[:, :feat_width]
    value_rows = window[:, feat_width:]
    key_split = key_rows.reshape(piece_len, HEADS, 2, head_dim)
    value_split = value_rows.reshape(piece_len, HEADS, 2 * head_dim)
    key_places = (tok_place - back) * row_count + jnp.arange(piece_len)
    key_segs = jnp.take(seg_row, jnp.clip(key_places, 0, seg_row.shape[0] - 1))
    visible = (
        (key_places[None, :] >= 0)
        & (key_segs[None, :] == query_segs[:, None])
        & (key_places[None, :] <= query_places[:, None])
    )
    scores = (
        jnp.einsum("qhmd,khmd->hmqk", query_split, key_split, preferred_element_type=jnp.float32)
        * score_scale
    )
    scores = jnp.where(visible, scores, NEG_FILL)
    new_max = jnp.maximum(run_max, jnp.max(scores, axis=-1))
    weights = jnp.where(visible, jnp.exp(scores - new_max[..., None]), 0.0)
    totals = jnp.sum(weights, axis=-1)
    weighted = jnp.einsum(
        "hmqk,khe->hmqe",
        weights.astype(jnp.bfloat16),
        value_split,
        preferred_element_type=jnp.float32,
    )
    run_max, totals, weighted = (new_max, totals, weighted)
    map_outputs = weighted / totals[..., None]
    difference = map_outputs[:, 0] - lambda_mix * map_outputs[:, 1]
    head_outputs = rms_rows(difference) * (1.0 - LAMBDA_INIT)
    attention = (
        jnp.transpose(head_outputs, (1, 0, 2)).reshape(row_count, feat_width).astype(jnp.bfloat16)
    )
    residual_mid = (
        layer_input.astype(jnp.float32)
        + jnp.dot(attention, out_weight, preferred_element_type=jnp.float32)
    ).astype(jnp.bfloat16)
    gathered = lax.all_gather(residual_mid, "req", axis=0, tiled=True)
    normed = (rms_rows(gathered.astype(jnp.float32)) * ffn_gain).astype(jnp.bfloat16)
    gate_proj = jnp.dot(normed, gate_weight, preferred_element_type=jnp.float32)
    up_proj = jnp.dot(normed, up_weight, preferred_element_type=jnp.float32)
    hidden = (jax.nn.silu(gate_proj) * up_proj).astype(jnp.bfloat16)
    ffn_own = lax.psum_scatter(
        jnp.dot(hidden, down_weight, preferred_element_type=jnp.float32).astype(jnp.bfloat16),
        "req",
        scatter_dimension=0,
        tiled=True,
    ).astype(jnp.float32)
    layer_output = (residual_mid.astype(jnp.float32) + ffn_own).astype(jnp.bfloat16)
    next_normed = (rms_rows(layer_output.astype(jnp.float32)) * next_gain).astype(jnp.bfloat16)
    projected_cols = jnp.dot(
        lax.all_gather(next_normed, "req", axis=0, tiled=True),
        qkv_weight,
        preferred_element_type=jnp.float32,
    ).astype(jnp.bfloat16)
    projected = lax.all_to_all(projected_cols, "req", split_axis=0, concat_axis=1, tiled=True)
    q_next = projected[:, :feat_width]
    pages_dev = row_count // PAGE
    per_owner = pages_dev // peer_count
    key_values = projected[:, feat_width:].reshape(pages_dev, PAGE, 2 * feat_width)
    owner_all = page_owner[0].reshape(peer_count, pages_dev)
    slot_all = page_slot[0].reshape(peer_count, pages_dev)
    page_numbers = jnp.arange(pages_dev, dtype=jnp.int32)
    my_owners = lax.dynamic_index_in_dim(owner_all, tok_place, 0, keepdims=False)
    send_order = jnp.argsort(my_owners * pages_dev + page_numbers)
    outgoing = key_values[send_order].reshape(peer_count, per_owner, PAGE, 2 * feat_width)
    incoming = lax.all_to_all(outgoing, "tok", split_axis=0, concat_axis=0, tiled=True)
    rank_keys = jnp.where(
        owner_all == tok_place, page_numbers[None, :], pages_dev + page_numbers[None, :]
    )
    chosen_pages = jnp.argsort(rank_keys, axis=1)[:, :per_owner]
    slot_list = jnp.take_along_axis(slot_all, chosen_pages, axis=1).reshape(pages_dev)
    page_cache = (
        jnp.zeros((pages_dev, PAGE, 2 * feat_width), jnp.bfloat16)
        .at[slot_list]
        .set(incoming.reshape(pages_dev, PAGE, 2 * feat_width))
    )
    return (layer_output, q_next, page_cache)


def solution(mesh):
    in_specs = (
        P(("req", "tok"), None),
        P(("req", "tok"), None),
        P(("req", "tok"), None),
        P(("req", "tok"), None),
        P("req", None),
        P(),
        P(),
        P(),
        P(None, "req"),
        P(None, "req"),
        P("req", None),
        P(),
        P(None, "req"),
        P("req", None),
        P("req", None),
    )
    out_specs = (P(("req", "tok"), None), P(("req", "tok"), None), P(("req", "tok"), None, None))
    return jax.shard_map(body, mesh=mesh, in_specs=in_specs, out_specs=out_specs, check_vma=False)
```

```python
import math

import jax
import jax.numpy as jnp
from jax import lax
from jax.sharding import Mesh
from jax.sharding import PartitionSpec as P

HEADS = 8
PAGE = 8


NEG_FILL = -1e30
LAMBDA_INIT = 0.2
EPSILON = 1e-05
MAX_SEG = 1024
TOK = ("tx", "tz")
REQ = ("ry", "rc")


def rms_rows(values):
    return values * lax.rsqrt(jnp.mean(values * values, axis=-1, keepdims=True) + EPSILON)


def lambda_value(lambda_parts):
    first_term = jnp.exp(jnp.sum(lambda_parts[0] * lambda_parts[1]))
    second_term = jnp.exp(jnp.sum(lambda_parts[2] * lambda_parts[3]))
    return first_term - second_term + LAMBDA_INIT


def gather_rows(rows):
    across = lax.all_gather(rows, "ry", axis=0, tiled=True)
    return lax.all_gather(across, "rc", axis=0, tiled=True)


def body(
    layer_input,
    q_in,
    k_in,
    v_in,
    segment_ids,
    lambda_parts,
    out_weight,
    ffn_gain,
    gate_weight,
    up_weight,
    down_weight,
    next_gain,
    qkv_weight,
    page_owner,
    page_slot,
):
    row_count = q_in.shape[0]
    feat_width = q_in.shape[1]
    head_dim = feat_width // (2 * HEADS)
    peer_count = lax.axis_size(TOK)
    tok_place = lax.axis_index(TOK)
    seg_row = segment_ids[0]
    first_row = tok_place * row_count
    query_places = first_row + jnp.arange(row_count)
    query_segs = lax.dynamic_slice_in_dim(seg_row, first_row, row_count)
    lambda_mix = lambda_value(lambda_parts)
    score_scale = 1.0 / math.sqrt(head_dim)
    query_split = q_in.reshape(row_count, HEADS, 2, head_dim)
    run_max = jnp.full((HEADS, 2, row_count), NEG_FILL, jnp.float32)
    back = -(-(MAX_SEG - 1) // row_count)
    own_kv = jnp.concatenate([k_in, v_in], axis=1)
    all_kv = lax.all_gather(own_kv, TOK, axis=0, tiled=True)
    padded_kv = jnp.concatenate(
        [jnp.zeros((back * row_count, 2 * feat_width), all_kv.dtype), all_kv], axis=0
    )
    window = lax.dynamic_slice_in_dim(padded_kv, first_row, (back + 1) * row_count, 0)
    piece_len = window.shape[0]
    key_rows = window[:, :feat_width]
    value_rows = window[:, feat_width:]
    key_split = key_rows.reshape(piece_len, HEADS, 2, head_dim)
    value_split = value_rows.reshape(piece_len, HEADS, 2 * head_dim)
    key_places = (tok_place - back) * row_count + jnp.arange(piece_len)
    key_segs = jnp.take(seg_row, jnp.clip(key_places, 0, seg_row.shape[0] - 1))
    visible = (
        (key_places[None, :] >= 0)
        & (key_segs[None, :] == query_segs[:, None])
        & (key_places[None, :] <= query_places[:, None])
    )
    scores = (
        jnp.einsum("qhmd,khmd->hmqk", query_split, key_split, preferred_element_type=jnp.float32)
        * score_scale
    )
    scores = jnp.where(visible, scores, NEG_FILL)
    new_max = jnp.maximum(run_max, jnp.max(scores, axis=-1))
    weights = jnp.where(visible, jnp.exp(scores - new_max[..., None]), 0.0)
    totals = jnp.sum(weights, axis=-1)
    weighted = jnp.einsum(
        "hmqk,khe->hmqe",
        weights.astype(jnp.bfloat16),
        value_split,
        preferred_element_type=jnp.float32,
    )
    run_max, totals, weighted = (new_max, totals, weighted)
    map_outputs = weighted / totals[..., None]
    difference = map_outputs[:, 0] - lambda_mix * map_outputs[:, 1]
    head_outputs = rms_rows(difference) * (1.0 - LAMBDA_INIT)
    attention = (
        jnp.transpose(head_outputs, (1, 0, 2)).reshape(row_count, feat_width).astype(jnp.bfloat16)
    )
    residual_mid = (
        layer_input.astype(jnp.float32)
        + jnp.dot(attention, out_weight, preferred_element_type=jnp.float32)
    ).astype(jnp.bfloat16)
    gathered = gather_rows(residual_mid)
    normed = (rms_rows(gathered.astype(jnp.float32)) * ffn_gain).astype(jnp.bfloat16)
    gate_proj = jnp.dot(normed, gate_weight, preferred_element_type=jnp.float32)
    up_proj = jnp.dot(normed, up_weight, preferred_element_type=jnp.float32)
    hidden = (jax.nn.silu(gate_proj) * up_proj).astype(jnp.bfloat16)
    partial = jnp.dot(hidden, down_weight, preferred_element_type=jnp.float32).astype(jnp.bfloat16)
    partial = lax.psum_scatter(partial, "rc", scatter_dimension=0, tiled=True)
    ffn_own = lax.psum_scatter(partial, "ry", scatter_dimension=0, tiled=True).astype(jnp.float32)
    layer_output = (residual_mid.astype(jnp.float32) + ffn_own).astype(jnp.bfloat16)
    next_normed = (rms_rows(layer_output.astype(jnp.float32)) * next_gain).astype(jnp.bfloat16)
    projected_cols = jnp.dot(
        gather_rows(next_normed),
        qkv_weight,
        preferred_element_type=jnp.float32,
    ).astype(jnp.bfloat16)
    n_rc = lax.axis_size("rc")
    n_ry = lax.axis_size("ry")
    col_w = projected_cols.shape[1]
    blocks = projected_cols.reshape(n_rc, n_ry, row_count, col_w)
    blocks = lax.all_to_all(blocks, "rc", 0, 0, tiled=True)
    blocks = lax.all_to_all(blocks, "ry", 1, 1, tiled=True)
    projected = jnp.transpose(blocks, (2, 1, 0, 3)).reshape(row_count, n_ry * n_rc * col_w)
    q_next = projected[:, :feat_width]
    pages_dev = row_count // PAGE
    per_owner = pages_dev // peer_count
    key_values = projected[:, feat_width:].reshape(pages_dev, PAGE, 2 * feat_width)
    owner_all = page_owner[0].reshape(peer_count, pages_dev)
    slot_all = page_slot[0].reshape(peer_count, pages_dev)
    page_numbers = jnp.arange(pages_dev, dtype=jnp.int32)
    my_owners = lax.dynamic_index_in_dim(owner_all, tok_place, 0, keepdims=False)
    send_order = jnp.argsort(my_owners * pages_dev + page_numbers)
    outgoing = key_values[send_order].reshape(peer_count, per_owner, PAGE, 2 * feat_width)
    incoming = lax.all_to_all(outgoing, TOK, split_axis=0, concat_axis=0, tiled=True)
    rank_keys = jnp.where(
        owner_all == tok_place, page_numbers[None, :], pages_dev + page_numbers[None, :]
    )
    chosen_pages = jnp.argsort(rank_keys, axis=1)[:, :per_owner]
    slot_list = jnp.take_along_axis(slot_all, chosen_pages, axis=1).reshape(pages_dev)
    page_cache = (
        jnp.zeros((pages_dev, PAGE, 2 * feat_width), jnp.bfloat16)
        .at[slot_list]
        .set(incoming.reshape(pages_dev, PAGE, 2 * feat_width))
    )
    return (layer_output, q_next, page_cache)


def solution(mesh):
    n_req, n_tok = mesh.devices.shape
    cores = 2
    lanes = 4
    fine = Mesh(
        mesh.devices.reshape(n_req // cores, cores, n_tok // lanes, lanes), ("ry", "rc", "tx", "tz")
    )
    rows = P(REQ + TOK, None)
    in_specs = (
        rows,
        rows,
        rows,
        rows,
        P(REQ, None),
        P(),
        P(),
        P(),
        P(None, REQ),
        P(None, REQ),
        P(REQ, None),
        P(),
        P(None, REQ),
        P(REQ, None),
        P(REQ, None),
    )
    out_specs = (rows, rows, P(REQ + TOK, None, None))
    return jax.shard_map(body, mesh=fine, in_specs=in_specs, out_specs=out_specs, check_vma=False)
```

```python
import math

import jax
import jax.numpy as jnp
from jax import lax
from jax.sharding import PartitionSpec as P

HEADS = 8
PAGE = 8


NEG_FILL = -1e30
LAMBDA_INIT = 0.2
EPSILON = 1e-05
MAX_SEG = 1024


def rms_rows(values):
    return values * lax.rsqrt(jnp.mean(values * values, axis=-1, keepdims=True) + EPSILON)


def lambda_value(lambda_parts):
    first_term = jnp.exp(jnp.sum(lambda_parts[0] * lambda_parts[1]))
    second_term = jnp.exp(jnp.sum(lambda_parts[2] * lambda_parts[3]))
    return first_term - second_term + LAMBDA_INIT


def body(
    layer_input,
    q_in,
    k_in,
    v_in,
    segment_ids,
    lambda_parts,
    out_weight,
    ffn_gain,
    gate_weight,
    up_weight,
    down_weight,
    next_gain,
    qkv_weight,
    page_owner,
    page_slot,
):
    row_count = q_in.shape[0]
    feat_width = q_in.shape[1]
    head_dim = feat_width // (2 * HEADS)
    peer_count = lax.axis_size("tok")
    tok_place = lax.axis_index("tok")
    seg_row = segment_ids[0]
    first_row = tok_place * row_count
    query_places = first_row + jnp.arange(row_count)
    query_segs = lax.dynamic_slice_in_dim(seg_row, first_row, row_count)
    lambda_mix = lambda_value(lambda_parts)
    score_scale = 1.0 / math.sqrt(head_dim)
    query_split = q_in.reshape(row_count, HEADS, 2, head_dim)
    run_max = jnp.full((HEADS, 2, row_count), NEG_FILL, jnp.float32)
    back = -(-(MAX_SEG - 1) // row_count)
    own_kv = jnp.concatenate([k_in, v_in], axis=1)
    all_kv = lax.all_gather(own_kv, "tok", axis=0, tiled=True)
    padded_kv = jnp.concatenate(
        [jnp.zeros((back * row_count, 2 * feat_width), all_kv.dtype), all_kv], axis=0
    )
    window = lax.dynamic_slice_in_dim(padded_kv, first_row, (back + 1) * row_count, 0)
    piece_len = window.shape[0]
    key_rows = window[:, :feat_width]
    value_rows = window[:, feat_width:]
    key_split = key_rows.reshape(piece_len, HEADS, 2, head_dim)
    value_split = value_rows.reshape(piece_len, HEADS, 2 * head_dim)
    key_places = (tok_place - back) * row_count + jnp.arange(piece_len)
    key_segs = jnp.take(seg_row, jnp.clip(key_places, 0, seg_row.shape[0] - 1))
    visible = (
        (key_places[None, :] >= 0)
        & (key_segs[None, :] == query_segs[:, None])
        & (key_places[None, :] <= query_places[:, None])
    )
    scores = (
        jnp.einsum("qhmd,khmd->hmqk", query_split, key_split, preferred_element_type=jnp.float32)
        * score_scale
    )
    scores = jnp.where(visible, scores, NEG_FILL)
    new_max = jnp.maximum(run_max, jnp.max(scores, axis=-1))
    weights = jnp.where(visible, jnp.exp(scores - new_max[..., None]), 0.0)
    totals = jnp.sum(weights, axis=-1)
    weighted = jnp.einsum(
        "hmqk,khe->hmqe",
        weights.astype(jnp.bfloat16),
        value_split,
        preferred_element_type=jnp.float32,
    )
    run_max, totals, weighted = (new_max, totals, weighted)
    map_outputs = weighted / totals[..., None]
    difference = map_outputs[:, 0] - lambda_mix * map_outputs[:, 1]
    head_outputs = rms_rows(difference) * (1.0 - LAMBDA_INIT)
    attention = (
        jnp.transpose(head_outputs, (1, 0, 2)).reshape(row_count, feat_width).astype(jnp.bfloat16)
    )
    residual_mid = (
        layer_input.astype(jnp.float32)
        + jnp.dot(attention, out_weight, preferred_element_type=jnp.float32)
    ).astype(jnp.bfloat16)
    gathered = lax.all_gather(residual_mid, "req", axis=0, tiled=True)
    normed = (rms_rows(gathered.astype(jnp.float32)) * ffn_gain).astype(jnp.bfloat16)
    gate_proj = jnp.dot(normed, gate_weight, preferred_element_type=jnp.float32)
    up_proj = jnp.dot(normed, up_weight, preferred_element_type=jnp.float32)
    hidden = (jax.nn.silu(gate_proj) * up_proj).astype(jnp.bfloat16)
    ffn_own = lax.psum_scatter(
        jnp.dot(hidden, down_weight, preferred_element_type=jnp.float32).astype(jnp.bfloat16),
        "req",
        scatter_dimension=0,
        tiled=True,
    ).astype(jnp.float32)
    layer_output = (residual_mid.astype(jnp.float32) + ffn_own).astype(jnp.bfloat16)
    next_normed = (rms_rows(layer_output.astype(jnp.float32)) * next_gain).astype(jnp.bfloat16)
    projected_cols = jnp.dot(
        lax.all_gather(next_normed, "req", axis=0, tiled=True),
        qkv_weight,
        preferred_element_type=jnp.float32,
    ).astype(jnp.bfloat16)
    projected = lax.all_to_all(projected_cols, "req", split_axis=0, concat_axis=1, tiled=True)
    q_next = projected[:, :feat_width]
    pages_dev = row_count // PAGE
    per_owner = pages_dev // peer_count
    key_values = projected[:, feat_width:].reshape(pages_dev, PAGE, 2 * feat_width)
    owner_all = page_owner[0].reshape(peer_count, pages_dev)
    slot_all = page_slot[0].reshape(peer_count, pages_dev)
    page_numbers = jnp.arange(pages_dev, dtype=jnp.int32)
    my_owners = lax.dynamic_index_in_dim(owner_all, tok_place, 0, keepdims=False)
    send_order = jnp.argsort(my_owners * pages_dev + page_numbers)
    outgoing = key_values[send_order].reshape(peer_count, per_owner, PAGE, 2 * feat_width)
    incoming = lax.all_to_all(outgoing, "tok", split_axis=0, concat_axis=0, tiled=True)
    rank_keys = jnp.where(
        owner_all == tok_place, page_numbers[None, :], pages_dev + page_numbers[None, :]
    )
    chosen_pages = jnp.argsort(rank_keys, axis=1)[:, :per_owner]
    slot_list = jnp.take_along_axis(slot_all, chosen_pages, axis=1).reshape(pages_dev)
    page_cache = (
        jnp.zeros((pages_dev, PAGE, 2 * feat_width), jnp.bfloat16)
        .at[slot_list]
        .set(incoming.reshape(pages_dev, PAGE, 2 * feat_width))
    )
    return (layer_output, q_next, page_cache)


def solution(mesh):
    in_specs = (
        P(("req", "tok"), None),
        P(("req", "tok"), None),
        P(("req", "tok"), None),
        P(("req", "tok"), None),
        P("req", None),
        P(),
        P(),
        P(),
        P(None, "req"),
        P(None, "req"),
        P("req", None),
        P(),
        P(None, "req"),
        P("req", None),
        P("req", None),
    )
    out_specs = (P(("req", "tok"), None), P(("req", "tok"), None), P(("req", "tok"), None, None))
    return jax.shard_map(body, mesh=mesh, in_specs=in_specs, out_specs=out_specs, check_vma=False)
```

```python
import math

import jax
import jax.numpy as jnp
from jax import lax
from jax.sharding import PartitionSpec as P

HEADS = 8
PAGE = 8


NEG_FILL = -1e30
LAMBDA_INIT = 0.2
EPSILON = 1e-05
MAX_SEG = 1024


def rms_rows(values):
    return values * lax.rsqrt(jnp.mean(values * values, axis=-1, keepdims=True) + EPSILON)


def lambda_value(lambda_parts):
    first_term = jnp.exp(jnp.sum(lambda_parts[0] * lambda_parts[1]))
    second_term = jnp.exp(jnp.sum(lambda_parts[2] * lambda_parts[3]))
    return first_term - second_term + LAMBDA_INIT


def body(
    layer_input,
    q_in,
    k_in,
    v_in,
    segment_ids,
    lambda_parts,
    out_weight,
    ffn_gain,
    gate_weight,
    up_weight,
    down_weight,
    next_gain,
    qkv_weight,
    page_owner,
    page_slot,
):
    row_count = q_in.shape[0]
    feat_width = q_in.shape[1]
    head_dim = feat_width // (2 * HEADS)
    peer_count = lax.axis_size("tok")
    tok_place = lax.axis_index("tok")
    seg_row = segment_ids[0]
    first_row = tok_place * row_count
    query_places = first_row + jnp.arange(row_count)
    query_segs = lax.dynamic_slice_in_dim(seg_row, first_row, row_count)
    lambda_mix = lambda_value(lambda_parts)
    score_scale = 1.0 / math.sqrt(head_dim)
    query_split = q_in.reshape(row_count, HEADS, 2, head_dim)
    run_max = jnp.full((HEADS, 2, row_count), NEG_FILL, jnp.float32)
    back = -(-(MAX_SEG - 1) // row_count)
    own_kv = jnp.concatenate([k_in, v_in], axis=1)
    all_kv = lax.all_gather(own_kv, "tok", axis=0, tiled=True)
    padded_kv = jnp.concatenate(
        [jnp.zeros((back * row_count, 2 * feat_width), all_kv.dtype), all_kv], axis=0
    )
    window = lax.dynamic_slice_in_dim(padded_kv, first_row, (back + 1) * row_count, 0)
    piece_len = window.shape[0]
    key_rows = window[:, :feat_width]
    value_rows = window[:, feat_width:]
    key_split = key_rows.reshape(piece_len, HEADS, 2, head_dim)
    value_split = value_rows.reshape(piece_len, HEADS, 2 * head_dim)
    key_places = (tok_place - back) * row_count + jnp.arange(piece_len)
    key_segs = jnp.take(seg_row, jnp.clip(key_places, 0, seg_row.shape[0] - 1))
    visible = (
        (key_places[None, :] >= 0)
        & (key_segs[None, :] == query_segs[:, None])
        & (key_places[None, :] <= query_places[:, None])
    )
    scores = (
        jnp.einsum("qhmd,khmd->hmqk", query_split, key_split, preferred_element_type=jnp.float32)
        * score_scale
    )
    scores = jnp.where(visible, scores, NEG_FILL)
    new_max = jnp.maximum(run_max, jnp.max(scores, axis=-1))
    weights = jnp.where(visible, jnp.exp(scores - new_max[..., None]), 0.0)
    totals = jnp.sum(weights, axis=-1)
    weighted = jnp.einsum(
        "hmqk,khe->hmqe",
        weights.astype(jnp.bfloat16),
        value_split,
        preferred_element_type=jnp.float32,
    )
    run_max, totals, weighted = (new_max, totals, weighted)
    map_outputs = weighted / totals[..., None]
    difference = map_outputs[:, 0] - lambda_mix * map_outputs[:, 1]
    head_outputs = rms_rows(difference) * (1.0 - LAMBDA_INIT)
    attention = (
        jnp.transpose(head_outputs, (1, 0, 2)).reshape(row_count, feat_width).astype(jnp.bfloat16)
    )
    residual_mid = (
        layer_input.astype(jnp.float32)
        + jnp.dot(attention, out_weight, preferred_element_type=jnp.float32)
    ).astype(jnp.bfloat16)
    gathered = lax.all_gather(residual_mid, "req", axis=0, tiled=True)
    normed = (rms_rows(gathered.astype(jnp.float32)) * ffn_gain).astype(jnp.bfloat16)
    gate_proj = jnp.dot(normed, gate_weight, preferred_element_type=jnp.float32)
    up_proj = jnp.dot(normed, up_weight, preferred_element_type=jnp.float32)
    hidden = (jax.nn.silu(gate_proj) * up_proj).astype(jnp.bfloat16)
    ffn_all = lax.psum(
        jnp.dot(hidden, down_weight, preferred_element_type=jnp.float32).astype(jnp.bfloat16), "req"
    ).astype(jnp.float32)
    output_all = (gathered.astype(jnp.float32) + ffn_all).astype(jnp.bfloat16)
    req_place = lax.axis_index("req")
    layer_output = lax.dynamic_slice_in_dim(output_all, req_place * row_count, row_count, 0)
    next_normed = (rms_rows(output_all.astype(jnp.float32)) * next_gain).astype(jnp.bfloat16)
    projected_cols = jnp.dot(
        next_normed,
        qkv_weight,
        preferred_element_type=jnp.float32,
    ).astype(jnp.bfloat16)
    projected = lax.all_to_all(projected_cols, "req", split_axis=0, concat_axis=1, tiled=True)
    q_next = projected[:, :feat_width]
    pages_dev = row_count // PAGE
    per_owner = pages_dev // peer_count
    key_values = projected[:, feat_width:].reshape(pages_dev, PAGE, 2 * feat_width)
    owner_all = page_owner[0].reshape(peer_count, pages_dev)
    slot_all = page_slot[0].reshape(peer_count, pages_dev)
    page_numbers = jnp.arange(pages_dev, dtype=jnp.int32)
    my_owners = lax.dynamic_index_in_dim(owner_all, tok_place, 0, keepdims=False)
    send_order = jnp.argsort(my_owners * pages_dev + page_numbers)
    outgoing = key_values[send_order].reshape(peer_count, per_owner, PAGE, 2 * feat_width)
    incoming = lax.all_to_all(outgoing, "tok", split_axis=0, concat_axis=0, tiled=True)
    rank_keys = jnp.where(
        owner_all == tok_place, page_numbers[None, :], pages_dev + page_numbers[None, :]
    )
    chosen_pages = jnp.argsort(rank_keys, axis=1)[:, :per_owner]
    slot_list = jnp.take_along_axis(slot_all, chosen_pages, axis=1).reshape(pages_dev)
    page_cache = (
        jnp.zeros((pages_dev, PAGE, 2 * feat_width), jnp.bfloat16)
        .at[slot_list]
        .set(incoming.reshape(pages_dev, PAGE, 2 * feat_width))
    )
    return (layer_output, q_next, page_cache)


def solution(mesh):
    in_specs = (
        P(("req", "tok"), None),
        P(("req", "tok"), None),
        P(("req", "tok"), None),
        P(("req", "tok"), None),
        P("req", None),
        P(),
        P(),
        P(),
        P(None, "req"),
        P(None, "req"),
        P("req", None),
        P(),
        P(None, "req"),
        P("req", None),
        P("req", None),
    )
    out_specs = (P(("req", "tok"), None), P(("req", "tok"), None), P(("req", "tok"), None, None))
    return jax.shard_map(body, mesh=mesh, in_specs=in_specs, out_specs=out_specs, check_vma=False)
```

```python
import functools
import math

import jax
import jax.numpy as jnp
from jax import lax
from jax.experimental import pallas as pl
from jax.experimental.pallas import tpu as pltpu
from jax.sharding import PartitionSpec as P

HEADS = 8
PAGE = 8


NEG_FILL = -1e30
LAMBDA_INIT = 0.2
EPSILON = 1e-05
MAX_SEG = 1024


def rms_rows(values):
    return values * lax.rsqrt(jnp.mean(values * values, axis=-1, keepdims=True) + EPSILON)


def lambda_value(lambda_parts):
    first_term = jnp.exp(jnp.sum(lambda_parts[0] * lambda_parts[1]))
    second_term = jnp.exp(jnp.sum(lambda_parts[2] * lambda_parts[3]))
    return first_term - second_term + LAMBDA_INIT


def attention_kernel(back, head_dim, scalars_ref, lam_ref, q_ref, k_ref, v_ref, qseg_ref, kseg_ref, out_ref):
    rows = q_ref.shape[0]
    span = (back + 1) * rows
    start = pl.multiple_of(scalars_ref[0], rows)
    query_places = scalars_ref[1] + lax.broadcasted_iota(jnp.int32, (rows, span), 0)
    key_places = start + lax.broadcasted_iota(jnp.int32, (rows, span), 1)
    key_segs = kseg_ref[:, pl.ds(start, span)]
    visible = (key_segs == qseg_ref[...]) & (key_places <= query_places)
    values = v_ref[pl.ds(start, span), :]
    score_scale = 1.0 / math.sqrt(head_dim)
    map_outputs = []
    for map_index in range(2):
        query_map = q_ref[:, map_index * head_dim:(map_index + 1) * head_dim]
        key_map = k_ref[pl.ds(start, span), map_index * head_dim:(map_index + 1) * head_dim]
        scores = (
            lax.dot_general(
                query_map, key_map, (((1,), (1,)), ((), ())), preferred_element_type=jnp.float32
            )
            * score_scale
        )
        scores = jnp.where(visible, scores, NEG_FILL)
        row_max = jnp.max(scores, axis=1, keepdims=True)
        weights = jnp.where(visible, jnp.exp(scores - row_max), 0.0)
        totals = jnp.sum(weights, axis=1, keepdims=True)
        map_out = (
            jnp.dot(weights.astype(jnp.bfloat16), values, preferred_element_type=jnp.float32) / totals
        )
        map_outputs.append(map_out)
    difference = map_outputs[0] - lam_ref[0] * map_outputs[1]
    out_ref[...] = (rms_rows(difference) * (1.0 - LAMBDA_INIT)).astype(out_ref.dtype)


def window_attention(q_in, all_kv, query_segs, seg_row, first_row, lambda_mix, back):
    rows, width = q_in.shape
    keys = all_kv.shape[0]
    head_w = width // HEADS
    start = jnp.maximum(first_row - back * rows, 0)
    scalars = jnp.stack([start, first_row]).astype(jnp.int32)
    lam = jnp.reshape(lambda_mix, (1,)).astype(jnp.float32)
    span = (back + 1) * rows
    flops = HEADS * 2 * (2 * rows * span * (head_w // 2) + 2 * rows * span * head_w)
    smem = pl.BlockSpec(memory_space=pltpu.SMEM)
    return pl.pallas_call(
        functools.partial(attention_kernel, back, head_w // 2),
        out_shape=jax.ShapeDtypeStruct((rows, width), jnp.bfloat16),
        grid=(HEADS,),
        in_specs=[
            smem,
            smem,
            pl.BlockSpec((rows, head_w), lambda h: (0, h)),
            pl.BlockSpec((keys, head_w), lambda h: (0, h)),
            pl.BlockSpec((keys, head_w), lambda h: (0, HEADS + h)),
            pl.BlockSpec((rows, 1), lambda h: (0, 0)),
            pl.BlockSpec((1, keys), lambda h: (0, 0)),
        ],
        out_specs=pl.BlockSpec((rows, head_w), lambda h: (0, h)),
        compiler_params=pltpu.CompilerParams(dimension_semantics=("arbitrary",)),
        cost_estimate=pl.CostEstimate(
            flops=flops,
            bytes_accessed=2 * keys * width * 2 + 2 * rows * width * 2,
            transcendentals=HEADS * 2 * rows * span,
        ),
    )(scalars, lam, q_in, all_kv, all_kv, query_segs.reshape(rows, 1), seg_row.reshape(1, keys))


def body(
    layer_input,
    q_in,
    k_in,
    v_in,
    segment_ids,
    lambda_parts,
    out_weight,
    ffn_gain,
    gate_weight,
    up_weight,
    down_weight,
    next_gain,
    qkv_weight,
    page_owner,
    page_slot,
):
    row_count = q_in.shape[0]
    feat_width = q_in.shape[1]
    head_dim = feat_width // (2 * HEADS)
    peer_count = lax.axis_size("tok")
    tok_place = lax.axis_index("tok")
    seg_row = segment_ids[0]
    first_row = tok_place * row_count
    query_places = first_row + jnp.arange(row_count)
    query_segs = lax.dynamic_slice_in_dim(seg_row, first_row, row_count)
    lambda_mix = lambda_value(lambda_parts)
    score_scale = 1.0 / math.sqrt(head_dim)
    query_split = q_in.reshape(row_count, HEADS, 2, head_dim)
    run_max = jnp.full((HEADS, 2, row_count), NEG_FILL, jnp.float32)
    back = -(-(MAX_SEG - 1) // row_count)
    own_kv = jnp.concatenate([k_in, v_in], axis=1)
    all_kv = lax.all_gather(own_kv, "tok", axis=0, tiled=True)
    attention = window_attention(q_in, all_kv, query_segs, seg_row, first_row, lambda_mix, back)
    residual_mid = (
        layer_input.astype(jnp.float32)
        + jnp.dot(attention, out_weight, preferred_element_type=jnp.float32)
    ).astype(jnp.bfloat16)
    gathered = lax.all_gather(residual_mid, "req", axis=0, tiled=True)
    normed = (rms_rows(gathered.astype(jnp.float32)) * ffn_gain).astype(jnp.bfloat16)
    gate_proj = jnp.dot(normed, gate_weight, preferred_element_type=jnp.float32)
    up_proj = jnp.dot(normed, up_weight, preferred_element_type=jnp.float32)
    hidden = (jax.nn.silu(gate_proj) * up_proj).astype(jnp.bfloat16)
    ffn_own = lax.psum_scatter(
        jnp.dot(hidden, down_weight, preferred_element_type=jnp.float32).astype(jnp.bfloat16),
        "req",
        scatter_dimension=0,
        tiled=True,
    ).astype(jnp.float32)
    layer_output = (residual_mid.astype(jnp.float32) + ffn_own).astype(jnp.bfloat16)
    next_normed = (rms_rows(layer_output.astype(jnp.float32)) * next_gain).astype(jnp.bfloat16)
    projected_cols = jnp.dot(
        lax.all_gather(next_normed, "req", axis=0, tiled=True),
        qkv_weight,
        preferred_element_type=jnp.float32,
    ).astype(jnp.bfloat16)
    projected = lax.all_to_all(projected_cols, "req", split_axis=0, concat_axis=1, tiled=True)
    q_next = projected[:, :feat_width]
    pages_dev = row_count // PAGE
    per_owner = pages_dev // peer_count
    key_values = projected[:, feat_width:].reshape(pages_dev, PAGE, 2 * feat_width)
    owner_all = page_owner[0].reshape(peer_count, pages_dev)
    slot_all = page_slot[0].reshape(peer_count, pages_dev)
    page_numbers = jnp.arange(pages_dev, dtype=jnp.int32)
    my_owners = lax.dynamic_index_in_dim(owner_all, tok_place, 0, keepdims=False)
    send_order = jnp.argsort(my_owners * pages_dev + page_numbers)
    outgoing = key_values[send_order].reshape(peer_count, per_owner, PAGE, 2 * feat_width)
    incoming = lax.all_to_all(outgoing, "tok", split_axis=0, concat_axis=0, tiled=True)
    rank_keys = jnp.where(
        owner_all == tok_place, page_numbers[None, :], pages_dev + page_numbers[None, :]
    )
    chosen_pages = jnp.argsort(rank_keys, axis=1)[:, :per_owner]
    slot_list = jnp.take_along_axis(slot_all, chosen_pages, axis=1).reshape(pages_dev)
    page_cache = (
        jnp.zeros((pages_dev, PAGE, 2 * feat_width), jnp.bfloat16)
        .at[slot_list]
        .set(incoming.reshape(pages_dev, PAGE, 2 * feat_width))
    )
    return (layer_output, q_next, page_cache)


def solution(mesh):
    in_specs = (
        P(("req", "tok"), None),
        P(("req", "tok"), None),
        P(("req", "tok"), None),
        P(("req", "tok"), None),
        P("req", None),
        P(),
        P(),
        P(),
        P(None, "req"),
        P(None, "req"),
        P("req", None),
        P(),
        P(None, "req"),
        P("req", None),
        P("req", None),
    )
    out_specs = (P(("req", "tok"), None), P(("req", "tok"), None), P(("req", "tok"), None, None))
    return jax.shard_map(body, mesh=mesh, in_specs=in_specs, out_specs=out_specs, check_vma=False)
```

```python
import functools
import math

import jax
import jax.numpy as jnp
from jax import lax
from jax.experimental import pallas as pl
from jax.experimental.pallas import tpu as pltpu
from jax.sharding import PartitionSpec as P

HEADS = 8
PAGE = 8


NEG_FILL = -1e30
LAMBDA_INIT = 0.2
EPSILON = 1e-05
MAX_SEG = 1024


def rms_rows(values):
    return values * lax.rsqrt(jnp.mean(values * values, axis=-1, keepdims=True) + EPSILON)


def lambda_value(lambda_parts):
    first_term = jnp.exp(jnp.sum(lambda_parts[0] * lambda_parts[1]))
    second_term = jnp.exp(jnp.sum(lambda_parts[2] * lambda_parts[3]))
    return first_term - second_term + LAMBDA_INIT


def attention_kernel(back, head_dim, scalars_ref, lam_ref, q_ref, k_ref, v_ref, qseg_ref, kseg_ref, out_ref):
    rows = q_ref.shape[0]
    span = (back + 1) * rows
    start = pl.multiple_of(scalars_ref[0], rows)
    query_places = scalars_ref[1] + lax.broadcasted_iota(jnp.int32, (rows, span), 0)
    key_places = start + lax.broadcasted_iota(jnp.int32, (rows, span), 1)
    key_segs = kseg_ref[:, pl.ds(start, span)]
    visible = (key_segs == qseg_ref[...]) & (key_places <= query_places)
    values = v_ref[pl.ds(start, span), :]
    score_scale = 1.0 / math.sqrt(head_dim)
    map_outputs = []
    for map_index in range(2):
        query_map = q_ref[:, map_index * head_dim:(map_index + 1) * head_dim]
        key_map = k_ref[pl.ds(start, span), map_index * head_dim:(map_index + 1) * head_dim]
        scores = (
            lax.dot_general(
                query_map, key_map, (((1,), (1,)), ((), ())), preferred_element_type=jnp.float32
            )
            * score_scale
        )
        scores = jnp.where(visible, scores, NEG_FILL)
        row_max = jnp.max(scores, axis=1, keepdims=True)
        weights = jnp.where(visible, jnp.exp(scores - row_max), 0.0)
        totals = jnp.sum(weights, axis=1, keepdims=True)
        map_out = (
            jnp.dot(weights.astype(jnp.bfloat16), values, preferred_element_type=jnp.float32) / totals
        )
        map_outputs.append(map_out)
    difference = map_outputs[0] - lam_ref[0] * map_outputs[1]
    out_ref[...] = (rms_rows(difference) * (1.0 - LAMBDA_INIT)).astype(out_ref.dtype)


def window_attention(q_in, all_kv, query_segs, seg_row, first_row, lambda_mix, back):
    rows, width = q_in.shape
    keys = all_kv.shape[0]
    head_w = width // HEADS
    start = jnp.maximum(first_row - back * rows, 0)
    scalars = jnp.stack([start, first_row]).astype(jnp.int32)
    lam = jnp.reshape(lambda_mix, (1,)).astype(jnp.float32)
    span = (back + 1) * rows
    flops = HEADS * 2 * (2 * rows * span * (head_w // 2) + 2 * rows * span * head_w)
    smem = pl.BlockSpec(memory_space=pltpu.SMEM)
    return pl.pallas_call(
        functools.partial(attention_kernel, back, head_w // 2),
        out_shape=jax.ShapeDtypeStruct((rows, width), jnp.bfloat16),
        grid=(HEADS,),
        in_specs=[
            smem,
            smem,
            pl.BlockSpec((rows, head_w), lambda h: (0, h)),
            pl.BlockSpec((keys, head_w), lambda h: (0, h)),
            pl.BlockSpec((keys, head_w), lambda h: (0, HEADS + h)),
            pl.BlockSpec((rows, 1), lambda h: (0, 0)),
            pl.BlockSpec((1, keys), lambda h: (0, 0)),
        ],
        out_specs=pl.BlockSpec((rows, head_w), lambda h: (0, h)),
        compiler_params=pltpu.CompilerParams(dimension_semantics=("arbitrary",)),
        cost_estimate=pl.CostEstimate(
            flops=flops,
            bytes_accessed=2 * keys * width * 2 + 2 * rows * width * 2,
            transcendentals=HEADS * 2 * rows * span,
        ),
    )(scalars, lam, q_in, all_kv, all_kv, query_segs.reshape(rows, 1), seg_row.reshape(1, keys))


def ffn_kernel(x_ref, gain_ref, gate_ref, up_ref, down_ref, out_ref):
    normed = (rms_rows(x_ref[...].astype(jnp.float32)) * gain_ref[...]).astype(jnp.bfloat16)
    gate_proj = jnp.dot(normed, gate_ref[...], preferred_element_type=jnp.float32)
    up_proj = jnp.dot(normed, up_ref[...], preferred_element_type=jnp.float32)
    hidden = (gate_proj / (1.0 + jnp.exp(-gate_proj)) * up_proj).astype(jnp.bfloat16)
    out_ref[...] = jnp.dot(hidden, down_ref[...], preferred_element_type=jnp.float32).astype(
        out_ref.dtype
    )


def ffn_partial(rows, gain, gate_weight, up_weight, down_weight, tile):
    count, width = rows.shape
    hidden_w = gate_weight.shape[1]
    full = lambda i: (0, 0)
    return pl.pallas_call(
        ffn_kernel,
        out_shape=jax.ShapeDtypeStruct((count, width), jnp.bfloat16),
        grid=(count // tile,),
        in_specs=[
            pl.BlockSpec((tile, width), lambda i: (i, 0)),
            pl.BlockSpec((1, width), full),
            pl.BlockSpec((width, hidden_w), full),
            pl.BlockSpec((width, hidden_w), full),
            pl.BlockSpec((hidden_w, width), full),
        ],
        out_specs=pl.BlockSpec((tile, width), lambda i: (i, 0)),
        compiler_params=pltpu.CompilerParams(
            dimension_semantics=("arbitrary",), vmem_limit_bytes=48 * 1024 * 1024
        ),
        cost_estimate=pl.CostEstimate(
            flops=6 * count * width * hidden_w,
            bytes_accessed=3 * width * hidden_w * 2 + 2 * count * width * 2,
            transcendentals=count * hidden_w,
        ),
    )(rows, gain.reshape(1, width), gate_weight, up_weight, down_weight)


def body(
    layer_input,
    q_in,
    k_in,
    v_in,
    segment_ids,
    lambda_parts,
    out_weight,
    ffn_gain,
    gate_weight,
    up_weight,
    down_weight,
    next_gain,
    qkv_weight,
    page_owner,
    page_slot,
):
    row_count = q_in.shape[0]
    feat_width = q_in.shape[1]
    head_dim = feat_width // (2 * HEADS)
    peer_count = lax.axis_size("tok")
    tok_place = lax.axis_index("tok")
    seg_row = segment_ids[0]
    first_row = tok_place * row_count
    query_places = first_row + jnp.arange(row_count)
    query_segs = lax.dynamic_slice_in_dim(seg_row, first_row, row_count)
    lambda_mix = lambda_value(lambda_parts)
    score_scale = 1.0 / math.sqrt(head_dim)
    query_split = q_in.reshape(row_count, HEADS, 2, head_dim)
    run_max = jnp.full((HEADS, 2, row_count), NEG_FILL, jnp.float32)
    back = -(-(MAX_SEG - 1) // row_count)
    own_kv = jnp.concatenate([k_in, v_in], axis=1)
    all_kv = lax.all_gather(own_kv, "tok", axis=0, tiled=True)
    attention = window_attention(q_in, all_kv, query_segs, seg_row, first_row, lambda_mix, back)
    residual_mid = (
        layer_input.astype(jnp.float32)
        + jnp.dot(attention, out_weight, preferred_element_type=jnp.float32)
    ).astype(jnp.bfloat16)
    gathered = lax.all_gather(residual_mid, "req", axis=0, tiled=True)
    partial = ffn_partial(gathered, ffn_gain, gate_weight, up_weight, down_weight, 256)
    ffn_own = lax.psum_scatter(partial, "req", scatter_dimension=0, tiled=True).astype(jnp.float32)
    layer_output = (residual_mid.astype(jnp.float32) + ffn_own).astype(jnp.bfloat16)
    next_normed = (rms_rows(layer_output.astype(jnp.float32)) * next_gain).astype(jnp.bfloat16)
    projected_cols = jnp.dot(
        lax.all_gather(next_normed, "req", axis=0, tiled=True),
        qkv_weight,
        preferred_element_type=jnp.float32,
    ).astype(jnp.bfloat16)
    projected = lax.all_to_all(projected_cols, "req", split_axis=0, concat_axis=1, tiled=True)
    q_next = projected[:, :feat_width]
    pages_dev = row_count // PAGE
    per_owner = pages_dev // peer_count
    key_values = projected[:, feat_width:].reshape(pages_dev, PAGE, 2 * feat_width)
    owner_all = page_owner[0].reshape(peer_count, pages_dev)
    slot_all = page_slot[0].reshape(peer_count, pages_dev)
    page_numbers = jnp.arange(pages_dev, dtype=jnp.int32)
    my_owners = lax.dynamic_index_in_dim(owner_all, tok_place, 0, keepdims=False)
    send_order = jnp.argsort(my_owners * pages_dev + page_numbers)
    outgoing = key_values[send_order].reshape(peer_count, per_owner, PAGE, 2 * feat_width)
    incoming = lax.all_to_all(outgoing, "tok", split_axis=0, concat_axis=0, tiled=True)
    rank_keys = jnp.where(
        owner_all == tok_place, page_numbers[None, :], pages_dev + page_numbers[None, :]
    )
    chosen_pages = jnp.argsort(rank_keys, axis=1)[:, :per_owner]
    slot_list = jnp.take_along_axis(slot_all, chosen_pages, axis=1).reshape(pages_dev)
    page_cache = (
        jnp.zeros((pages_dev, PAGE, 2 * feat_width), jnp.bfloat16)
        .at[slot_list]
        .set(incoming.reshape(pages_dev, PAGE, 2 * feat_width))
    )
    return (layer_output, q_next, page_cache)


def solution(mesh):
    in_specs = (
        P(("req", "tok"), None),
        P(("req", "tok"), None),
        P(("req", "tok"), None),
        P(("req", "tok"), None),
        P("req", None),
        P(),
        P(),
        P(),
        P(None, "req"),
        P(None, "req"),
        P("req", None),
        P(),
        P(None, "req"),
        P("req", None),
        P("req", None),
    )
    out_specs = (P(("req", "tok"), None), P(("req", "tok"), None), P(("req", "tok"), None, None))
    return jax.shard_map(body, mesh=mesh, in_specs=in_specs, out_specs=out_specs, check_vma=False)
```

```python
import functools
import math

import jax
import jax.numpy as jnp
from jax import lax
from jax.experimental import pallas as pl
from jax.experimental.pallas import tpu as pltpu
from jax.sharding import PartitionSpec as P

HEADS = 8
PAGE = 8


NEG_FILL = -1e30
LAMBDA_INIT = 0.2
EPSILON = 1e-05
MAX_SEG = 1024


def rms_rows(values):
    return values * lax.rsqrt(jnp.mean(values * values, axis=-1, keepdims=True) + EPSILON)


def lambda_value(lambda_parts):
    first_term = jnp.exp(jnp.sum(lambda_parts[0] * lambda_parts[1]))
    second_term = jnp.exp(jnp.sum(lambda_parts[2] * lambda_parts[3]))
    return first_term - second_term + LAMBDA_INIT


def attention_kernel(back, head_dim, scalars_ref, lam_ref, q_ref, k_ref, v_ref, qseg_ref, kseg_ref, out_ref):
    rows = q_ref.shape[0]
    span = (back + 1) * rows
    start = pl.multiple_of(scalars_ref[0], rows)
    query_places = scalars_ref[1] + lax.broadcasted_iota(jnp.int32, (rows, span), 0)
    key_places = start + lax.broadcasted_iota(jnp.int32, (rows, span), 1)
    key_segs = kseg_ref[:, pl.ds(start, span)]
    visible = (key_segs == qseg_ref[...]) & (key_places <= query_places)
    values = v_ref[pl.ds(start, span), :]
    score_scale = 1.0 / math.sqrt(head_dim)
    map_outputs = []
    for map_index in range(2):
        query_map = q_ref[:, map_index * head_dim:(map_index + 1) * head_dim]
        key_map = k_ref[pl.ds(start, span), map_index * head_dim:(map_index + 1) * head_dim]
        scores = (
            lax.dot_general(
                query_map, key_map, (((1,), (1,)), ((), ())), preferred_element_type=jnp.float32
            )
            * score_scale
        )
        scores = jnp.where(visible, scores, NEG_FILL)
        row_max = jnp.max(scores, axis=1, keepdims=True)
        weights = jnp.where(visible, jnp.exp(scores - row_max), 0.0)
        totals = jnp.sum(weights, axis=1, keepdims=True)
        map_out = (
            jnp.dot(weights.astype(jnp.bfloat16), values, preferred_element_type=jnp.float32) / totals
        )
        map_outputs.append(map_out)
    difference = map_outputs[0] - lam_ref[0] * map_outputs[1]
    out_ref[...] = (rms_rows(difference) * (1.0 - LAMBDA_INIT)).astype(out_ref.dtype)


def window_attention(q_in, all_kv, query_segs, seg_row, first_row, lambda_mix, back):
    rows, width = q_in.shape
    keys = all_kv.shape[0]
    head_w = width // HEADS
    start = jnp.maximum(first_row - back * rows, 0)
    scalars = jnp.stack([start, first_row]).astype(jnp.int32)
    lam = jnp.reshape(lambda_mix, (1,)).astype(jnp.float32)
    span = (back + 1) * rows
    flops = HEADS * 2 * (2 * rows * span * (head_w // 2) + 2 * rows * span * head_w)
    smem = pl.BlockSpec(memory_space=pltpu.SMEM)
    return pl.pallas_call(
        functools.partial(attention_kernel, back, head_w // 2),
        out_shape=jax.ShapeDtypeStruct((rows, width), jnp.bfloat16),
        grid=(HEADS,),
        in_specs=[
            smem,
            smem,
            pl.BlockSpec((rows, head_w), lambda h: (0, h)),
            pl.BlockSpec((keys, head_w), lambda h: (0, h)),
            pl.BlockSpec((keys, head_w), lambda h: (0, HEADS + h)),
            pl.BlockSpec((rows, 1), lambda h: (0, 0)),
            pl.BlockSpec((1, keys), lambda h: (0, 0)),
        ],
        out_specs=pl.BlockSpec((rows, head_w), lambda h: (0, h)),
        compiler_params=pltpu.CompilerParams(dimension_semantics=("arbitrary",)),
        cost_estimate=pl.CostEstimate(
            flops=flops,
            bytes_accessed=2 * keys * width * 2 + 2 * rows * width * 2,
            transcendentals=HEADS * 2 * rows * span,
        ),
    )(scalars, lam, q_in, all_kv, all_kv, query_segs.reshape(rows, 1), seg_row.reshape(1, keys))


def ffn_kernel(x_ref, gain_ref, gate_ref, up_ref, down_ref, out_ref):
    normed = (rms_rows(x_ref[...].astype(jnp.float32)) * gain_ref[...]).astype(jnp.bfloat16)
    contract = (((1,), (1,)), ((), ()))
    gate_proj = lax.dot_general(normed, gate_ref[...], contract, preferred_element_type=jnp.float32)
    up_proj = lax.dot_general(normed, up_ref[...], contract, preferred_element_type=jnp.float32)
    hidden = (gate_proj / (1.0 + jnp.exp(-gate_proj)) * up_proj).astype(jnp.bfloat16)
    out_ref[...] = jnp.dot(hidden, down_ref[...], preferred_element_type=jnp.float32).astype(
        out_ref.dtype
    )


def ffn_partial(rows, gain, gate_weight, up_weight, down_weight, tile):
    count, width = rows.shape
    hidden_w = gate_weight.shape[1]
    full = lambda i: (0, 0)
    gate_t = gate_weight.T
    up_t = up_weight.T
    return pl.pallas_call(
        ffn_kernel,
        out_shape=jax.ShapeDtypeStruct((count, width), jnp.bfloat16),
        grid=(count // tile,),
        in_specs=[
            pl.BlockSpec((tile, width), lambda i: (i, 0)),
            pl.BlockSpec((1, width), full),
            pl.BlockSpec((hidden_w, width), full),
            pl.BlockSpec((hidden_w, width), full),
            pl.BlockSpec((hidden_w, width), full),
        ],
        out_specs=pl.BlockSpec((tile, width), lambda i: (i, 0)),
        compiler_params=pltpu.CompilerParams(
            dimension_semantics=("arbitrary",), vmem_limit_bytes=48 * 1024 * 1024
        ),
        cost_estimate=pl.CostEstimate(
            flops=6 * count * width * hidden_w,
            bytes_accessed=3 * width * hidden_w * 2 + 2 * count * width * 2,
            transcendentals=count * hidden_w,
        ),
    )(rows, gain.reshape(1, width), gate_t, up_t, down_weight)


def body(
    layer_input,
    q_in,
    k_in,
    v_in,
    segment_ids,
    lambda_parts,
    out_weight,
    ffn_gain,
    gate_weight,
    up_weight,
    down_weight,
    next_gain,
    qkv_weight,
    page_owner,
    page_slot,
):
    row_count = q_in.shape[0]
    feat_width = q_in.shape[1]
    head_dim = feat_width // (2 * HEADS)
    peer_count = lax.axis_size("tok")
    tok_place = lax.axis_index("tok")
    seg_row = segment_ids[0]
    first_row = tok_place * row_count
    query_places = first_row + jnp.arange(row_count)
    query_segs = lax.dynamic_slice_in_dim(seg_row, first_row, row_count)
    lambda_mix = lambda_value(lambda_parts)
    score_scale = 1.0 / math.sqrt(head_dim)
    query_split = q_in.reshape(row_count, HEADS, 2, head_dim)
    run_max = jnp.full((HEADS, 2, row_count), NEG_FILL, jnp.float32)
    back = -(-(MAX_SEG - 1) // row_count)
    own_kv = jnp.concatenate([k_in, v_in], axis=1)
    all_kv = lax.all_gather(own_kv, "tok", axis=0, tiled=True)
    attention = window_attention(q_in, all_kv, query_segs, seg_row, first_row, lambda_mix, back)
    residual_mid = (
        layer_input.astype(jnp.float32)
        + jnp.dot(attention, out_weight, preferred_element_type=jnp.float32)
    ).astype(jnp.bfloat16)
    gathered = lax.all_gather(residual_mid, "req", axis=0, tiled=True)
    partial = ffn_partial(gathered, ffn_gain, gate_weight, up_weight, down_weight, 256)
    ffn_own = lax.psum_scatter(partial, "req", scatter_dimension=0, tiled=True).astype(jnp.float32)
    layer_output = (residual_mid.astype(jnp.float32) + ffn_own).astype(jnp.bfloat16)
    next_normed = (rms_rows(layer_output.astype(jnp.float32)) * next_gain).astype(jnp.bfloat16)
    projected_cols = jnp.dot(
        lax.all_gather(next_normed, "req", axis=0, tiled=True),
        qkv_weight,
        preferred_element_type=jnp.float32,
    ).astype(jnp.bfloat16)
    projected = lax.all_to_all(projected_cols, "req", split_axis=0, concat_axis=1, tiled=True)
    q_next = projected[:, :feat_width]
    pages_dev = row_count // PAGE
    per_owner = pages_dev // peer_count
    key_values = projected[:, feat_width:].reshape(pages_dev, PAGE, 2 * feat_width)
    owner_all = page_owner[0].reshape(peer_count, pages_dev)
    slot_all = page_slot[0].reshape(peer_count, pages_dev)
    page_numbers = jnp.arange(pages_dev, dtype=jnp.int32)
    my_owners = lax.dynamic_index_in_dim(owner_all, tok_place, 0, keepdims=False)
    send_order = jnp.argsort(my_owners * pages_dev + page_numbers)
    outgoing = key_values[send_order].reshape(peer_count, per_owner, PAGE, 2 * feat_width)
    incoming = lax.all_to_all(outgoing, "tok", split_axis=0, concat_axis=0, tiled=True)
    rank_keys = jnp.where(
        owner_all == tok_place, page_numbers[None, :], pages_dev + page_numbers[None, :]
    )
    chosen_pages = jnp.argsort(rank_keys, axis=1)[:, :per_owner]
    slot_list = jnp.take_along_axis(slot_all, chosen_pages, axis=1).reshape(pages_dev)
    page_cache = (
        jnp.zeros((pages_dev, PAGE, 2 * feat_width), jnp.bfloat16)
        .at[slot_list]
        .set(incoming.reshape(pages_dev, PAGE, 2 * feat_width))
    )
    return (layer_output, q_next, page_cache)


def solution(mesh):
    in_specs = (
        P(("req", "tok"), None),
        P(("req", "tok"), None),
        P(("req", "tok"), None),
        P(("req", "tok"), None),
        P("req", None),
        P(),
        P(),
        P(),
        P(None, "req"),
        P(None, "req"),
        P("req", None),
        P(),
        P(None, "req"),
        P("req", None),
        P("req", None),
    )
    out_specs = (P(("req", "tok"), None), P(("req", "tok"), None), P(("req", "tok"), None, None))
    return jax.shard_map(body, mesh=mesh, in_specs=in_specs, out_specs=out_specs, check_vma=False)
```

```python
import functools
import math

import jax
import jax.numpy as jnp
from jax import lax
from jax.experimental import pallas as pl
from jax.experimental.pallas import tpu as pltpu
from jax.sharding import PartitionSpec as P

HEADS = 8
PAGE = 8


NEG_FILL = -1e30
LAMBDA_INIT = 0.2
EPSILON = 1e-05
MAX_SEG = 1024


def rms_rows(values):
    return values * lax.rsqrt(jnp.mean(values * values, axis=-1, keepdims=True) + EPSILON)


def lambda_value(lambda_parts):
    first_term = jnp.exp(jnp.sum(lambda_parts[0] * lambda_parts[1]))
    second_term = jnp.exp(jnp.sum(lambda_parts[2] * lambda_parts[3]))
    return first_term - second_term + LAMBDA_INIT


def attention_kernel(back, head_dim, scalars_ref, lam_ref, q_ref, k_ref, v_ref, qseg_ref, kseg_ref, out_ref):
    rows = q_ref.shape[0]
    span = (back + 1) * rows
    start = pl.multiple_of(scalars_ref[0], rows)
    query_places = scalars_ref[1] + lax.broadcasted_iota(jnp.int32, (rows, span), 0)
    key_places = start + lax.broadcasted_iota(jnp.int32, (rows, span), 1)
    key_segs = kseg_ref[:, pl.ds(start, span)]
    visible = (key_segs == qseg_ref[...]) & (key_places <= query_places)
    values = v_ref[pl.ds(start, span), :]
    score_scale = 1.0 / math.sqrt(head_dim)
    map_outputs = []
    for map_index in range(2):
        query_map = q_ref[:, map_index * head_dim:(map_index + 1) * head_dim]
        key_map = k_ref[pl.ds(start, span), map_index * head_dim:(map_index + 1) * head_dim]
        scores = (
            lax.dot_general(
                query_map, key_map, (((1,), (1,)), ((), ())), preferred_element_type=jnp.float32
            )
            * score_scale
        )
        scores = jnp.where(visible, scores, NEG_FILL)
        row_max = jnp.max(scores, axis=1, keepdims=True)
        weights = jnp.where(visible, jnp.exp(scores - row_max), 0.0)
        totals = jnp.sum(weights, axis=1, keepdims=True)
        map_out = (
            jnp.dot(weights.astype(jnp.bfloat16), values, preferred_element_type=jnp.float32) / totals
        )
        map_outputs.append(map_out)
    difference = map_outputs[0] - lam_ref[0] * map_outputs[1]
    out_ref[...] = (rms_rows(difference) * (1.0 - LAMBDA_INIT)).astype(out_ref.dtype)


def window_attention(q_in, all_kv, query_segs, seg_row, first_row, lambda_mix, back):
    rows, width = q_in.shape
    keys = all_kv.shape[0]
    head_w = width // HEADS
    start = jnp.maximum(first_row - back * rows, 0)
    scalars = jnp.stack([start, first_row]).astype(jnp.int32)
    lam = jnp.reshape(lambda_mix, (1,)).astype(jnp.float32)
    span = (back + 1) * rows
    flops = HEADS * 2 * (2 * rows * span * (head_w // 2) + 2 * rows * span * head_w)
    smem = pl.BlockSpec(memory_space=pltpu.SMEM)
    return pl.pallas_call(
        functools.partial(attention_kernel, back, head_w // 2),
        out_shape=jax.ShapeDtypeStruct((rows, width), jnp.bfloat16),
        grid=(HEADS,),
        in_specs=[
            smem,
            smem,
            pl.BlockSpec((rows, head_w), lambda h: (0, h)),
            pl.BlockSpec((keys, head_w), lambda h: (0, h)),
            pl.BlockSpec((keys, head_w), lambda h: (0, HEADS + h)),
            pl.BlockSpec((rows, 1), lambda h: (0, 0)),
            pl.BlockSpec((1, keys), lambda h: (0, 0)),
        ],
        out_specs=pl.BlockSpec((rows, head_w), lambda h: (0, h)),
        compiler_params=pltpu.CompilerParams(dimension_semantics=("arbitrary",)),
        cost_estimate=pl.CostEstimate(
            flops=flops,
            bytes_accessed=2 * keys * width * 2 + 2 * rows * width * 2,
            transcendentals=HEADS * 2 * rows * span,
        ),
    )(scalars, lam, q_in, all_kv, all_kv, query_segs.reshape(rows, 1), seg_row.reshape(1, keys))


def ffn_kernel(x_ref, gain_ref, gate_ref, up_ref, down_ref, out_ref):
    normed = (rms_rows(x_ref[...].astype(jnp.float32)) * gain_ref[...]).astype(jnp.bfloat16)
    contract = (((1,), (1,)), ((), ()))
    gate_proj = lax.dot_general(normed, gate_ref[...], contract, preferred_element_type=jnp.float32)
    up_proj = lax.dot_general(normed, up_ref[...], contract, preferred_element_type=jnp.float32)
    hidden = (gate_proj / (1.0 + jnp.exp(-gate_proj)) * up_proj).astype(jnp.bfloat16)
    out_ref[...] = jnp.dot(hidden, down_ref[...], preferred_element_type=jnp.float32).astype(
        out_ref.dtype
    )


def ffn_partial(rows, gain, gate_weight, up_weight, down_weight, tile):
    count, width = rows.shape
    hidden_w = gate_weight.shape[1]
    full = lambda i: (0, 0)
    gate_t = gate_weight.T
    up_t = up_weight.T
    return pl.pallas_call(
        ffn_kernel,
        out_shape=jax.ShapeDtypeStruct((count, width), jnp.bfloat16),
        grid=(count // tile,),
        in_specs=[
            pl.BlockSpec((tile, width), lambda i: (i, 0)),
            pl.BlockSpec((1, width), full),
            pl.BlockSpec((hidden_w, width), full),
            pl.BlockSpec((hidden_w, width), full),
            pl.BlockSpec((hidden_w, width), full),
        ],
        out_specs=pl.BlockSpec((tile, width), lambda i: (i, 0)),
        compiler_params=pltpu.CompilerParams(
            dimension_semantics=("arbitrary",), vmem_limit_bytes=48 * 1024 * 1024
        ),
        cost_estimate=pl.CostEstimate(
            flops=6 * count * width * hidden_w,
            bytes_accessed=3 * width * hidden_w * 2 + 2 * count * width * 2,
            transcendentals=count * hidden_w,
        ),
    )(rows, gain.reshape(1, width), gate_t, up_t, down_weight)


def body(
    layer_input,
    q_in,
    k_in,
    v_in,
    segment_ids,
    lambda_parts,
    out_weight,
    ffn_gain,
    gate_weight,
    up_weight,
    down_weight,
    next_gain,
    qkv_weight,
    page_owner,
    page_slot,
):
    row_count = q_in.shape[0]
    feat_width = q_in.shape[1]
    head_dim = feat_width // (2 * HEADS)
    peer_count = lax.axis_size("tok")
    tok_place = lax.axis_index("tok")
    seg_row = segment_ids[0]
    first_row = tok_place * row_count
    query_places = first_row + jnp.arange(row_count)
    query_segs = lax.dynamic_slice_in_dim(seg_row, first_row, row_count)
    lambda_mix = lambda_value(lambda_parts)
    score_scale = 1.0 / math.sqrt(head_dim)
    query_split = q_in.reshape(row_count, HEADS, 2, head_dim)
    run_max = jnp.full((HEADS, 2, row_count), NEG_FILL, jnp.float32)
    back = -(-(MAX_SEG - 1) // row_count)
    own_kv = jnp.concatenate([k_in, v_in], axis=1)
    all_kv = lax.all_gather(own_kv, "tok", axis=0, tiled=True)
    attention = window_attention(q_in, all_kv, query_segs, seg_row, first_row, lambda_mix, back)
    residual_mid = (
        layer_input.astype(jnp.float32)
        + jnp.dot(attention, out_weight, preferred_element_type=jnp.float32)
    ).astype(jnp.bfloat16)
    gathered = lax.all_gather(residual_mid, "req", axis=0, tiled=True)
    partial = ffn_partial(gathered, ffn_gain, gate_weight, up_weight, down_weight, 256)
    ffn_own = lax.psum_scatter(partial, "req", scatter_dimension=0, tiled=True).astype(jnp.float32)
    layer_output = (residual_mid.astype(jnp.float32) + ffn_own).astype(jnp.bfloat16)
    next_normed = (rms_rows(layer_output.astype(jnp.float32)) * next_gain).astype(jnp.bfloat16)
    projected_cols = jnp.dot(
        lax.all_gather(next_normed, "req", axis=0, tiled=True),
        qkv_weight,
        preferred_element_type=jnp.float32,
    ).astype(jnp.bfloat16)
    n_req = lax.axis_size("req")
    col_w = projected_cols.shape[1]
    arrived = lax.all_to_all(
        projected_cols.reshape(n_req, row_count, col_w), "req", 0, 0, tiled=True
    )
    projected = jnp.transpose(arrived, (1, 0, 2)).reshape(row_count, n_req * col_w)
    q_next = projected[:, :feat_width]
    pages_dev = row_count // PAGE
    assert pages_dev == peer_count
    key_values = projected[:, feat_width:].reshape(pages_dev, PAGE, 2 * feat_width)
    owner_all = page_owner[0].reshape(peer_count, pages_dev)
    slot_all = page_slot[0].reshape(peer_count, pages_dev)
    numbers = jnp.arange(pages_dev, dtype=jnp.int32)
    my_owners = lax.dynamic_index_in_dim(owner_all, tok_place, 0, keepdims=False)
    send_order = jnp.sum(
        jnp.where(my_owners[None, :] == numbers[:, None], numbers[None, :], 0), axis=1
    )
    outgoing = key_values[send_order].reshape(peer_count, 1, PAGE, 2 * feat_width)
    incoming = lax.all_to_all(outgoing, "tok", split_axis=0, concat_axis=0, tiled=True)
    incoming = incoming.reshape(pages_dev, PAGE, 2 * feat_width)
    slot_list = jnp.sum(jnp.where(owner_all == tok_place, slot_all, 0), axis=1)
    source_of_slot = jnp.sum(
        jnp.where(slot_list[None, :] == numbers[:, None], numbers[None, :], 0), axis=1
    )
    page_cache = incoming[source_of_slot]
    return (layer_output, q_next, page_cache)


def solution(mesh):
    in_specs = (
        P(("req", "tok"), None),
        P(("req", "tok"), None),
        P(("req", "tok"), None),
        P(("req", "tok"), None),
        P("req", None),
        P(),
        P(),
        P(),
        P(None, "req"),
        P(None, "req"),
        P("req", None),
        P(),
        P(None, "req"),
        P("req", None),
        P("req", None),
    )
    out_specs = (P(("req", "tok"), None), P(("req", "tok"), None), P(("req", "tok"), None, None))
    return jax.shard_map(body, mesh=mesh, in_specs=in_specs, out_specs=out_specs, check_vma=False)
```

```python
import functools
import math

import jax
import jax.numpy as jnp
from jax import lax
from jax.experimental import pallas as pl
from jax.experimental.pallas import tpu as pltpu
from jax.sharding import PartitionSpec as P

HEADS = 8
PAGE = 8


NEG_FILL = -1e30
LAMBDA_INIT = 0.2
EPSILON = 1e-05
MAX_SEG = 1024


def rms_rows(values):
    return values * lax.rsqrt(jnp.mean(values * values, axis=-1, keepdims=True) + EPSILON)


def lambda_value(lambda_parts):
    first_term = jnp.exp(jnp.sum(lambda_parts[0] * lambda_parts[1]))
    second_term = jnp.exp(jnp.sum(lambda_parts[2] * lambda_parts[3]))
    return first_term - second_term + LAMBDA_INIT


def attention_kernel(back, head_dim, scalars_ref, lam_ref, q_ref, k_ref, v_ref, qseg_ref, kseg_ref, out_ref):
    rows = q_ref.shape[0]
    span = (back + 1) * rows
    start = pl.multiple_of(scalars_ref[0], rows)
    query_places = scalars_ref[1] + lax.broadcasted_iota(jnp.int32, (rows, span), 0)
    key_places = start + lax.broadcasted_iota(jnp.int32, (rows, span), 1)
    key_segs = kseg_ref[:, pl.ds(start, span)]
    visible = (key_segs == qseg_ref[...]) & (key_places <= query_places)
    values = v_ref[pl.ds(start, span), :]
    score_scale = 1.0 / math.sqrt(head_dim)
    map_outputs = []
    for map_index in range(2):
        query_map = q_ref[:, map_index * head_dim:(map_index + 1) * head_dim]
        key_map = k_ref[pl.ds(start, span), map_index * head_dim:(map_index + 1) * head_dim]
        scores = (
            lax.dot_general(
                query_map, key_map, (((1,), (1,)), ((), ())), preferred_element_type=jnp.float32
            )
            * score_scale
        )
        scores = jnp.where(visible, scores, NEG_FILL)
        row_max = jnp.max(scores, axis=1, keepdims=True)
        weights = jnp.where(visible, jnp.exp(scores - row_max), 0.0)
        totals = jnp.sum(weights, axis=1, keepdims=True)
        map_out = (
            jnp.dot(weights.astype(jnp.bfloat16), values, preferred_element_type=jnp.float32) / totals
        )
        map_outputs.append(map_out)
    difference = map_outputs[0] - lam_ref[0] * map_outputs[1]
    out_ref[...] = (rms_rows(difference) * (1.0 - LAMBDA_INIT)).astype(out_ref.dtype)


def window_attention(q_in, all_kv, query_segs, seg_row, first_row, lambda_mix, back):
    rows, width = q_in.shape
    keys = all_kv.shape[0]
    head_w = width // HEADS
    start = jnp.maximum(first_row - back * rows, 0)
    scalars = jnp.stack([start, first_row]).astype(jnp.int32)
    lam = jnp.reshape(lambda_mix, (1,)).astype(jnp.float32)
    span = (back + 1) * rows
    flops = HEADS * 2 * (2 * rows * span * (head_w // 2) + 2 * rows * span * head_w)
    smem = pl.BlockSpec(memory_space=pltpu.SMEM)
    return pl.pallas_call(
        functools.partial(attention_kernel, back, head_w // 2),
        out_shape=jax.ShapeDtypeStruct((rows, width), jnp.bfloat16),
        grid=(HEADS,),
        in_specs=[
            smem,
            smem,
            pl.BlockSpec((rows, head_w), lambda h: (0, h)),
            pl.BlockSpec((keys, head_w), lambda h: (0, h)),
            pl.BlockSpec((keys, head_w), lambda h: (0, HEADS + h)),
            pl.BlockSpec((rows, 1), lambda h: (0, 0)),
            pl.BlockSpec((1, keys), lambda h: (0, 0)),
        ],
        out_specs=pl.BlockSpec((rows, head_w), lambda h: (0, h)),
        compiler_params=pltpu.CompilerParams(dimension_semantics=("arbitrary",)),
        cost_estimate=pl.CostEstimate(
            flops=flops,
            bytes_accessed=2 * keys * width * 2 + 2 * rows * width * 2,
            transcendentals=HEADS * 2 * rows * span,
        ),
    )(scalars, lam, q_in, all_kv, all_kv, query_segs.reshape(rows, 1), seg_row.reshape(1, keys))


def ffn_kernel(x_ref, gain_ref, gate_ref, up_ref, down_ref, out_ref, normed_ref, total_ref):
    step = pl.program_id(0)

    @pl.when(step == 0)
    def _():
        normed_ref[...] = (rms_rows(x_ref[...].astype(jnp.float32)) * gain_ref[...]).astype(
            jnp.bfloat16
        )
        total_ref[...] = jnp.zeros_like(total_ref)

    normed = normed_ref[...]
    contract = (((1,), (1,)), ((), ()))
    gate_proj = lax.dot_general(normed, gate_ref[...], contract, preferred_element_type=jnp.float32)
    up_proj = lax.dot_general(normed, up_ref[...], contract, preferred_element_type=jnp.float32)
    hidden = (gate_proj / (1.0 + jnp.exp(-gate_proj)) * up_proj).astype(jnp.bfloat16)
    total_ref[...] += jnp.dot(hidden, down_ref[...], preferred_element_type=jnp.float32)

    @pl.when(step == pl.num_programs(0) - 1)
    def _():
        out_ref[...] = total_ref[...].astype(out_ref.dtype)


def ffn_partial(rows, gain, gate_weight, up_weight, down_weight, chunk):
    count, width = rows.shape
    hidden_w = gate_weight.shape[1]
    full = lambda i: (0, 0)
    part = lambda i: (i, 0)
    return pl.pallas_call(
        ffn_kernel,
        out_shape=jax.ShapeDtypeStruct((count, width), jnp.bfloat16),
        grid=(hidden_w // chunk,),
        in_specs=[
            pl.BlockSpec((count, width), full),
            pl.BlockSpec((1, width), full),
            pl.BlockSpec((chunk, width), part),
            pl.BlockSpec((chunk, width), part),
            pl.BlockSpec((chunk, width), part),
        ],
        out_specs=pl.BlockSpec((count, width), full),
        scratch_shapes=[
            pltpu.VMEM((count, width), jnp.bfloat16),
            pltpu.VMEM((count, width), jnp.float32),
        ],
        compiler_params=pltpu.CompilerParams(
            dimension_semantics=("arbitrary",), vmem_limit_bytes=56 * 1024 * 1024
        ),
        cost_estimate=pl.CostEstimate(
            flops=6 * count * width * hidden_w,
            bytes_accessed=3 * width * hidden_w * 2 + 2 * count * width * 2,
            transcendentals=count * hidden_w,
        ),
    )(rows, gain.reshape(1, width), gate_weight.T, up_weight.T, down_weight)


def body(
    layer_input,
    q_in,
    k_in,
    v_in,
    segment_ids,
    lambda_parts,
    out_weight,
    ffn_gain,
    gate_weight,
    up_weight,
    down_weight,
    next_gain,
    qkv_weight,
    page_owner,
    page_slot,
):
    row_count = q_in.shape[0]
    feat_width = q_in.shape[1]
    head_dim = feat_width // (2 * HEADS)
    peer_count = lax.axis_size("tok")
    tok_place = lax.axis_index("tok")
    seg_row = segment_ids[0]
    first_row = tok_place * row_count
    query_places = first_row + jnp.arange(row_count)
    query_segs = lax.dynamic_slice_in_dim(seg_row, first_row, row_count)
    lambda_mix = lambda_value(lambda_parts)
    score_scale = 1.0 / math.sqrt(head_dim)
    query_split = q_in.reshape(row_count, HEADS, 2, head_dim)
    run_max = jnp.full((HEADS, 2, row_count), NEG_FILL, jnp.float32)
    back = -(-(MAX_SEG - 1) // row_count)
    own_kv = jnp.concatenate([k_in, v_in], axis=1)
    all_kv = lax.all_gather(own_kv, "tok", axis=0, tiled=True)
    attention = window_attention(q_in, all_kv, query_segs, seg_row, first_row, lambda_mix, back)
    residual_mid = (
        layer_input.astype(jnp.float32)
        + jnp.dot(attention, out_weight, preferred_element_type=jnp.float32)
    ).astype(jnp.bfloat16)
    gathered = lax.all_gather(residual_mid, "req", axis=0, tiled=True)
    partial = ffn_partial(gathered, ffn_gain, gate_weight, up_weight, down_weight, 176)
    ffn_own = lax.psum_scatter(partial, "req", scatter_dimension=0, tiled=True).astype(jnp.float32)
    layer_output = (residual_mid.astype(jnp.float32) + ffn_own).astype(jnp.bfloat16)
    next_normed = (rms_rows(layer_output.astype(jnp.float32)) * next_gain).astype(jnp.bfloat16)
    projected_cols = jnp.dot(
        lax.all_gather(next_normed, "req", axis=0, tiled=True),
        qkv_weight,
        preferred_element_type=jnp.float32,
    ).astype(jnp.bfloat16)
    n_req = lax.axis_size("req")
    col_w = projected_cols.shape[1]
    arrived = lax.all_to_all(
        projected_cols.reshape(n_req, row_count, col_w), "req", 0, 0, tiled=True
    )
    projected = jnp.transpose(arrived, (1, 0, 2)).reshape(row_count, n_req * col_w)
    q_next = projected[:, :feat_width]
    pages_dev = row_count // PAGE
    assert pages_dev == peer_count
    key_values = projected[:, feat_width:].reshape(pages_dev, PAGE, 2 * feat_width)
    owner_all = page_owner[0].reshape(peer_count, pages_dev)
    slot_all = page_slot[0].reshape(peer_count, pages_dev)
    numbers = jnp.arange(pages_dev, dtype=jnp.int32)
    my_owners = lax.dynamic_index_in_dim(owner_all, tok_place, 0, keepdims=False)
    send_order = jnp.sum(
        jnp.where(my_owners[None, :] == numbers[:, None], numbers[None, :], 0), axis=1
    )
    outgoing = key_values[send_order].reshape(peer_count, 1, PAGE, 2 * feat_width)
    incoming = lax.all_to_all(outgoing, "tok", split_axis=0, concat_axis=0, tiled=True)
    incoming = incoming.reshape(pages_dev, PAGE, 2 * feat_width)
    slot_list = jnp.sum(jnp.where(owner_all == tok_place, slot_all, 0), axis=1)
    source_of_slot = jnp.sum(
        jnp.where(slot_list[None, :] == numbers[:, None], numbers[None, :], 0), axis=1
    )
    page_cache = incoming[source_of_slot]
    return (layer_output, q_next, page_cache)


def solution(mesh):
    in_specs = (
        P(("req", "tok"), None),
        P(("req", "tok"), None),
        P(("req", "tok"), None),
        P(("req", "tok"), None),
        P("req", None),
        P(),
        P(),
        P(),
        P(None, "req"),
        P(None, "req"),
        P("req", None),
        P(),
        P(None, "req"),
        P("req", None),
        P("req", None),
    )
    out_specs = (P(("req", "tok"), None), P(("req", "tok"), None), P(("req", "tok"), None, None))
    return jax.shard_map(body, mesh=mesh, in_specs=in_specs, out_specs=out_specs, check_vma=False)
```

```python
import functools
import math

import jax
import jax.numpy as jnp
from jax import lax
from jax.experimental import pallas as pl
from jax.experimental.pallas import tpu as pltpu
from jax.sharding import PartitionSpec as P

HEADS = 8
PAGE = 8


NEG_FILL = -1e30
LAMBDA_INIT = 0.2
EPSILON = 1e-05
MAX_SEG = 1024


def rms_rows(values):
    return values * lax.rsqrt(jnp.mean(values * values, axis=-1, keepdims=True) + EPSILON)


def lambda_value(lambda_parts):
    first_term = jnp.exp(jnp.sum(lambda_parts[0] * lambda_parts[1]))
    second_term = jnp.exp(jnp.sum(lambda_parts[2] * lambda_parts[3]))
    return first_term - second_term + LAMBDA_INIT


def attention_kernel(
    back, head_dim, scalars_ref, lam_ref, q_ref, k_ref, v_ref, qseg_ref, kseg_ref, w_ref, base_ref, out_ref, total_ref
):
    rows = q_ref.shape[0]
    span = (back + 1) * rows
    start = pl.multiple_of(scalars_ref[0], rows)
    query_places = scalars_ref[1] + lax.broadcasted_iota(jnp.int32, (rows, span), 0)
    key_places = start + lax.broadcasted_iota(jnp.int32, (rows, span), 1)
    key_segs = kseg_ref[:, pl.ds(start, span)]
    visible = (key_segs == qseg_ref[...]) & (key_places <= query_places)
    values = v_ref[pl.ds(start, span), :]
    score_scale = 1.0 / math.sqrt(head_dim)
    map_outputs = []
    for map_index in range(2):
        query_map = q_ref[:, map_index * head_dim:(map_index + 1) * head_dim]
        key_map = k_ref[pl.ds(start, span), map_index * head_dim:(map_index + 1) * head_dim]
        scores = (
            lax.dot_general(
                query_map, key_map, (((1,), (1,)), ((), ())), preferred_element_type=jnp.float32
            )
            * score_scale
        )
        scores = jnp.where(visible, scores, NEG_FILL)
        row_max = jnp.max(scores, axis=1, keepdims=True)
        weights = jnp.where(visible, jnp.exp(scores - row_max), 0.0)
        totals = jnp.sum(weights, axis=1, keepdims=True)
        map_out = (
            jnp.dot(weights.astype(jnp.bfloat16), values, preferred_element_type=jnp.float32) / totals
        )
        map_outputs.append(map_out)
    difference = map_outputs[0] - lam_ref[0] * map_outputs[1]
    head_out = (rms_rows(difference) * (1.0 - LAMBDA_INIT)).astype(jnp.bfloat16)
    step = pl.program_id(0)

    @pl.when(step == 0)
    def _():
        total_ref[...] = jnp.zeros_like(total_ref)

    total_ref[...] += jnp.dot(head_out, w_ref[...], preferred_element_type=jnp.float32)

    @pl.when(step == pl.num_programs(0) - 1)
    def _():
        out_ref[...] = (base_ref[...].astype(jnp.float32) + total_ref[...]).astype(out_ref.dtype)


def window_attention(q_in, all_kv, query_segs, seg_row, first_row, lambda_mix, back, out_weight, base):
    rows, width = q_in.shape
    keys = all_kv.shape[0]
    head_w = width // HEADS
    start = jnp.maximum(first_row - back * rows, 0)
    scalars = jnp.stack([start, first_row]).astype(jnp.int32)
    lam = jnp.reshape(lambda_mix, (1,)).astype(jnp.float32)
    span = (back + 1) * rows
    flops = HEADS * 2 * (2 * rows * span * (head_w // 2) + 2 * rows * span * head_w) + 2 * rows * width * width
    smem = pl.BlockSpec(memory_space=pltpu.SMEM)
    return pl.pallas_call(
        functools.partial(attention_kernel, back, head_w // 2),
        out_shape=jax.ShapeDtypeStruct((rows, width), jnp.bfloat16),
        grid=(HEADS,),
        in_specs=[
            smem,
            smem,
            pl.BlockSpec((rows, head_w), lambda h: (0, h)),
            pl.BlockSpec((keys, head_w), lambda h: (0, h)),
            pl.BlockSpec((keys, head_w), lambda h: (0, HEADS + h)),
            pl.BlockSpec((rows, 1), lambda h: (0, 0)),
            pl.BlockSpec((1, keys), lambda h: (0, 0)),
            pl.BlockSpec((head_w, width), lambda h: (h, 0)),
            pl.BlockSpec((rows, width), lambda h: (0, 0)),
        ],
        out_specs=pl.BlockSpec((rows, width), lambda h: (0, 0)),
        scratch_shapes=[pltpu.VMEM((rows, width), jnp.float32)],
        compiler_params=pltpu.CompilerParams(dimension_semantics=("arbitrary",)),
        cost_estimate=pl.CostEstimate(
            flops=flops,
            bytes_accessed=2 * keys * width * 2 + 3 * rows * width * 2 + width * width * 2,
            transcendentals=HEADS * 2 * rows * span,
        ),
    )(
        scalars,
        lam,
        q_in,
        all_kv,
        all_kv,
        query_segs.reshape(rows, 1),
        seg_row.reshape(1, keys),
        out_weight,
        base,
    )


def ffn_kernel(x_ref, gain_ref, gate_ref, up_ref, down_ref, out_ref):
    normed = (rms_rows(x_ref[...].astype(jnp.float32)) * gain_ref[...]).astype(jnp.bfloat16)
    contract = (((1,), (1,)), ((), ()))
    gate_proj = lax.dot_general(normed, gate_ref[...], contract, preferred_element_type=jnp.float32)
    up_proj = lax.dot_general(normed, up_ref[...], contract, preferred_element_type=jnp.float32)
    hidden = (gate_proj / (1.0 + jnp.exp(-gate_proj)) * up_proj).astype(jnp.bfloat16)
    out_ref[...] = jnp.dot(hidden, down_ref[...], preferred_element_type=jnp.float32).astype(
        out_ref.dtype
    )


def ffn_partial(rows, gain, gate_weight, up_weight, down_weight, tile):
    count, width = rows.shape
    hidden_w = gate_weight.shape[1]
    full = lambda i: (0, 0)
    gate_t = gate_weight.T
    up_t = up_weight.T
    return pl.pallas_call(
        ffn_kernel,
        out_shape=jax.ShapeDtypeStruct((count, width), jnp.bfloat16),
        grid=(count // tile,),
        in_specs=[
            pl.BlockSpec((tile, width), lambda i: (i, 0)),
            pl.BlockSpec((1, width), full),
            pl.BlockSpec((hidden_w, width), full),
            pl.BlockSpec((hidden_w, width), full),
            pl.BlockSpec((hidden_w, width), full),
        ],
        out_specs=pl.BlockSpec((tile, width), lambda i: (i, 0)),
        compiler_params=pltpu.CompilerParams(
            dimension_semantics=("arbitrary",), vmem_limit_bytes=48 * 1024 * 1024
        ),
        cost_estimate=pl.CostEstimate(
            flops=6 * count * width * hidden_w,
            bytes_accessed=3 * width * hidden_w * 2 + 2 * count * width * 2,
            transcendentals=count * hidden_w,
        ),
    )(rows, gain.reshape(1, width), gate_t, up_t, down_weight)


def body(
    layer_input,
    q_in,
    k_in,
    v_in,
    segment_ids,
    lambda_parts,
    out_weight,
    ffn_gain,
    gate_weight,
    up_weight,
    down_weight,
    next_gain,
    qkv_weight,
    page_owner,
    page_slot,
):
    row_count = q_in.shape[0]
    feat_width = q_in.shape[1]
    head_dim = feat_width // (2 * HEADS)
    peer_count = lax.axis_size("tok")
    tok_place = lax.axis_index("tok")
    seg_row = segment_ids[0]
    first_row = tok_place * row_count
    query_places = first_row + jnp.arange(row_count)
    query_segs = lax.dynamic_slice_in_dim(seg_row, first_row, row_count)
    lambda_mix = lambda_value(lambda_parts)
    score_scale = 1.0 / math.sqrt(head_dim)
    query_split = q_in.reshape(row_count, HEADS, 2, head_dim)
    run_max = jnp.full((HEADS, 2, row_count), NEG_FILL, jnp.float32)
    back = -(-(MAX_SEG - 1) // row_count)
    own_kv = jnp.concatenate([k_in, v_in], axis=1)
    all_kv = lax.all_gather(own_kv, "tok", axis=0, tiled=True)
    residual_mid = window_attention(
        q_in, all_kv, query_segs, seg_row, first_row, lambda_mix, back, out_weight, layer_input
    )
    gathered = lax.all_gather(residual_mid, "req", axis=0, tiled=True)
    partial = ffn_partial(gathered, ffn_gain, gate_weight, up_weight, down_weight, 256)
    ffn_own = lax.psum_scatter(partial, "req", scatter_dimension=0, tiled=True).astype(jnp.float32)
    layer_output = (residual_mid.astype(jnp.float32) + ffn_own).astype(jnp.bfloat16)
    next_normed = (rms_rows(layer_output.astype(jnp.float32)) * next_gain).astype(jnp.bfloat16)
    projected_cols = jnp.dot(
        lax.all_gather(next_normed, "req", axis=0, tiled=True),
        qkv_weight,
        preferred_element_type=jnp.float32,
    ).astype(jnp.bfloat16)
    n_req = lax.axis_size("req")
    col_w = projected_cols.shape[1]
    arrived = lax.all_to_all(
        projected_cols.reshape(n_req, row_count, col_w), "req", 0, 0, tiled=True
    )
    projected = jnp.transpose(arrived, (1, 0, 2)).reshape(row_count, n_req * col_w)
    q_next = projected[:, :feat_width]
    pages_dev = row_count // PAGE
    assert pages_dev == peer_count
    key_values = projected[:, feat_width:].reshape(pages_dev, PAGE, 2 * feat_width)
    owner_all = page_owner[0].reshape(peer_count, pages_dev)
    slot_all = page_slot[0].reshape(peer_count, pages_dev)
    numbers = jnp.arange(pages_dev, dtype=jnp.int32)
    my_owners = lax.dynamic_index_in_dim(owner_all, tok_place, 0, keepdims=False)
    send_order = jnp.sum(
        jnp.where(my_owners[None, :] == numbers[:, None], numbers[None, :], 0), axis=1
    )
    outgoing = key_values[send_order].reshape(peer_count, 1, PAGE, 2 * feat_width)
    incoming = lax.all_to_all(outgoing, "tok", split_axis=0, concat_axis=0, tiled=True)
    incoming = incoming.reshape(pages_dev, PAGE, 2 * feat_width)
    slot_list = jnp.sum(jnp.where(owner_all == tok_place, slot_all, 0), axis=1)
    source_of_slot = jnp.sum(
        jnp.where(slot_list[None, :] == numbers[:, None], numbers[None, :], 0), axis=1
    )
    page_cache = incoming[source_of_slot]
    return (layer_output, q_next, page_cache)


def solution(mesh):
    in_specs = (
        P(("req", "tok"), None),
        P(("req", "tok"), None),
        P(("req", "tok"), None),
        P(("req", "tok"), None),
        P("req", None),
        P(),
        P(),
        P(),
        P(None, "req"),
        P(None, "req"),
        P("req", None),
        P(),
        P(None, "req"),
        P("req", None),
        P("req", None),
    )
    out_specs = (P(("req", "tok"), None), P(("req", "tok"), None), P(("req", "tok"), None, None))
    return jax.shard_map(body, mesh=mesh, in_specs=in_specs, out_specs=out_specs, check_vma=False)
```

```python
import functools
import math

import jax
import jax.numpy as jnp
from jax import lax
from jax.experimental import pallas as pl
from jax.experimental.pallas import tpu as pltpu
from jax.sharding import PartitionSpec as P

HEADS = 8
PAGE = 8


NEG_FILL = -1e30
LAMBDA_INIT = 0.2
EPSILON = 1e-05
MAX_SEG = 1024


def rms_rows(values):
    return values * lax.rsqrt(jnp.mean(values * values, axis=-1, keepdims=True) + EPSILON)


def lambda_value(lambda_parts):
    first_term = jnp.exp(jnp.sum(lambda_parts[0] * lambda_parts[1]))
    second_term = jnp.exp(jnp.sum(lambda_parts[2] * lambda_parts[3]))
    return first_term - second_term + LAMBDA_INIT


def attention_kernel(
    back, head_dim, scalars_ref, lam_ref, q_ref, k_ref, v_ref, qseg_ref, kseg_ref, w_ref, base_ref, out_ref, total_ref
):
    rows = q_ref.shape[0]
    span = (back + 1) * rows
    start = pl.multiple_of(scalars_ref[0], rows)
    query_places = scalars_ref[1] + lax.broadcasted_iota(jnp.int32, (rows, span), 0)
    key_places = start + lax.broadcasted_iota(jnp.int32, (rows, span), 1)
    key_segs = kseg_ref[:, pl.ds(start, span)]
    visible = (key_segs == qseg_ref[...]) & (key_places <= query_places)
    values = v_ref[pl.ds(start, span), :]
    score_scale = 1.0 / math.sqrt(head_dim)
    map_outputs = []
    for map_index in range(2):
        query_map = q_ref[:, map_index * head_dim:(map_index + 1) * head_dim]
        key_map = k_ref[pl.ds(start, span), map_index * head_dim:(map_index + 1) * head_dim]
        scores = (
            lax.dot_general(
                query_map, key_map, (((1,), (1,)), ((), ())), preferred_element_type=jnp.float32
            )
            * score_scale
        )
        scores = jnp.where(visible, scores, NEG_FILL)
        row_max = jnp.max(scores, axis=1, keepdims=True)
        weights = jnp.where(visible, jnp.exp(scores - row_max), 0.0)
        totals = jnp.sum(weights, axis=1, keepdims=True)
        map_out = (
            jnp.dot(weights.astype(jnp.bfloat16), values, preferred_element_type=jnp.float32) / totals
        )
        map_outputs.append(map_out)
    difference = map_outputs[0] - lam_ref[0] * map_outputs[1]
    head_out = (rms_rows(difference) * (1.0 - LAMBDA_INIT)).astype(jnp.bfloat16)
    step = pl.program_id(0)

    @pl.when(step == 0)
    def _():
        total_ref[...] = jnp.zeros_like(total_ref)

    total_ref[...] += jnp.dot(head_out, w_ref[...], preferred_element_type=jnp.float32)

    @pl.when(step == pl.num_programs(0) - 1)
    def _():
        out_ref[...] = (base_ref[...].astype(jnp.float32) + total_ref[...]).astype(out_ref.dtype)


def window_attention(q_in, all_kv, query_segs, seg_row, first_row, lambda_mix, back, out_weight, base):
    rows, width = q_in.shape
    keys = all_kv.shape[0]
    head_w = width // HEADS
    start = jnp.maximum(first_row - back * rows, 0)
    scalars = jnp.stack([start, first_row]).astype(jnp.int32)
    lam = jnp.reshape(lambda_mix, (1,)).astype(jnp.float32)
    span = (back + 1) * rows
    flops = HEADS * 2 * (2 * rows * span * (head_w // 2) + 2 * rows * span * head_w) + 2 * rows * width * width
    smem = pl.BlockSpec(memory_space=pltpu.SMEM)
    return pl.pallas_call(
        functools.partial(attention_kernel, back, head_w // 2),
        out_shape=jax.ShapeDtypeStruct((rows, width), jnp.bfloat16),
        grid=(HEADS,),
        in_specs=[
            smem,
            smem,
            pl.BlockSpec((rows, head_w), lambda h: (0, h)),
            pl.BlockSpec((keys, head_w), lambda h: (0, h)),
            pl.BlockSpec((keys, head_w), lambda h: (0, HEADS + h)),
            pl.BlockSpec((rows, 1), lambda h: (0, 0)),
            pl.BlockSpec((1, keys), lambda h: (0, 0)),
            pl.BlockSpec((head_w, width), lambda h: (h, 0)),
            pl.BlockSpec((rows, width), lambda h: (0, 0)),
        ],
        out_specs=pl.BlockSpec((rows, width), lambda h: (0, 0)),
        scratch_shapes=[pltpu.VMEM((rows, width), jnp.float32)],
        compiler_params=pltpu.CompilerParams(dimension_semantics=("arbitrary",)),
        cost_estimate=pl.CostEstimate(
            flops=flops,
            bytes_accessed=2 * keys * width * 2 + 3 * rows * width * 2 + width * width * 2,
            transcendentals=HEADS * 2 * rows * span,
        ),
    )(
        scalars,
        lam,
        q_in,
        all_kv,
        all_kv,
        query_segs.reshape(rows, 1),
        seg_row.reshape(1, keys),
        out_weight,
        base,
    )


def ffn_kernel(x_ref, gain_ref, gate_ref, up_ref, down_ref, out_ref):
    normed = (rms_rows(x_ref[...].astype(jnp.float32)) * gain_ref[...]).astype(jnp.bfloat16)
    contract = (((1,), (1,)), ((), ()))
    gate_proj = lax.dot_general(normed, gate_ref[...], contract, preferred_element_type=jnp.float32)
    up_proj = lax.dot_general(normed, up_ref[...], contract, preferred_element_type=jnp.float32)
    hidden = (gate_proj / (1.0 + jnp.exp(-gate_proj)) * up_proj).astype(jnp.bfloat16)
    out_ref[...] = jnp.dot(hidden, down_ref[...], preferred_element_type=jnp.float32).astype(
        out_ref.dtype
    )


def ffn_partial(rows, gain, gate_weight, up_weight, down_weight, tile):
    count, width = rows.shape
    hidden_w = gate_weight.shape[1]
    full = lambda i: (0, 0)
    gate_t = gate_weight.T
    up_t = up_weight.T
    return pl.pallas_call(
        ffn_kernel,
        out_shape=jax.ShapeDtypeStruct((count, width), jnp.bfloat16),
        grid=(count // tile,),
        in_specs=[
            pl.BlockSpec((tile, width), lambda i: (i, 0)),
            pl.BlockSpec((1, width), full),
            pl.BlockSpec((hidden_w, width), full),
            pl.BlockSpec((hidden_w, width), full),
            pl.BlockSpec((hidden_w, width), full),
        ],
        out_specs=pl.BlockSpec((tile, width), lambda i: (i, 0)),
        compiler_params=pltpu.CompilerParams(
            dimension_semantics=("arbitrary",), vmem_limit_bytes=48 * 1024 * 1024
        ),
        cost_estimate=pl.CostEstimate(
            flops=6 * count * width * hidden_w,
            bytes_accessed=3 * width * hidden_w * 2 + 2 * count * width * 2,
            transcendentals=count * hidden_w,
        ),
    )(rows, gain.reshape(1, width), gate_t, up_t, down_weight)


def project_kernel(x_ref, w_ref, out_ref):
    out_ref[...] = jnp.dot(x_ref[...], w_ref[...], preferred_element_type=jnp.float32).astype(
        out_ref.dtype
    )


def project_rows(rows, weight, tile):
    count, width = rows.shape
    cols = weight.shape[1]
    return pl.pallas_call(
        project_kernel,
        out_shape=jax.ShapeDtypeStruct((count, cols), jnp.bfloat16),
        grid=(count // tile,),
        in_specs=[
            pl.BlockSpec((tile, width), lambda i: (i, 0)),
            pl.BlockSpec((width, cols), lambda i: (0, 0)),
        ],
        out_specs=pl.BlockSpec((tile, cols), lambda i: (i, 0)),
        compiler_params=pltpu.CompilerParams(
            dimension_semantics=("arbitrary",), vmem_limit_bytes=48 * 1024 * 1024
        ),
        cost_estimate=pl.CostEstimate(
            flops=2 * count * width * cols,
            bytes_accessed=2 * (count * width + width * cols + count * cols),
            transcendentals=0,
        ),
    )(rows, weight)


def body(
    layer_input,
    q_in,
    k_in,
    v_in,
    segment_ids,
    lambda_parts,
    out_weight,
    ffn_gain,
    gate_weight,
    up_weight,
    down_weight,
    next_gain,
    qkv_weight,
    page_owner,
    page_slot,
):
    row_count = q_in.shape[0]
    feat_width = q_in.shape[1]
    head_dim = feat_width // (2 * HEADS)
    peer_count = lax.axis_size("tok")
    tok_place = lax.axis_index("tok")
    seg_row = segment_ids[0]
    first_row = tok_place * row_count
    query_places = first_row + jnp.arange(row_count)
    query_segs = lax.dynamic_slice_in_dim(seg_row, first_row, row_count)
    lambda_mix = lambda_value(lambda_parts)
    score_scale = 1.0 / math.sqrt(head_dim)
    query_split = q_in.reshape(row_count, HEADS, 2, head_dim)
    run_max = jnp.full((HEADS, 2, row_count), NEG_FILL, jnp.float32)
    back = -(-(MAX_SEG - 1) // row_count)
    own_kv = jnp.concatenate([k_in, v_in], axis=1)
    all_kv = lax.all_gather(own_kv, "tok", axis=0, tiled=True)
    residual_mid = window_attention(
        q_in, all_kv, query_segs, seg_row, first_row, lambda_mix, back, out_weight, layer_input
    )
    gathered = lax.all_gather(residual_mid, "req", axis=0, tiled=True)
    partial = ffn_partial(gathered, ffn_gain, gate_weight, up_weight, down_weight, 256)
    ffn_own = lax.psum_scatter(partial, "req", scatter_dimension=0, tiled=True).astype(jnp.float32)
    layer_output = (residual_mid.astype(jnp.float32) + ffn_own).astype(jnp.bfloat16)
    next_normed = (rms_rows(layer_output.astype(jnp.float32)) * next_gain).astype(jnp.bfloat16)
    projected_cols = project_rows(
        lax.all_gather(next_normed, "req", axis=0, tiled=True), qkv_weight, 256
    )
    n_req = lax.axis_size("req")
    col_w = projected_cols.shape[1]
    arrived = lax.all_to_all(
        projected_cols.reshape(n_req, row_count, col_w), "req", 0, 0, tiled=True
    )
    projected = jnp.transpose(arrived, (1, 0, 2)).reshape(row_count, n_req * col_w)
    q_next = projected[:, :feat_width]
    pages_dev = row_count // PAGE
    assert pages_dev == peer_count
    key_values = projected[:, feat_width:].reshape(pages_dev, PAGE, 2 * feat_width)
    owner_all = page_owner[0].reshape(peer_count, pages_dev)
    slot_all = page_slot[0].reshape(peer_count, pages_dev)
    numbers = jnp.arange(pages_dev, dtype=jnp.int32)
    my_owners = lax.dynamic_index_in_dim(owner_all, tok_place, 0, keepdims=False)
    send_order = jnp.sum(
        jnp.where(my_owners[None, :] == numbers[:, None], numbers[None, :], 0), axis=1
    )
    outgoing = key_values[send_order].reshape(peer_count, 1, PAGE, 2 * feat_width)
    incoming = lax.all_to_all(outgoing, "tok", split_axis=0, concat_axis=0, tiled=True)
    incoming = incoming.reshape(pages_dev, PAGE, 2 * feat_width)
    slot_list = jnp.sum(jnp.where(owner_all == tok_place, slot_all, 0), axis=1)
    source_of_slot = jnp.sum(
        jnp.where(slot_list[None, :] == numbers[:, None], numbers[None, :], 0), axis=1
    )
    page_cache = incoming[source_of_slot]
    return (layer_output, q_next, page_cache)


def solution(mesh):
    in_specs = (
        P(("req", "tok"), None),
        P(("req", "tok"), None),
        P(("req", "tok"), None),
        P(("req", "tok"), None),
        P("req", None),
        P(),
        P(),
        P(),
        P(None, "req"),
        P(None, "req"),
        P("req", None),
        P(),
        P(None, "req"),
        P("req", None),
        P("req", None),
    )
    out_specs = (P(("req", "tok"), None), P(("req", "tok"), None), P(("req", "tok"), None, None))
    return jax.shard_map(body, mesh=mesh, in_specs=in_specs, out_specs=out_specs, check_vma=False)
```

```python
import functools
import math

import jax
import jax.numpy as jnp
from jax import lax
from jax.experimental import pallas as pl
from jax.experimental.pallas import tpu as pltpu
from jax.sharding import PartitionSpec as P

HEADS = 8
PAGE = 8


NEG_FILL = -1e30
LAMBDA_INIT = 0.2
EPSILON = 1e-05
MAX_SEG = 1024


def rms_rows(values):
    return values * lax.rsqrt(jnp.mean(values * values, axis=-1, keepdims=True) + EPSILON)


def lambda_value(lambda_parts):
    first_term = jnp.exp(jnp.sum(lambda_parts[0] * lambda_parts[1]))
    second_term = jnp.exp(jnp.sum(lambda_parts[2] * lambda_parts[3]))
    return first_term - second_term + LAMBDA_INIT


def attention_kernel(
    back, head_dim, scalars_ref, lam_ref, q_ref, k_ref, v_ref, qseg_ref, kseg_ref, w_ref, base_ref, out_ref, total_ref
):
    rows = q_ref.shape[0]
    span = (back + 1) * rows
    start = pl.multiple_of(scalars_ref[0], rows)
    query_places = scalars_ref[1] + lax.broadcasted_iota(jnp.int32, (rows, span), 0)
    key_places = start + lax.broadcasted_iota(jnp.int32, (rows, span), 1)
    key_segs = kseg_ref[:, pl.ds(start, span)]
    visible = (key_segs == qseg_ref[...]) & (key_places <= query_places)
    values = v_ref[pl.ds(start, span), :]
    score_scale = 1.0 / math.sqrt(head_dim)
    map_outputs = []
    for map_index in range(2):
        query_map = q_ref[:, map_index * head_dim:(map_index + 1) * head_dim]
        key_map = k_ref[pl.ds(start, span), map_index * head_dim:(map_index + 1) * head_dim]
        scores = (
            lax.dot_general(
                query_map, key_map, (((1,), (1,)), ((), ())), preferred_element_type=jnp.float32
            )
            * score_scale
        )
        scores = jnp.where(visible, scores, NEG_FILL)
        row_max = jnp.max(scores, axis=1, keepdims=True)
        weights = jnp.where(visible, jnp.exp(scores - row_max), 0.0)
        totals = jnp.sum(weights, axis=1, keepdims=True)
        map_out = (
            jnp.dot(weights.astype(jnp.bfloat16), values, preferred_element_type=jnp.float32) / totals
        )
        map_outputs.append(map_out)
    difference = map_outputs[0] - lam_ref[0] * map_outputs[1]
    head_out = (rms_rows(difference) * (1.0 - LAMBDA_INIT)).astype(jnp.bfloat16)
    step = pl.program_id(0)

    @pl.when(step == 0)
    def _():
        total_ref[...] = jnp.zeros_like(total_ref)

    total_ref[...] += jnp.dot(head_out, w_ref[...], preferred_element_type=jnp.float32)

    @pl.when(step == pl.num_programs(0) - 1)
    def _():
        out_ref[...] = (base_ref[...].astype(jnp.float32) + total_ref[...]).astype(out_ref.dtype)


def window_attention(q_in, all_kv, query_segs, seg_row, first_row, lambda_mix, back, out_weight, base):
    rows, width = q_in.shape
    keys = all_kv.shape[0]
    head_w = width // HEADS
    start = jnp.maximum(first_row - back * rows, 0)
    scalars = jnp.stack([start, first_row]).astype(jnp.int32)
    lam = jnp.reshape(lambda_mix, (1,)).astype(jnp.float32)
    span = (back + 1) * rows
    flops = HEADS * 2 * (2 * rows * span * (head_w // 2) + 2 * rows * span * head_w) + 2 * rows * width * width
    smem = pl.BlockSpec(memory_space=pltpu.SMEM)
    return pl.pallas_call(
        functools.partial(attention_kernel, back, head_w // 2),
        out_shape=jax.ShapeDtypeStruct((rows, width), jnp.bfloat16),
        grid=(HEADS,),
        in_specs=[
            smem,
            smem,
            pl.BlockSpec((rows, head_w), lambda h: (0, h)),
            pl.BlockSpec((keys, head_w), lambda h: (0, h)),
            pl.BlockSpec((keys, head_w), lambda h: (0, HEADS + h)),
            pl.BlockSpec((rows, 1), lambda h: (0, 0)),
            pl.BlockSpec((1, keys), lambda h: (0, 0)),
            pl.BlockSpec((head_w, width), lambda h: (h, 0)),
            pl.BlockSpec((rows, width), lambda h: (0, 0)),
        ],
        out_specs=pl.BlockSpec((rows, width), lambda h: (0, 0)),
        scratch_shapes=[pltpu.VMEM((rows, width), jnp.float32)],
        compiler_params=pltpu.CompilerParams(dimension_semantics=("arbitrary",)),
        cost_estimate=pl.CostEstimate(
            flops=flops,
            bytes_accessed=2 * keys * width * 2 + 3 * rows * width * 2 + width * width * 2,
            transcendentals=HEADS * 2 * rows * span,
        ),
    )(
        scalars,
        lam,
        q_in,
        all_kv,
        all_kv,
        query_segs.reshape(rows, 1),
        seg_row.reshape(1, keys),
        out_weight,
        base,
    )


def ffn_kernel(x_ref, gain_ref, gate_ref, up_ref, down_ref, out_ref):
    normed = (rms_rows(x_ref[...].astype(jnp.float32)) * gain_ref[...]).astype(jnp.bfloat16)
    contract = (((1,), (1,)), ((), ()))
    gate_proj = lax.dot_general(normed, gate_ref[...], contract, preferred_element_type=jnp.float32)
    up_proj = lax.dot_general(normed, up_ref[...], contract, preferred_element_type=jnp.float32)
    hidden = (gate_proj / (1.0 + jnp.exp(-gate_proj)) * up_proj).astype(jnp.bfloat16)
    out_ref[...] = jnp.dot(hidden, down_ref[...], preferred_element_type=jnp.float32).astype(
        out_ref.dtype
    )


def ffn_partial(rows, gain, gate_weight, up_weight, down_weight, tile):
    count, width = rows.shape
    hidden_w = gate_weight.shape[1]
    full = lambda i: (0, 0)
    gate_t = gate_weight.T
    up_t = up_weight.T
    return pl.pallas_call(
        ffn_kernel,
        out_shape=jax.ShapeDtypeStruct((count, width), jnp.bfloat16),
        grid=(count // tile,),
        in_specs=[
            pl.BlockSpec((tile, width), lambda i: (i, 0)),
            pl.BlockSpec((1, width), full),
            pl.BlockSpec((hidden_w, width), full),
            pl.BlockSpec((hidden_w, width), full),
            pl.BlockSpec((hidden_w, width), full),
        ],
        out_specs=pl.BlockSpec((tile, width), lambda i: (i, 0)),
        compiler_params=pltpu.CompilerParams(
            dimension_semantics=("arbitrary",), vmem_limit_bytes=48 * 1024 * 1024
        ),
        cost_estimate=pl.CostEstimate(
            flops=6 * count * width * hidden_w,
            bytes_accessed=3 * width * hidden_w * 2 + 2 * count * width * 2,
            transcendentals=count * hidden_w,
        ),
    )(rows, gain.reshape(1, width), gate_t, up_t, down_weight)


def project_kernel(x_ref, w_ref, out_ref):
    out_ref[...] = jnp.dot(x_ref[...], w_ref[...], preferred_element_type=jnp.float32).astype(
        out_ref.dtype
    )


def project_rows(rows, weight, tile):
    count, width = rows.shape
    cols = weight.shape[1]
    return pl.pallas_call(
        project_kernel,
        out_shape=jax.ShapeDtypeStruct((count, cols), jnp.bfloat16),
        grid=(count // tile,),
        in_specs=[
            pl.BlockSpec((tile, width), lambda i: (i, 0)),
            pl.BlockSpec((width, cols), lambda i: (0, 0)),
        ],
        out_specs=pl.BlockSpec((tile, cols), lambda i: (i, 0)),
        compiler_params=pltpu.CompilerParams(
            dimension_semantics=("arbitrary",), vmem_limit_bytes=48 * 1024 * 1024
        ),
        cost_estimate=pl.CostEstimate(
            flops=2 * count * width * cols,
            bytes_accessed=2 * (count * width + width * cols + count * cols),
            transcendentals=0,
        ),
    )(rows, weight)


def output_kernel(mid_ref, ffn_ref, gain_ref, out_ref, normed_ref):
    layer_output = (mid_ref[...].astype(jnp.float32) + ffn_ref[...].astype(jnp.float32)).astype(
        out_ref.dtype
    )
    out_ref[...] = layer_output
    normed_ref[...] = (rms_rows(layer_output.astype(jnp.float32)) * gain_ref[...]).astype(
        normed_ref.dtype
    )


def finish_rows(residual_mid, ffn_own, gain):
    rows, width = residual_mid.shape
    vmem = pl.BlockSpec(memory_space=pltpu.VMEM)
    shape = jax.ShapeDtypeStruct((rows, width), jnp.bfloat16)
    return pl.pallas_call(
        output_kernel,
        out_shape=(shape, shape),
        in_specs=[vmem, vmem, vmem],
        out_specs=(vmem, vmem),
        cost_estimate=pl.CostEstimate(
            flops=6 * rows * width, bytes_accessed=8 * rows * width, transcendentals=rows
        ),
    )(residual_mid, ffn_own, gain.reshape(1, width))


def body(
    layer_input,
    q_in,
    k_in,
    v_in,
    segment_ids,
    lambda_parts,
    out_weight,
    ffn_gain,
    gate_weight,
    up_weight,
    down_weight,
    next_gain,
    qkv_weight,
    page_owner,
    page_slot,
):
    row_count = q_in.shape[0]
    feat_width = q_in.shape[1]
    head_dim = feat_width // (2 * HEADS)
    peer_count = lax.axis_size("tok")
    tok_place = lax.axis_index("tok")
    seg_row = segment_ids[0]
    first_row = tok_place * row_count
    query_places = first_row + jnp.arange(row_count)
    query_segs = lax.dynamic_slice_in_dim(seg_row, first_row, row_count)
    lambda_mix = lambda_value(lambda_parts)
    score_scale = 1.0 / math.sqrt(head_dim)
    query_split = q_in.reshape(row_count, HEADS, 2, head_dim)
    run_max = jnp.full((HEADS, 2, row_count), NEG_FILL, jnp.float32)
    back = -(-(MAX_SEG - 1) // row_count)
    own_kv = jnp.concatenate([k_in, v_in], axis=1)
    all_kv = lax.all_gather(own_kv, "tok", axis=0, tiled=True)
    residual_mid = window_attention(
        q_in, all_kv, query_segs, seg_row, first_row, lambda_mix, back, out_weight, layer_input
    )
    gathered = lax.all_gather(residual_mid, "req", axis=0, tiled=True)
    partial = ffn_partial(gathered, ffn_gain, gate_weight, up_weight, down_weight, 256)
    ffn_own = lax.psum_scatter(partial, "req", scatter_dimension=0, tiled=True)
    layer_output, next_normed = finish_rows(residual_mid, ffn_own, next_gain)
    projected_cols = project_rows(
        lax.all_gather(next_normed, "req", axis=0, tiled=True), qkv_weight, 256
    )
    n_req = lax.axis_size("req")
    col_w = projected_cols.shape[1]
    arrived = lax.all_to_all(
        projected_cols.reshape(n_req, row_count, col_w), "req", 0, 0, tiled=True
    )
    projected = jnp.transpose(arrived, (1, 0, 2)).reshape(row_count, n_req * col_w)
    q_next = projected[:, :feat_width]
    pages_dev = row_count // PAGE
    assert pages_dev == peer_count
    key_values = projected[:, feat_width:].reshape(pages_dev, PAGE, 2 * feat_width)
    owner_all = page_owner[0].reshape(peer_count, pages_dev)
    slot_all = page_slot[0].reshape(peer_count, pages_dev)
    numbers = jnp.arange(pages_dev, dtype=jnp.int32)
    my_owners = lax.dynamic_index_in_dim(owner_all, tok_place, 0, keepdims=False)
    send_order = jnp.sum(
        jnp.where(my_owners[None, :] == numbers[:, None], numbers[None, :], 0), axis=1
    )
    outgoing = key_values[send_order].reshape(peer_count, 1, PAGE, 2 * feat_width)
    incoming = lax.all_to_all(outgoing, "tok", split_axis=0, concat_axis=0, tiled=True)
    incoming = incoming.reshape(pages_dev, PAGE, 2 * feat_width)
    slot_list = jnp.sum(jnp.where(owner_all == tok_place, slot_all, 0), axis=1)
    source_of_slot = jnp.sum(
        jnp.where(slot_list[None, :] == numbers[:, None], numbers[None, :], 0), axis=1
    )
    page_cache = incoming[source_of_slot]
    return (layer_output, q_next, page_cache)


def solution(mesh):
    in_specs = (
        P(("req", "tok"), None),
        P(("req", "tok"), None),
        P(("req", "tok"), None),
        P(("req", "tok"), None),
        P("req", None),
        P(),
        P(),
        P(),
        P(None, "req"),
        P(None, "req"),
        P("req", None),
        P(),
        P(None, "req"),
        P("req", None),
        P("req", None),
    )
    out_specs = (P(("req", "tok"), None), P(("req", "tok"), None), P(("req", "tok"), None, None))
    return jax.shard_map(body, mesh=mesh, in_specs=in_specs, out_specs=out_specs, check_vma=False)
```

```python
import functools
import math

import jax
import jax.numpy as jnp
from jax import lax
from jax.experimental import pallas as pl
from jax.experimental.pallas import tpu as pltpu
from jax.sharding import PartitionSpec as P

HEADS = 8
PAGE = 8


NEG_FILL = -1e30
LAMBDA_INIT = 0.2
EPSILON = 1e-05
MAX_SEG = 1024


def rms_rows(values):
    return values * lax.rsqrt(jnp.mean(values * values, axis=-1, keepdims=True) + EPSILON)


def lambda_value(lambda_parts):
    first_term = jnp.exp(jnp.sum(lambda_parts[0] * lambda_parts[1]))
    second_term = jnp.exp(jnp.sum(lambda_parts[2] * lambda_parts[3]))
    return first_term - second_term + LAMBDA_INIT


def attention_kernel(
    back, head_dim, scalars_ref, lam_ref, q_ref, k_ref, v_ref, qseg_ref, kseg_ref, w_ref, base_ref, out_ref, total_ref
):
    rows = q_ref.shape[0]
    span = (back + 1) * rows
    start = pl.multiple_of(scalars_ref[0], rows)
    query_places = scalars_ref[1] + lax.broadcasted_iota(jnp.int32, (rows, span), 0)
    key_places = start + lax.broadcasted_iota(jnp.int32, (rows, span), 1)
    key_segs = kseg_ref[:, pl.ds(start, span)]
    visible = (key_segs == qseg_ref[...]) & (key_places <= query_places)
    values = v_ref[pl.ds(start, span), :]
    score_scale = 1.0 / math.sqrt(head_dim)
    map_outputs = []
    for map_index in range(2):
        query_map = q_ref[:, map_index * head_dim:(map_index + 1) * head_dim]
        key_map = k_ref[pl.ds(start, span), map_index * head_dim:(map_index + 1) * head_dim]
        scores = (
            lax.dot_general(
                query_map, key_map, (((1,), (1,)), ((), ())), preferred_element_type=jnp.float32
            )
            * score_scale
        )
        scores = jnp.where(visible, scores, NEG_FILL)
        row_max = jnp.max(scores, axis=1, keepdims=True)
        weights = jnp.where(visible, jnp.exp(scores - row_max), 0.0)
        totals = jnp.sum(weights, axis=1, keepdims=True)
        map_out = (
            jnp.dot(weights.astype(jnp.bfloat16), values, preferred_element_type=jnp.float32) / totals
        )
        map_outputs.append(map_out)
    difference = map_outputs[0] - lam_ref[0] * map_outputs[1]
    head_out = (rms_rows(difference) * (1.0 - LAMBDA_INIT)).astype(jnp.bfloat16)
    step = pl.program_id(0)

    @pl.when(step == 0)
    def _():
        total_ref[...] = jnp.zeros_like(total_ref)

    total_ref[...] += jnp.dot(head_out, w_ref[...], preferred_element_type=jnp.float32)

    @pl.when(step == pl.num_programs(0) - 1)
    def _():
        out_ref[...] = (base_ref[...].astype(jnp.float32) + total_ref[...]).astype(out_ref.dtype)


def window_attention(q_in, all_kv, query_segs, seg_row, first_row, lambda_mix, back, out_weight, base):
    rows, width = q_in.shape
    keys = all_kv.shape[0]
    head_w = width // HEADS
    start = jnp.maximum(first_row - back * rows, 0)
    scalars = jnp.stack([start, first_row]).astype(jnp.int32)
    lam = jnp.reshape(lambda_mix, (1,)).astype(jnp.float32)
    span = (back + 1) * rows
    flops = HEADS * 2 * (2 * rows * span * (head_w // 2) + 2 * rows * span * head_w) + 2 * rows * width * width
    smem = pl.BlockSpec(memory_space=pltpu.SMEM)
    return pl.pallas_call(
        functools.partial(attention_kernel, back, head_w // 2),
        out_shape=jax.ShapeDtypeStruct((rows, width), jnp.bfloat16),
        grid=(HEADS,),
        in_specs=[
            smem,
            smem,
            pl.BlockSpec((rows, head_w), lambda h: (0, h)),
            pl.BlockSpec((keys, head_w), lambda h: (0, h)),
            pl.BlockSpec((keys, head_w), lambda h: (0, HEADS + h)),
            pl.BlockSpec((rows, 1), lambda h: (0, 0)),
            pl.BlockSpec((1, keys), lambda h: (0, 0)),
            pl.BlockSpec((head_w, width), lambda h: (h, 0)),
            pl.BlockSpec((rows, width), lambda h: (0, 0)),
        ],
        out_specs=pl.BlockSpec((rows, width), lambda h: (0, 0)),
        scratch_shapes=[pltpu.VMEM((rows, width), jnp.float32)],
        compiler_params=pltpu.CompilerParams(dimension_semantics=("arbitrary",)),
        cost_estimate=pl.CostEstimate(
            flops=flops,
            bytes_accessed=2 * keys * width * 2 + 3 * rows * width * 2 + width * width * 2,
            transcendentals=HEADS * 2 * rows * span,
        ),
    )(
        scalars,
        lam,
        q_in,
        all_kv,
        all_kv,
        query_segs.reshape(rows, 1),
        seg_row.reshape(1, keys),
        out_weight,
        base,
    )


def ffn_kernel(x_ref, gain_ref, gate_ref, up_ref, down_ref, out_ref):
    normed = (rms_rows(x_ref[...].astype(jnp.float32)) * gain_ref[...]).astype(jnp.bfloat16)
    contract = (((1,), (1,)), ((), ()))
    gate_proj = lax.dot_general(normed, gate_ref[...], contract, preferred_element_type=jnp.float32)
    up_proj = lax.dot_general(normed, up_ref[...], contract, preferred_element_type=jnp.float32)
    hidden = (gate_proj / (1.0 + jnp.exp(-gate_proj)) * up_proj).astype(jnp.bfloat16)
    out_ref[...] = jnp.dot(hidden, down_ref[...], preferred_element_type=jnp.float32).astype(
        out_ref.dtype
    )


def ffn_partial(rows, gain, gate_weight, up_weight, down_weight, tile):
    count, width = rows.shape
    hidden_w = gate_weight.shape[1]
    full = lambda i: (0, 0)
    gate_t = gate_weight.T
    up_t = up_weight.T
    return pl.pallas_call(
        ffn_kernel,
        out_shape=jax.ShapeDtypeStruct((count, width), jnp.bfloat16),
        grid=(count // tile,),
        in_specs=[
            pl.BlockSpec((tile, width), lambda i: (i, 0)),
            pl.BlockSpec((1, width), full),
            pl.BlockSpec((hidden_w, width), full),
            pl.BlockSpec((hidden_w, width), full),
            pl.BlockSpec((hidden_w, width), full),
        ],
        out_specs=pl.BlockSpec((tile, width), lambda i: (i, 0)),
        compiler_params=pltpu.CompilerParams(
            dimension_semantics=("arbitrary",), vmem_limit_bytes=48 * 1024 * 1024
        ),
        cost_estimate=pl.CostEstimate(
            flops=6 * count * width * hidden_w,
            bytes_accessed=3 * width * hidden_w * 2 + 2 * count * width * 2,
            transcendentals=count * hidden_w,
        ),
    )(rows, gain.reshape(1, width), gate_t, up_t, down_weight)


def project_kernel(x_ref, w_ref, out_ref):
    out_ref[...] = jnp.dot(x_ref[...], w_ref[...], preferred_element_type=jnp.float32).astype(
        out_ref.dtype
    )


def project_rows(rows, weight, tile):
    count, width = rows.shape
    cols = weight.shape[1]
    return pl.pallas_call(
        project_kernel,
        out_shape=jax.ShapeDtypeStruct((count, cols), jnp.bfloat16),
        grid=(count // tile,),
        in_specs=[
            pl.BlockSpec((tile, width), lambda i: (i, 0)),
            pl.BlockSpec((width, cols), lambda i: (0, 0)),
        ],
        out_specs=pl.BlockSpec((tile, cols), lambda i: (i, 0)),
        compiler_params=pltpu.CompilerParams(
            dimension_semantics=("arbitrary",), vmem_limit_bytes=48 * 1024 * 1024
        ),
        cost_estimate=pl.CostEstimate(
            flops=2 * count * width * cols,
            bytes_accessed=2 * (count * width + width * cols + count * cols),
            transcendentals=0,
        ),
    )(rows, weight)


def output_kernel(mid_ref, ffn_ref, gain_ref, out_ref, normed_ref):
    layer_output = (mid_ref[...].astype(jnp.float32) + ffn_ref[...].astype(jnp.float32)).astype(
        out_ref.dtype
    )
    out_ref[...] = layer_output
    normed_ref[...] = (rms_rows(layer_output.astype(jnp.float32)) * gain_ref[...]).astype(
        normed_ref.dtype
    )


def finish_rows(residual_mid, ffn_own, gain):
    rows, width = residual_mid.shape
    vmem = pl.BlockSpec(memory_space=pltpu.VMEM)
    shape = jax.ShapeDtypeStruct((rows, width), jnp.bfloat16)
    return pl.pallas_call(
        output_kernel,
        out_shape=(shape, shape),
        in_specs=[vmem, vmem, vmem],
        out_specs=(vmem, vmem),
        cost_estimate=pl.CostEstimate(
            flops=6 * rows * width, bytes_accessed=8 * rows * width, transcendentals=rows
        ),
    )(residual_mid, ffn_own, gain.reshape(1, width))


def join_kernel(k_ref, v_ref, out_ref):
    width = k_ref.shape[1]
    out_ref[:, :width] = k_ref[...]
    out_ref[:, width:] = v_ref[...]


def join_columns(k_in, v_in):
    rows, width = k_in.shape
    vmem = pl.BlockSpec(memory_space=pltpu.VMEM)
    return pl.pallas_call(
        join_kernel,
        out_shape=jax.ShapeDtypeStruct((rows, 2 * width), k_in.dtype),
        in_specs=[vmem, vmem],
        out_specs=vmem,
        cost_estimate=pl.CostEstimate(flops=0, bytes_accessed=8 * rows * width, transcendentals=0),
    )(k_in, v_in)


def body(
    layer_input,
    q_in,
    k_in,
    v_in,
    segment_ids,
    lambda_parts,
    out_weight,
    ffn_gain,
    gate_weight,
    up_weight,
    down_weight,
    next_gain,
    qkv_weight,
    page_owner,
    page_slot,
):
    row_count = q_in.shape[0]
    feat_width = q_in.shape[1]
    head_dim = feat_width // (2 * HEADS)
    peer_count = lax.axis_size("tok")
    tok_place = lax.axis_index("tok")
    seg_row = segment_ids[0]
    first_row = tok_place * row_count
    query_places = first_row + jnp.arange(row_count)
    query_segs = lax.dynamic_slice_in_dim(seg_row, first_row, row_count)
    lambda_mix = lambda_value(lambda_parts)
    score_scale = 1.0 / math.sqrt(head_dim)
    query_split = q_in.reshape(row_count, HEADS, 2, head_dim)
    run_max = jnp.full((HEADS, 2, row_count), NEG_FILL, jnp.float32)
    back = -(-(MAX_SEG - 1) // row_count)
    own_kv = join_columns(k_in, v_in)
    all_kv = lax.all_gather(own_kv, "tok", axis=0, tiled=True)
    residual_mid = window_attention(
        q_in, all_kv, query_segs, seg_row, first_row, lambda_mix, back, out_weight, layer_input
    )
    gathered = lax.all_gather(residual_mid, "req", axis=0, tiled=True)
    partial = ffn_partial(gathered, ffn_gain, gate_weight, up_weight, down_weight, 256)
    ffn_own = lax.psum_scatter(partial, "req", scatter_dimension=0, tiled=True)
    layer_output, next_normed = finish_rows(residual_mid, ffn_own, next_gain)
    projected_cols = project_rows(
        lax.all_gather(next_normed, "req", axis=0, tiled=True), qkv_weight, 256
    )
    n_req = lax.axis_size("req")
    col_w = projected_cols.shape[1]
    arrived = lax.all_to_all(
        projected_cols.reshape(n_req, row_count, col_w), "req", 0, 0, tiled=True
    )
    projected = jnp.transpose(arrived, (1, 0, 2)).reshape(row_count, n_req * col_w)
    q_next = projected[:, :feat_width]
    pages_dev = row_count // PAGE
    assert pages_dev == peer_count
    key_values = projected[:, feat_width:].reshape(pages_dev, PAGE, 2 * feat_width)
    owner_all = page_owner[0].reshape(peer_count, pages_dev)
    slot_all = page_slot[0].reshape(peer_count, pages_dev)
    numbers = jnp.arange(pages_dev, dtype=jnp.int32)
    my_owners = lax.dynamic_index_in_dim(owner_all, tok_place, 0, keepdims=False)
    send_order = jnp.sum(
        jnp.where(my_owners[None, :] == numbers[:, None], numbers[None, :], 0), axis=1
    )
    outgoing = key_values[send_order].reshape(peer_count, 1, PAGE, 2 * feat_width)
    incoming = lax.all_to_all(outgoing, "tok", split_axis=0, concat_axis=0, tiled=True)
    incoming = incoming.reshape(pages_dev, PAGE, 2 * feat_width)
    slot_list = jnp.sum(jnp.where(owner_all == tok_place, slot_all, 0), axis=1)
    source_of_slot = jnp.sum(
        jnp.where(slot_list[None, :] == numbers[:, None], numbers[None, :], 0), axis=1
    )
    page_cache = incoming[source_of_slot]
    return (layer_output, q_next, page_cache)


def solution(mesh):
    in_specs = (
        P(("req", "tok"), None),
        P(("req", "tok"), None),
        P(("req", "tok"), None),
        P(("req", "tok"), None),
        P("req", None),
        P(),
        P(),
        P(),
        P(None, "req"),
        P(None, "req"),
        P("req", None),
        P(),
        P(None, "req"),
        P("req", None),
        P("req", None),
    )
    out_specs = (P(("req", "tok"), None), P(("req", "tok"), None), P(("req", "tok"), None, None))
    return jax.shard_map(body, mesh=mesh, in_specs=in_specs, out_specs=out_specs, check_vma=False)
```

```python
import functools
import math

import jax
import jax.numpy as jnp
from jax import lax
from jax.experimental import pallas as pl
from jax.experimental.pallas import tpu as pltpu
from jax.sharding import PartitionSpec as P

HEADS = 8
PAGE = 8


NEG_FILL = -1e30
LAMBDA_INIT = 0.2
EPSILON = 1e-05
MAX_SEG = 1024


def rms_rows(values):
    return values * lax.rsqrt(jnp.mean(values * values, axis=-1, keepdims=True) + EPSILON)


def lambda_value(lambda_parts):
    first_term = jnp.exp(jnp.sum(lambda_parts[0] * lambda_parts[1]))
    second_term = jnp.exp(jnp.sum(lambda_parts[2] * lambda_parts[3]))
    return first_term - second_term + LAMBDA_INIT


def attention_kernel(
    back, head_dim, scalars_ref, lam_ref, q_ref, k_ref, v_ref, qseg_ref, kseg_ref, w_ref, base_ref, out_ref, total_ref
):
    rows = q_ref.shape[0]
    span = (back + 1) * rows
    start = pl.multiple_of(scalars_ref[0], rows)
    query_places = scalars_ref[1] + lax.broadcasted_iota(jnp.int32, (rows, span), 0)
    key_places = start + lax.broadcasted_iota(jnp.int32, (rows, span), 1)
    key_segs = kseg_ref[:, pl.ds(start, span)]
    visible = (key_segs == qseg_ref[...]) & (key_places <= query_places)
    score_scale = 1.0 / math.sqrt(head_dim)
    head_w = 2 * head_dim
    head_outs = []
    for head in range(q_ref.shape[1] // head_w):
        values = v_ref[pl.ds(start, span), head * head_w:(head + 1) * head_w]
        map_outputs = []
        for map_index in range(2):
            first = head * head_w + map_index * head_dim
            query_map = q_ref[:, first:first + head_dim]
            key_map = k_ref[pl.ds(start, span), first:first + head_dim]
            scores = (
                lax.dot_general(
                    query_map, key_map, (((1,), (1,)), ((), ())), preferred_element_type=jnp.float32
                )
                * score_scale
            )
            scores = jnp.where(visible, scores, NEG_FILL)
            row_max = jnp.max(scores, axis=1, keepdims=True)
            weights = jnp.exp(scores - row_max)
            totals = jnp.sum(weights, axis=1, keepdims=True)
            map_out = (
                jnp.dot(weights.astype(jnp.bfloat16), values, preferred_element_type=jnp.float32)
                / totals
            )
            map_outputs.append(map_out)
        difference = map_outputs[0] - lam_ref[0] * map_outputs[1]
        head_outs.append((rms_rows(difference) * (1.0 - LAMBDA_INIT)).astype(jnp.bfloat16))
    head_out = jnp.concatenate(head_outs, axis=1)
    step = pl.program_id(0)

    @pl.when(step == 0)
    def _():
        total_ref[...] = jnp.zeros_like(total_ref)

    total_ref[...] += jnp.dot(head_out, w_ref[...], preferred_element_type=jnp.float32)

    @pl.when(step == pl.num_programs(0) - 1)
    def _():
        out_ref[...] = (base_ref[...].astype(jnp.float32) + total_ref[...]).astype(out_ref.dtype)


def window_attention(q_in, all_kv, query_segs, seg_row, first_row, lambda_mix, back, out_weight, base):
    rows, width = q_in.shape
    keys = all_kv.shape[0]
    head_w = width // HEADS
    start = jnp.maximum(first_row - back * rows, 0)
    scalars = jnp.stack([start, first_row]).astype(jnp.int32)
    lam = jnp.reshape(lambda_mix, (1,)).astype(jnp.float32)
    span = (back + 1) * rows
    flops = HEADS * 2 * (2 * rows * span * (head_w // 2) + 2 * rows * span * head_w) + 2 * rows * width * width
    smem = pl.BlockSpec(memory_space=pltpu.SMEM)
    steps = HEADS // 2
    step_w = width // steps
    return pl.pallas_call(
        functools.partial(attention_kernel, back, head_w // 2),
        out_shape=jax.ShapeDtypeStruct((rows, width), jnp.bfloat16),
        grid=(steps,),
        in_specs=[
            smem,
            smem,
            pl.BlockSpec((rows, step_w), lambda h: (0, h)),
            pl.BlockSpec((keys, step_w), lambda h: (0, h)),
            pl.BlockSpec((keys, step_w), lambda h: (0, steps + h)),
            pl.BlockSpec((rows, 1), lambda h: (0, 0)),
            pl.BlockSpec((1, keys), lambda h: (0, 0)),
            pl.BlockSpec((step_w, width), lambda h: (h, 0)),
            pl.BlockSpec((rows, width), lambda h: (0, 0)),
        ],
        out_specs=pl.BlockSpec((rows, width), lambda h: (0, 0)),
        scratch_shapes=[pltpu.VMEM((rows, width), jnp.float32)],
        compiler_params=pltpu.CompilerParams(dimension_semantics=("arbitrary",)),
        cost_estimate=pl.CostEstimate(
            flops=flops,
            bytes_accessed=2 * keys * width * 2 + 3 * rows * width * 2 + width * width * 2,
            transcendentals=HEADS * 2 * rows * span,
        ),
    )(
        scalars,
        lam,
        q_in,
        all_kv,
        all_kv,
        query_segs.reshape(rows, 1),
        seg_row.reshape(1, keys),
        out_weight,
        base,
    )


def ffn_kernel(x_ref, gain_ref, gate_ref, up_ref, down_ref, out_ref):
    normed = (rms_rows(x_ref[...].astype(jnp.float32)) * gain_ref[...]).astype(jnp.bfloat16)
    contract = (((1,), (1,)), ((), ()))
    gate_proj = lax.dot_general(normed, gate_ref[...], contract, preferred_element_type=jnp.float32)
    up_proj = lax.dot_general(normed, up_ref[...], contract, preferred_element_type=jnp.float32)
    hidden = (gate_proj / (1.0 + jnp.exp(-gate_proj)) * up_proj).astype(jnp.bfloat16)
    out_ref[...] = jnp.dot(hidden, down_ref[...], preferred_element_type=jnp.float32).astype(
        out_ref.dtype
    )


def ffn_partial(rows, gain, gate_weight, up_weight, down_weight, tile):
    count, width = rows.shape
    hidden_w = gate_weight.shape[1]
    full = lambda i: (0, 0)
    gate_t = gate_weight.T
    up_t = up_weight.T
    return pl.pallas_call(
        ffn_kernel,
        out_shape=jax.ShapeDtypeStruct((count, width), jnp.bfloat16),
        grid=(count // tile,),
        in_specs=[
            pl.BlockSpec((tile, width), lambda i: (i, 0)),
            pl.BlockSpec((1, width), full),
            pl.BlockSpec((hidden_w, width), full),
            pl.BlockSpec((hidden_w, width), full),
            pl.BlockSpec((hidden_w, width), full),
        ],
        out_specs=pl.BlockSpec((tile, width), lambda i: (i, 0)),
        compiler_params=pltpu.CompilerParams(
            dimension_semantics=("arbitrary",), vmem_limit_bytes=48 * 1024 * 1024
        ),
        cost_estimate=pl.CostEstimate(
            flops=6 * count * width * hidden_w,
            bytes_accessed=3 * width * hidden_w * 2 + 2 * count * width * 2,
            transcendentals=count * hidden_w,
        ),
    )(rows, gain.reshape(1, width), gate_t, up_t, down_weight)


def project_kernel(x_ref, w_ref, out_ref):
    out_ref[...] = jnp.dot(x_ref[...], w_ref[...], preferred_element_type=jnp.float32).astype(
        out_ref.dtype
    )


def project_rows(rows, weight, tile):
    count, width = rows.shape
    cols = weight.shape[1]
    return pl.pallas_call(
        project_kernel,
        out_shape=jax.ShapeDtypeStruct((count, cols), jnp.bfloat16),
        grid=(count // tile,),
        in_specs=[
            pl.BlockSpec((tile, width), lambda i: (i, 0)),
            pl.BlockSpec((width, cols), lambda i: (0, 0)),
        ],
        out_specs=pl.BlockSpec((tile, cols), lambda i: (i, 0)),
        compiler_params=pltpu.CompilerParams(
            dimension_semantics=("arbitrary",), vmem_limit_bytes=48 * 1024 * 1024
        ),
        cost_estimate=pl.CostEstimate(
            flops=2 * count * width * cols,
            bytes_accessed=2 * (count * width + width * cols + count * cols),
            transcendentals=0,
        ),
    )(rows, weight)


def output_kernel(mid_ref, ffn_ref, gain_ref, out_ref, normed_ref):
    layer_output = (mid_ref[...].astype(jnp.float32) + ffn_ref[...].astype(jnp.float32)).astype(
        out_ref.dtype
    )
    out_ref[...] = layer_output
    normed_ref[...] = (rms_rows(layer_output.astype(jnp.float32)) * gain_ref[...]).astype(
        normed_ref.dtype
    )


def finish_rows(residual_mid, ffn_own, gain):
    rows, width = residual_mid.shape
    vmem = pl.BlockSpec(memory_space=pltpu.VMEM)
    shape = jax.ShapeDtypeStruct((rows, width), jnp.bfloat16)
    return pl.pallas_call(
        output_kernel,
        out_shape=(shape, shape),
        in_specs=[vmem, vmem, vmem],
        out_specs=(vmem, vmem),
        cost_estimate=pl.CostEstimate(
            flops=6 * rows * width, bytes_accessed=8 * rows * width, transcendentals=rows
        ),
    )(residual_mid, ffn_own, gain.reshape(1, width))


def body(
    layer_input,
    q_in,
    k_in,
    v_in,
    segment_ids,
    lambda_parts,
    out_weight,
    ffn_gain,
    gate_weight,
    up_weight,
    down_weight,
    next_gain,
    qkv_weight,
    page_owner,
    page_slot,
):
    row_count = q_in.shape[0]
    feat_width = q_in.shape[1]
    head_dim = feat_width // (2 * HEADS)
    peer_count = lax.axis_size("tok")
    tok_place = lax.axis_index("tok")
    seg_row = segment_ids[0]
    first_row = tok_place * row_count
    query_places = first_row + jnp.arange(row_count)
    query_segs = lax.dynamic_slice_in_dim(seg_row, first_row, row_count)
    lambda_mix = lambda_value(lambda_parts)
    score_scale = 1.0 / math.sqrt(head_dim)
    query_split = q_in.reshape(row_count, HEADS, 2, head_dim)
    run_max = jnp.full((HEADS, 2, row_count), NEG_FILL, jnp.float32)
    back = -(-(MAX_SEG - 1) // row_count)
    own_kv = jnp.concatenate([k_in, v_in], axis=1)
    all_kv = lax.all_gather(own_kv, "tok", axis=0, tiled=True)
    residual_mid = window_attention(
        q_in, all_kv, query_segs, seg_row, first_row, lambda_mix, back, out_weight, layer_input
    )
    gathered = lax.all_gather(residual_mid, "req", axis=0, tiled=True)
    partial = ffn_partial(gathered, ffn_gain, gate_weight, up_weight, down_weight, 256)
    ffn_own = lax.psum_scatter(partial, "req", scatter_dimension=0, tiled=True)
    layer_output, next_normed = finish_rows(residual_mid, ffn_own, next_gain)
    projected_cols = project_rows(
        lax.all_gather(next_normed, "req", axis=0, tiled=True), qkv_weight, 256
    )
    n_req = lax.axis_size("req")
    col_w = projected_cols.shape[1]
    arrived = lax.all_to_all(
        projected_cols.reshape(n_req, row_count, col_w), "req", 0, 0, tiled=True
    )
    projected = jnp.transpose(arrived, (1, 0, 2)).reshape(row_count, n_req * col_w)
    q_next = projected[:, :feat_width]
    pages_dev = row_count // PAGE
    assert pages_dev == peer_count
    key_values = projected[:, feat_width:].reshape(pages_dev, PAGE, 2 * feat_width)
    owner_all = page_owner[0].reshape(peer_count, pages_dev)
    slot_all = page_slot[0].reshape(peer_count, pages_dev)
    numbers = jnp.arange(pages_dev, dtype=jnp.int32)
    my_owners = lax.dynamic_index_in_dim(owner_all, tok_place, 0, keepdims=False)
    send_order = jnp.sum(
        jnp.where(my_owners[None, :] == numbers[:, None], numbers[None, :], 0), axis=1
    )
    outgoing = key_values[send_order].reshape(peer_count, 1, PAGE, 2 * feat_width)
    incoming = lax.all_to_all(outgoing, "tok", split_axis=0, concat_axis=0, tiled=True)
    incoming = incoming.reshape(pages_dev, PAGE, 2 * feat_width)
    slot_list = jnp.sum(jnp.where(owner_all == tok_place, slot_all, 0), axis=1)
    source_of_slot = jnp.sum(
        jnp.where(slot_list[None, :] == numbers[:, None], numbers[None, :], 0), axis=1
    )
    page_cache = incoming[source_of_slot]
    return (layer_output, q_next, page_cache)


def solution(mesh):
    in_specs = (
        P(("req", "tok"), None),
        P(("req", "tok"), None),
        P(("req", "tok"), None),
        P(("req", "tok"), None),
        P("req", None),
        P(),
        P(),
        P(),
        P(None, "req"),
        P(None, "req"),
        P("req", None),
        P(),
        P(None, "req"),
        P("req", None),
        P("req", None),
    )
    out_specs = (P(("req", "tok"), None), P(("req", "tok"), None), P(("req", "tok"), None, None))
    return jax.shard_map(body, mesh=mesh, in_specs=in_specs, out_specs=out_specs, check_vma=False)
```

```python
import functools
import math

import jax
import jax.numpy as jnp
from jax import lax
from jax.experimental import pallas as pl
from jax.experimental.pallas import tpu as pltpu
from jax.sharding import PartitionSpec as P

HEADS = 8
PAGE = 8


NEG_FILL = -1e30
LAMBDA_INIT = 0.2
EPSILON = 1e-05
MAX_SEG = 1024


def rms_rows(values):
    return values * lax.rsqrt(jnp.mean(values * values, axis=-1, keepdims=True) + EPSILON)


def lambda_value(lambda_parts):
    first_term = jnp.exp(jnp.sum(lambda_parts[0] * lambda_parts[1]))
    second_term = jnp.exp(jnp.sum(lambda_parts[2] * lambda_parts[3]))
    return first_term - second_term + LAMBDA_INIT


def attention_kernel(
    back, head_dim, scalars_ref, lam_ref, q_ref, k_ref, v_ref, qseg_ref, kseg_ref, w_ref, base_ref, out_ref, total_ref
):
    rows = q_ref.shape[0]
    span = (back + 1) * rows
    start = pl.multiple_of(scalars_ref[0], rows)
    query_places = scalars_ref[1] + lax.broadcasted_iota(jnp.int32, (rows, span), 0)
    key_places = start + lax.broadcasted_iota(jnp.int32, (rows, span), 1)
    key_segs = kseg_ref[:, pl.ds(start, span)]
    visible = (key_segs == qseg_ref[...]) & (key_places <= query_places)
    score_scale = 1.0 / math.sqrt(head_dim)
    head_w = 2 * head_dim
    head_outs = []
    for head in range(q_ref.shape[1] // head_w):
        values = v_ref[pl.ds(start, span), head * head_w:(head + 1) * head_w]
        map_outputs = []
        for map_index in range(2):
            first = head * head_w + map_index * head_dim
            query_map = q_ref[:, first:first + head_dim]
            key_map = k_ref[pl.ds(start, span), first:first + head_dim]
            scores = (
                lax.dot_general(
                    query_map, key_map, (((1,), (1,)), ((), ())), preferred_element_type=jnp.float32
                )
                * score_scale
            )
            scores = jnp.where(visible, scores, NEG_FILL)
            row_max = jnp.max(scores, axis=1, keepdims=True)
            weights = jnp.exp(scores - row_max)
            totals = jnp.sum(weights, axis=1, keepdims=True)
            map_out = (
                jnp.dot(weights.astype(jnp.bfloat16), values, preferred_element_type=jnp.float32)
                / totals
            )
            map_outputs.append(map_out)
        difference = map_outputs[0] - lam_ref[0] * map_outputs[1]
        head_outs.append((rms_rows(difference) * (1.0 - LAMBDA_INIT)).astype(jnp.bfloat16))
    head_out = jnp.concatenate(head_outs, axis=1)
    step = pl.program_id(0)

    @pl.when(step == 0)
    def _():
        total_ref[...] = jnp.zeros_like(total_ref)

    total_ref[...] += jnp.dot(head_out, w_ref[...], preferred_element_type=jnp.float32)

    @pl.when(step == pl.num_programs(0) - 1)
    def _():
        out_ref[...] = (base_ref[...].astype(jnp.float32) + total_ref[...]).astype(out_ref.dtype)


def window_attention(q_in, all_kv, query_segs, seg_row, first_row, lambda_mix, back, out_weight, base):
    rows, width = q_in.shape
    keys = all_kv.shape[0]
    head_w = width // HEADS
    start = jnp.maximum(first_row - back * rows, 0)
    scalars = jnp.stack([start, first_row]).astype(jnp.int32)
    lam = jnp.reshape(lambda_mix, (1,)).astype(jnp.float32)
    span = (back + 1) * rows
    flops = HEADS * 2 * (2 * rows * span * (head_w // 2) + 2 * rows * span * head_w) + 2 * rows * width * width
    smem = pl.BlockSpec(memory_space=pltpu.SMEM)
    steps = HEADS // 4
    step_w = width // steps
    return pl.pallas_call(
        functools.partial(attention_kernel, back, head_w // 2),
        out_shape=jax.ShapeDtypeStruct((rows, width), jnp.bfloat16),
        grid=(steps,),
        in_specs=[
            smem,
            smem,
            pl.BlockSpec((rows, step_w), lambda h: (0, h)),
            pl.BlockSpec((keys, step_w), lambda h: (0, h)),
            pl.BlockSpec((keys, step_w), lambda h: (0, steps + h)),
            pl.BlockSpec((rows, 1), lambda h: (0, 0)),
            pl.BlockSpec((1, keys), lambda h: (0, 0)),
            pl.BlockSpec((step_w, width), lambda h: (h, 0)),
            pl.BlockSpec((rows, width), lambda h: (0, 0)),
        ],
        out_specs=pl.BlockSpec((rows, width), lambda h: (0, 0)),
        scratch_shapes=[pltpu.VMEM((rows, width), jnp.float32)],
        compiler_params=pltpu.CompilerParams(dimension_semantics=("arbitrary",)),
        cost_estimate=pl.CostEstimate(
            flops=flops,
            bytes_accessed=2 * keys * width * 2 + 3 * rows * width * 2 + width * width * 2,
            transcendentals=HEADS * 2 * rows * span,
        ),
    )(
        scalars,
        lam,
        q_in,
        all_kv,
        all_kv,
        query_segs.reshape(rows, 1),
        seg_row.reshape(1, keys),
        out_weight,
        base,
    )


def ffn_kernel(x_ref, gain_ref, gate_ref, up_ref, down_ref, out_ref):
    normed = (rms_rows(x_ref[...].astype(jnp.float32)) * gain_ref[...]).astype(jnp.bfloat16)
    contract = (((1,), (1,)), ((), ()))
    gate_proj = lax.dot_general(normed, gate_ref[...], contract, preferred_element_type=jnp.float32)
    up_proj = lax.dot_general(normed, up_ref[...], contract, preferred_element_type=jnp.float32)
    hidden = (gate_proj / (1.0 + jnp.exp(-gate_proj)) * up_proj).astype(jnp.bfloat16)
    out_ref[...] = jnp.dot(hidden, down_ref[...], preferred_element_type=jnp.float32).astype(
        out_ref.dtype
    )


def ffn_partial(rows, gain, gate_weight, up_weight, down_weight, tile):
    count, width = rows.shape
    hidden_w = gate_weight.shape[1]
    full = lambda i: (0, 0)
    gate_t = gate_weight.T
    up_t = up_weight.T
    return pl.pallas_call(
        ffn_kernel,
        out_shape=jax.ShapeDtypeStruct((count, width), jnp.bfloat16),
        grid=(count // tile,),
        in_specs=[
            pl.BlockSpec((tile, width), lambda i: (i, 0)),
            pl.BlockSpec((1, width), full),
            pl.BlockSpec((hidden_w, width), full),
            pl.BlockSpec((hidden_w, width), full),
            pl.BlockSpec((hidden_w, width), full),
        ],
        out_specs=pl.BlockSpec((tile, width), lambda i: (i, 0)),
        compiler_params=pltpu.CompilerParams(
            dimension_semantics=("arbitrary",), vmem_limit_bytes=48 * 1024 * 1024
        ),
        cost_estimate=pl.CostEstimate(
            flops=6 * count * width * hidden_w,
            bytes_accessed=3 * width * hidden_w * 2 + 2 * count * width * 2,
            transcendentals=count * hidden_w,
        ),
    )(rows, gain.reshape(1, width), gate_t, up_t, down_weight)


def project_kernel(x_ref, w_ref, out_ref):
    out_ref[...] = jnp.dot(x_ref[...], w_ref[...], preferred_element_type=jnp.float32).astype(
        out_ref.dtype
    )


def project_rows(rows, weight, tile):
    count, width = rows.shape
    cols = weight.shape[1]
    return pl.pallas_call(
        project_kernel,
        out_shape=jax.ShapeDtypeStruct((count, cols), jnp.bfloat16),
        grid=(count // tile,),
        in_specs=[
            pl.BlockSpec((tile, width), lambda i: (i, 0)),
            pl.BlockSpec((width, cols), lambda i: (0, 0)),
        ],
        out_specs=pl.BlockSpec((tile, cols), lambda i: (i, 0)),
        compiler_params=pltpu.CompilerParams(
            dimension_semantics=("arbitrary",), vmem_limit_bytes=48 * 1024 * 1024
        ),
        cost_estimate=pl.CostEstimate(
            flops=2 * count * width * cols,
            bytes_accessed=2 * (count * width + width * cols + count * cols),
            transcendentals=0,
        ),
    )(rows, weight)


def output_kernel(mid_ref, ffn_ref, gain_ref, out_ref, normed_ref):
    layer_output = (mid_ref[...].astype(jnp.float32) + ffn_ref[...].astype(jnp.float32)).astype(
        out_ref.dtype
    )
    out_ref[...] = layer_output
    normed_ref[...] = (rms_rows(layer_output.astype(jnp.float32)) * gain_ref[...]).astype(
        normed_ref.dtype
    )


def finish_rows(residual_mid, ffn_own, gain):
    rows, width = residual_mid.shape
    vmem = pl.BlockSpec(memory_space=pltpu.VMEM)
    shape = jax.ShapeDtypeStruct((rows, width), jnp.bfloat16)
    return pl.pallas_call(
        output_kernel,
        out_shape=(shape, shape),
        in_specs=[vmem, vmem, vmem],
        out_specs=(vmem, vmem),
        cost_estimate=pl.CostEstimate(
            flops=6 * rows * width, bytes_accessed=8 * rows * width, transcendentals=rows
        ),
    )(residual_mid, ffn_own, gain.reshape(1, width))


def body(
    layer_input,
    q_in,
    k_in,
    v_in,
    segment_ids,
    lambda_parts,
    out_weight,
    ffn_gain,
    gate_weight,
    up_weight,
    down_weight,
    next_gain,
    qkv_weight,
    page_owner,
    page_slot,
):
    row_count = q_in.shape[0]
    feat_width = q_in.shape[1]
    head_dim = feat_width // (2 * HEADS)
    peer_count = lax.axis_size("tok")
    tok_place = lax.axis_index("tok")
    seg_row = segment_ids[0]
    first_row = tok_place * row_count
    query_places = first_row + jnp.arange(row_count)
    query_segs = lax.dynamic_slice_in_dim(seg_row, first_row, row_count)
    lambda_mix = lambda_value(lambda_parts)
    score_scale = 1.0 / math.sqrt(head_dim)
    query_split = q_in.reshape(row_count, HEADS, 2, head_dim)
    run_max = jnp.full((HEADS, 2, row_count), NEG_FILL, jnp.float32)
    back = -(-(MAX_SEG - 1) // row_count)
    own_kv = jnp.concatenate([k_in, v_in], axis=1)
    all_kv = lax.all_gather(own_kv, "tok", axis=0, tiled=True)
    residual_mid = window_attention(
        q_in, all_kv, query_segs, seg_row, first_row, lambda_mix, back, out_weight, layer_input
    )
    gathered = lax.all_gather(residual_mid, "req", axis=0, tiled=True)
    partial = ffn_partial(gathered, ffn_gain, gate_weight, up_weight, down_weight, 256)
    ffn_own = lax.psum_scatter(partial, "req", scatter_dimension=0, tiled=True)
    layer_output, next_normed = finish_rows(residual_mid, ffn_own, next_gain)
    projected_cols = project_rows(
        lax.all_gather(next_normed, "req", axis=0, tiled=True), qkv_weight, 256
    )
    n_req = lax.axis_size("req")
    col_w = projected_cols.shape[1]
    arrived = lax.all_to_all(
        projected_cols.reshape(n_req, row_count, col_w), "req", 0, 0, tiled=True
    )
    projected = jnp.transpose(arrived, (1, 0, 2)).reshape(row_count, n_req * col_w)
    q_next = projected[:, :feat_width]
    pages_dev = row_count // PAGE
    assert pages_dev == peer_count
    key_values = projected[:, feat_width:].reshape(pages_dev, PAGE, 2 * feat_width)
    owner_all = page_owner[0].reshape(peer_count, pages_dev)
    slot_all = page_slot[0].reshape(peer_count, pages_dev)
    numbers = jnp.arange(pages_dev, dtype=jnp.int32)
    my_owners = lax.dynamic_index_in_dim(owner_all, tok_place, 0, keepdims=False)
    send_order = jnp.sum(
        jnp.where(my_owners[None, :] == numbers[:, None], numbers[None, :], 0), axis=1
    )
    outgoing = key_values[send_order].reshape(peer_count, 1, PAGE, 2 * feat_width)
    incoming = lax.all_to_all(outgoing, "tok", split_axis=0, concat_axis=0, tiled=True)
    incoming = incoming.reshape(pages_dev, PAGE, 2 * feat_width)
    slot_list = jnp.sum(jnp.where(owner_all == tok_place, slot_all, 0), axis=1)
    source_of_slot = jnp.sum(
        jnp.where(slot_list[None, :] == numbers[:, None], numbers[None, :], 0), axis=1
    )
    page_cache = incoming[source_of_slot]
    return (layer_output, q_next, page_cache)


def solution(mesh):
    in_specs = (
        P(("req", "tok"), None),
        P(("req", "tok"), None),
        P(("req", "tok"), None),
        P(("req", "tok"), None),
        P("req", None),
        P(),
        P(),
        P(),
        P(None, "req"),
        P(None, "req"),
        P("req", None),
        P(),
        P(None, "req"),
        P("req", None),
        P("req", None),
    )
    out_specs = (P(("req", "tok"), None), P(("req", "tok"), None), P(("req", "tok"), None, None))
    return jax.shard_map(body, mesh=mesh, in_specs=in_specs, out_specs=out_specs, check_vma=False)
```

```python
import functools
import math

import jax
import jax.numpy as jnp
from jax import lax
from jax.experimental import pallas as pl
from jax.experimental.pallas import tpu as pltpu
from jax.sharding import PartitionSpec as P

HEADS = 8
PAGE = 8


NEG_FILL = -1e30
LAMBDA_INIT = 0.2
EPSILON = 1e-05
MAX_SEG = 1024


def rms_rows(values):
    return values * lax.rsqrt(jnp.mean(values * values, axis=-1, keepdims=True) + EPSILON)


def lambda_value(lambda_parts):
    first_term = jnp.exp(jnp.sum(lambda_parts[0] * lambda_parts[1]))
    second_term = jnp.exp(jnp.sum(lambda_parts[2] * lambda_parts[3]))
    return first_term - second_term + LAMBDA_INIT


def attention_kernel(
    back, head_dim, scalars_ref, lam_ref, q_ref, k_ref, v_ref, qseg_ref, kseg_ref, w_ref, base_ref, out_ref, total_ref
):
    rows = q_ref.shape[0]
    span = (back + 1) * rows
    start = pl.multiple_of(scalars_ref[0], rows)
    query_places = scalars_ref[1] + lax.broadcasted_iota(jnp.int32, (rows, span), 0)
    key_places = start + lax.broadcasted_iota(jnp.int32, (rows, span), 1)
    key_segs = kseg_ref[:, pl.ds(start, span)]
    visible = (key_segs == qseg_ref[...]) & (key_places <= query_places)
    score_scale = 1.0 / math.sqrt(head_dim)
    head_w = 2 * head_dim
    head_outs = []
    for head in range(q_ref.shape[1] // head_w):
        values = v_ref[pl.ds(start, span), head * head_w:(head + 1) * head_w]
        map_outputs = []
        for map_index in range(2):
            first = head * head_w + map_index * head_dim
            query_map = q_ref[:, first:first + head_dim]
            key_map = k_ref[pl.ds(start, span), first:first + head_dim]
            scores = (
                lax.dot_general(
                    query_map, key_map, (((1,), (1,)), ((), ())), preferred_element_type=jnp.float32
                )
                * score_scale
            )
            scores = jnp.where(visible, scores, NEG_FILL)
            row_max = jnp.max(scores, axis=1, keepdims=True)
            weights = jnp.exp(scores - row_max)
            totals = jnp.sum(weights, axis=1, keepdims=True)
            map_out = (
                jnp.dot(weights.astype(jnp.bfloat16), values, preferred_element_type=jnp.float32)
                / totals
            )
            map_outputs.append(map_out)
        difference = map_outputs[0] - lam_ref[0] * map_outputs[1]
        head_outs.append((rms_rows(difference) * (1.0 - LAMBDA_INIT)).astype(jnp.bfloat16))
    head_out = jnp.concatenate(head_outs, axis=1)
    step = pl.program_id(0)

    @pl.when(step == 0)
    def _():
        total_ref[...] = jnp.zeros_like(total_ref)

    total_ref[...] += jnp.dot(head_out, w_ref[...], preferred_element_type=jnp.float32)

    @pl.when(step == pl.num_programs(0) - 1)
    def _():
        out_ref[...] = (base_ref[...].astype(jnp.float32) + total_ref[...]).astype(out_ref.dtype)


def window_attention(q_in, all_kv, query_segs, seg_row, first_row, lambda_mix, back, out_weight, base):
    rows, width = q_in.shape
    keys = all_kv.shape[0]
    head_w = width // HEADS
    start = jnp.maximum(first_row - back * rows, 0)
    scalars = jnp.stack([start, first_row]).astype(jnp.int32)
    lam = jnp.reshape(lambda_mix, (1,)).astype(jnp.float32)
    span = (back + 1) * rows
    flops = HEADS * 2 * (2 * rows * span * (head_w // 2) + 2 * rows * span * head_w) + 2 * rows * width * width
    smem = pl.BlockSpec(memory_space=pltpu.SMEM)
    steps = HEADS // 2
    step_w = width // steps
    return pl.pallas_call(
        functools.partial(attention_kernel, back, head_w // 2),
        out_shape=jax.ShapeDtypeStruct((rows, width), jnp.bfloat16),
        grid=(steps,),
        in_specs=[
            smem,
            smem,
            pl.BlockSpec((rows, step_w), lambda h: (0, h)),
            pl.BlockSpec((keys, step_w), lambda h: (0, h)),
            pl.BlockSpec((keys, step_w), lambda h: (0, steps + h)),
            pl.BlockSpec((rows, 1), lambda h: (0, 0)),
            pl.BlockSpec((1, keys), lambda h: (0, 0)),
            pl.BlockSpec((step_w, width), lambda h: (h, 0)),
            pl.BlockSpec((rows, width), lambda h: (0, 0)),
        ],
        out_specs=pl.BlockSpec((rows, width), lambda h: (0, 0)),
        scratch_shapes=[pltpu.VMEM((rows, width), jnp.float32)],
        compiler_params=pltpu.CompilerParams(dimension_semantics=("arbitrary",)),
        cost_estimate=pl.CostEstimate(
            flops=flops,
            bytes_accessed=2 * keys * width * 2 + 3 * rows * width * 2 + width * width * 2,
            transcendentals=HEADS * 2 * rows * span,
        ),
    )(
        scalars,
        lam,
        q_in,
        all_kv,
        all_kv,
        query_segs.reshape(rows, 1),
        seg_row.reshape(1, keys),
        out_weight,
        base,
    )


def ffn_kernel(x_ref, gain_ref, gate_ref, up_ref, down_hbm, out_ref, down_ref, down_sem):
    step = pl.program_id(0)
    fetch = pltpu.make_async_copy(down_hbm, down_ref, down_sem)

    @pl.when(step == 0)
    def _():
        fetch.start()

    normed = (rms_rows(x_ref[...].astype(jnp.float32)) * gain_ref[...]).astype(jnp.bfloat16)
    contract = (((1,), (1,)), ((), ()))
    gate_proj = lax.dot_general(normed, gate_ref[...], contract, preferred_element_type=jnp.float32)
    up_proj = lax.dot_general(normed, up_ref[...], contract, preferred_element_type=jnp.float32)
    hidden = (gate_proj / (1.0 + jnp.exp(-gate_proj)) * up_proj).astype(jnp.bfloat16)

    @pl.when(step == 0)
    def _():
        fetch.wait()

    out_ref[...] = jnp.dot(hidden, down_ref[...], preferred_element_type=jnp.float32).astype(
        out_ref.dtype
    )


def ffn_partial(rows, gain, gate_weight, up_weight, down_weight, tile):
    count, width = rows.shape
    hidden_w = gate_weight.shape[1]
    full = lambda i: (0, 0)
    gate_t = gate_weight.T
    up_t = up_weight.T
    return pl.pallas_call(
        ffn_kernel,
        out_shape=jax.ShapeDtypeStruct((count, width), jnp.bfloat16),
        grid=(count // tile,),
        in_specs=[
            pl.BlockSpec((tile, width), lambda i: (i, 0)),
            pl.BlockSpec((1, width), full),
            pl.BlockSpec((hidden_w, width), full),
            pl.BlockSpec((hidden_w, width), full),
            pl.BlockSpec(memory_space=pl.ANY),
        ],
        out_specs=pl.BlockSpec((tile, width), lambda i: (i, 0)),
        scratch_shapes=[
            pltpu.VMEM((hidden_w, width), down_weight.dtype),
            pltpu.SemaphoreType.DMA(()),
        ],
        compiler_params=pltpu.CompilerParams(
            dimension_semantics=("arbitrary",), vmem_limit_bytes=48 * 1024 * 1024
        ),
        cost_estimate=pl.CostEstimate(
            flops=6 * count * width * hidden_w,
            bytes_accessed=3 * width * hidden_w * 2 + 2 * count * width * 2,
            transcendentals=count * hidden_w,
        ),
    )(rows, gain.reshape(1, width), gate_t, up_t, down_weight)


def project_kernel(x_ref, w_ref, out_ref):
    out_ref[...] = jnp.dot(x_ref[...], w_ref[...], preferred_element_type=jnp.float32).astype(
        out_ref.dtype
    )


def project_rows(rows, weight, tile):
    count, width = rows.shape
    cols = weight.shape[1]
    return pl.pallas_call(
        project_kernel,
        out_shape=jax.ShapeDtypeStruct((count, cols), jnp.bfloat16),
        grid=(count // tile,),
        in_specs=[
            pl.BlockSpec((tile, width), lambda i: (i, 0)),
            pl.BlockSpec((width, cols), lambda i: (0, 0)),
        ],
        out_specs=pl.BlockSpec((tile, cols), lambda i: (i, 0)),
        compiler_params=pltpu.CompilerParams(
            dimension_semantics=("arbitrary",), vmem_limit_bytes=48 * 1024 * 1024
        ),
        cost_estimate=pl.CostEstimate(
            flops=2 * count * width * cols,
            bytes_accessed=2 * (count * width + width * cols + count * cols),
            transcendentals=0,
        ),
    )(rows, weight)


def output_kernel(mid_ref, ffn_ref, gain_ref, out_ref, normed_ref):
    layer_output = (mid_ref[...].astype(jnp.float32) + ffn_ref[...].astype(jnp.float32)).astype(
        out_ref.dtype
    )
    out_ref[...] = layer_output
    normed_ref[...] = (rms_rows(layer_output.astype(jnp.float32)) * gain_ref[...]).astype(
        normed_ref.dtype
    )


def finish_rows(residual_mid, ffn_own, gain):
    rows, width = residual_mid.shape
    vmem = pl.BlockSpec(memory_space=pltpu.VMEM)
    shape = jax.ShapeDtypeStruct((rows, width), jnp.bfloat16)
    return pl.pallas_call(
        output_kernel,
        out_shape=(shape, shape),
        in_specs=[vmem, vmem, vmem],
        out_specs=(vmem, vmem),
        cost_estimate=pl.CostEstimate(
            flops=6 * rows * width, bytes_accessed=8 * rows * width, transcendentals=rows
        ),
    )(residual_mid, ffn_own, gain.reshape(1, width))


def body(
    layer_input,
    q_in,
    k_in,
    v_in,
    segment_ids,
    lambda_parts,
    out_weight,
    ffn_gain,
    gate_weight,
    up_weight,
    down_weight,
    next_gain,
    qkv_weight,
    page_owner,
    page_slot,
):
    row_count = q_in.shape[0]
    feat_width = q_in.shape[1]
    head_dim = feat_width // (2 * HEADS)
    peer_count = lax.axis_size("tok")
    tok_place = lax.axis_index("tok")
    seg_row = segment_ids[0]
    first_row = tok_place * row_count
    query_places = first_row + jnp.arange(row_count)
    query_segs = lax.dynamic_slice_in_dim(seg_row, first_row, row_count)
    lambda_mix = lambda_value(lambda_parts)
    score_scale = 1.0 / math.sqrt(head_dim)
    query_split = q_in.reshape(row_count, HEADS, 2, head_dim)
    run_max = jnp.full((HEADS, 2, row_count), NEG_FILL, jnp.float32)
    back = -(-(MAX_SEG - 1) // row_count)
    own_kv = jnp.concatenate([k_in, v_in], axis=1)
    all_kv = lax.all_gather(own_kv, "tok", axis=0, tiled=True)
    residual_mid = window_attention(
        q_in, all_kv, query_segs, seg_row, first_row, lambda_mix, back, out_weight, layer_input
    )
    gathered = lax.all_gather(residual_mid, "req", axis=0, tiled=True)
    partial = ffn_partial(gathered, ffn_gain, gate_weight, up_weight, down_weight, 256)
    ffn_own = lax.psum_scatter(partial, "req", scatter_dimension=0, tiled=True)
    layer_output, next_normed = finish_rows(residual_mid, ffn_own, next_gain)
    projected_cols = project_rows(
        lax.all_gather(next_normed, "req", axis=0, tiled=True), qkv_weight, 256
    )
    n_req = lax.axis_size("req")
    col_w = projected_cols.shape[1]
    arrived = lax.all_to_all(
        projected_cols.reshape(n_req, row_count, col_w), "req", 0, 0, tiled=True
    )
    projected = jnp.transpose(arrived, (1, 0, 2)).reshape(row_count, n_req * col_w)
    q_next = projected[:, :feat_width]
    pages_dev = row_count // PAGE
    assert pages_dev == peer_count
    key_values = projected[:, feat_width:].reshape(pages_dev, PAGE, 2 * feat_width)
    owner_all = page_owner[0].reshape(peer_count, pages_dev)
    slot_all = page_slot[0].reshape(peer_count, pages_dev)
    numbers = jnp.arange(pages_dev, dtype=jnp.int32)
    my_owners = lax.dynamic_index_in_dim(owner_all, tok_place, 0, keepdims=False)
    send_order = jnp.sum(
        jnp.where(my_owners[None, :] == numbers[:, None], numbers[None, :], 0), axis=1
    )
    outgoing = key_values[send_order].reshape(peer_count, 1, PAGE, 2 * feat_width)
    incoming = lax.all_to_all(outgoing, "tok", split_axis=0, concat_axis=0, tiled=True)
    incoming = incoming.reshape(pages_dev, PAGE, 2 * feat_width)
    slot_list = jnp.sum(jnp.where(owner_all == tok_place, slot_all, 0), axis=1)
    source_of_slot = jnp.sum(
        jnp.where(slot_list[None, :] == numbers[:, None], numbers[None, :], 0), axis=1
    )
    page_cache = incoming[source_of_slot]
    return (layer_output, q_next, page_cache)


def solution(mesh):
    in_specs = (
        P(("req", "tok"), None),
        P(("req", "tok"), None),
        P(("req", "tok"), None),
        P(("req", "tok"), None),
        P("req", None),
        P(),
        P(),
        P(),
        P(None, "req"),
        P(None, "req"),
        P("req", None),
        P(),
        P(None, "req"),
        P("req", None),
        P("req", None),
    )
    out_specs = (P(("req", "tok"), None), P(("req", "tok"), None), P(("req", "tok"), None, None))
    return jax.shard_map(body, mesh=mesh, in_specs=in_specs, out_specs=out_specs, check_vma=False)
```

```python
import functools
import math

import jax
import jax.numpy as jnp
from jax import lax
from jax.experimental import pallas as pl
from jax.experimental.pallas import tpu as pltpu
from jax.sharding import PartitionSpec as P

HEADS = 8
PAGE = 8


NEG_FILL = -1e30
LAMBDA_INIT = 0.2
EPSILON = 1e-05
MAX_SEG = 1024


def rms_rows(values):
    return values * lax.rsqrt(jnp.mean(values * values, axis=-1, keepdims=True) + EPSILON)


def lambda_value(lambda_parts):
    first_term = jnp.exp(jnp.sum(lambda_parts[0] * lambda_parts[1]))
    second_term = jnp.exp(jnp.sum(lambda_parts[2] * lambda_parts[3]))
    return first_term - second_term + LAMBDA_INIT


def attention_kernel(
    back, head_dim, scalars_ref, lam_ref, q_ref, k_ref, v_ref, qseg_ref, kseg_ref, w_ref, base_ref, out_ref, total_ref
):
    rows = q_ref.shape[0]
    span = (back + 1) * rows
    start = pl.multiple_of(scalars_ref[0], rows)
    query_places = scalars_ref[1] + lax.broadcasted_iota(jnp.int32, (rows, span), 0)
    key_places = start + lax.broadcasted_iota(jnp.int32, (rows, span), 1)
    key_segs = kseg_ref[:, pl.ds(start, span)]
    visible = (key_segs == qseg_ref[...]) & (key_places <= query_places)
    score_scale = 1.0 / math.sqrt(head_dim)
    head_w = 2 * head_dim
    head_outs = []
    for head in range(q_ref.shape[1] // head_w):
        values = v_ref[pl.ds(start, span), head * head_w:(head + 1) * head_w]
        map_outputs = []
        for map_index in range(2):
            first = head * head_w + map_index * head_dim
            query_map = q_ref[:, first:first + head_dim]
            key_map = k_ref[pl.ds(start, span), first:first + head_dim]
            scores = (
                lax.dot_general(
                    query_map, key_map, (((1,), (1,)), ((), ())), preferred_element_type=jnp.float32
                )
                * score_scale
            )
            scores = jnp.where(visible, scores, NEG_FILL)
            row_max = jnp.max(scores, axis=1, keepdims=True)
            weights = jnp.exp(scores - row_max)
            totals = jnp.sum(weights, axis=1, keepdims=True)
            map_out = (
                jnp.dot(weights.astype(jnp.bfloat16), values, preferred_element_type=jnp.float32)
                / totals
            )
            map_outputs.append(map_out)
        difference = map_outputs[0] - lam_ref[0] * map_outputs[1]
        head_outs.append((rms_rows(difference) * (1.0 - LAMBDA_INIT)).astype(jnp.bfloat16))
    head_out = jnp.concatenate(head_outs, axis=1)
    step = pl.program_id(0)

    @pl.when(step == 0)
    def _():
        total_ref[...] = jnp.zeros_like(total_ref)

    total_ref[...] += jnp.dot(head_out, w_ref[...], preferred_element_type=jnp.float32)

    @pl.when(step == pl.num_programs(0) - 1)
    def _():
        out_ref[...] = (base_ref[...].astype(jnp.float32) + total_ref[...]).astype(out_ref.dtype)


def window_attention(q_in, all_kv, query_segs, seg_row, first_row, lambda_mix, back, out_weight, base):
    rows, width = q_in.shape
    keys = all_kv.shape[0]
    head_w = width // HEADS
    start = jnp.maximum(first_row - back * rows, 0)
    scalars = jnp.stack([start, first_row]).astype(jnp.int32)
    lam = jnp.reshape(lambda_mix, (1,)).astype(jnp.float32)
    span = (back + 1) * rows
    flops = HEADS * 2 * (2 * rows * span * (head_w // 2) + 2 * rows * span * head_w) + 2 * rows * width * width
    smem = pl.BlockSpec(memory_space=pltpu.SMEM)
    steps = HEADS // 2
    step_w = width // steps
    return pl.pallas_call(
        functools.partial(attention_kernel, back, head_w // 2),
        out_shape=jax.ShapeDtypeStruct((rows, width), jnp.bfloat16),
        grid=(steps,),
        in_specs=[
            smem,
            smem,
            pl.BlockSpec((rows, step_w), lambda h: (0, h)),
            pl.BlockSpec((keys, step_w), lambda h: (0, h)),
            pl.BlockSpec((keys, step_w), lambda h: (0, steps + h)),
            pl.BlockSpec((rows, 1), lambda h: (0, 0)),
            pl.BlockSpec((1, keys), lambda h: (0, 0)),
            pl.BlockSpec((step_w, width), lambda h: (h, 0)),
            pl.BlockSpec((rows, width), lambda h: (0, 0)),
        ],
        out_specs=pl.BlockSpec((rows, width), lambda h: (0, 0)),
        scratch_shapes=[pltpu.VMEM((rows, width), jnp.float32)],
        compiler_params=pltpu.CompilerParams(dimension_semantics=("arbitrary",)),
        cost_estimate=pl.CostEstimate(
            flops=flops,
            bytes_accessed=2 * keys * width * 2 + 3 * rows * width * 2 + width * width * 2,
            transcendentals=HEADS * 2 * rows * span,
        ),
    )(
        scalars,
        lam,
        q_in,
        all_kv,
        all_kv,
        query_segs.reshape(rows, 1),
        seg_row.reshape(1, keys),
        out_weight,
        base,
    )


def ffn_kernel(x_ref, gain_ref, gate_ref, up_ref, down_hbm, out_ref, down_ref, down_sem):
    step = pl.program_id(0)
    fetch = pltpu.make_async_copy(down_hbm, down_ref, down_sem)

    @pl.when(step == 0)
    def _():
        fetch.start()

    normed = (rms_rows(x_ref[...].astype(jnp.float32)) * gain_ref[...]).astype(jnp.bfloat16)
    contract = (((1,), (1,)), ((), ()))
    gate_proj = lax.dot_general(normed, gate_ref[...], contract, preferred_element_type=jnp.float32)
    up_proj = lax.dot_general(normed, up_ref[...], contract, preferred_element_type=jnp.float32)
    hidden = (gate_proj / (1.0 + jnp.exp(-gate_proj)) * up_proj).astype(jnp.bfloat16)

    @pl.when(step == 0)
    def _():
        fetch.wait()

    out_ref[...] = jnp.dot(hidden, down_ref[...], preferred_element_type=jnp.float32).astype(
        out_ref.dtype
    )


def ffn_partial(rows, gain, gate_weight, up_weight, down_weight, tile):
    count, width = rows.shape
    hidden_w = gate_weight.shape[1]
    full = lambda i: (0, 0)
    gate_t = gate_weight.T
    up_t = up_weight.T
    return pl.pallas_call(
        ffn_kernel,
        out_shape=jax.ShapeDtypeStruct((count, width), jnp.bfloat16),
        grid=(count // tile,),
        in_specs=[
            pl.BlockSpec((tile, width), lambda i: (i, 0)),
            pl.BlockSpec((1, width), full),
            pl.BlockSpec((hidden_w, width), full),
            pl.BlockSpec((hidden_w, width), full),
            pl.BlockSpec(memory_space=pl.ANY),
        ],
        out_specs=pl.BlockSpec((tile, width), lambda i: (i, 0)),
        scratch_shapes=[
            pltpu.VMEM((hidden_w, width), down_weight.dtype),
            pltpu.SemaphoreType.DMA(()),
        ],
        compiler_params=pltpu.CompilerParams(
            dimension_semantics=("arbitrary",), vmem_limit_bytes=48 * 1024 * 1024
        ),
        cost_estimate=pl.CostEstimate(
            flops=6 * count * width * hidden_w,
            bytes_accessed=3 * width * hidden_w * 2 + 2 * count * width * 2,
            transcendentals=count * hidden_w,
        ),
    )(rows, gain.reshape(1, width), gate_t, up_t, down_weight)


def project_kernel(x_ref, w_ref, out_ref):
    out_ref[...] = jnp.dot(x_ref[...], w_ref[...], preferred_element_type=jnp.float32).astype(
        out_ref.dtype
    )


def project_rows(rows, weight, tile):
    count, width = rows.shape
    cols = weight.shape[1]
    return pl.pallas_call(
        project_kernel,
        out_shape=jax.ShapeDtypeStruct((count, cols), jnp.bfloat16),
        grid=(count // tile,),
        in_specs=[
            pl.BlockSpec((tile, width), lambda i: (i, 0)),
            pl.BlockSpec((width, cols), lambda i: (0, 0)),
        ],
        out_specs=pl.BlockSpec((tile, cols), lambda i: (i, 0)),
        compiler_params=pltpu.CompilerParams(
            dimension_semantics=("arbitrary",), vmem_limit_bytes=48 * 1024 * 1024
        ),
        cost_estimate=pl.CostEstimate(
            flops=2 * count * width * cols,
            bytes_accessed=2 * (count * width + width * cols + count * cols),
            transcendentals=0,
        ),
    )(rows, weight)


def output_kernel(mid_ref, ffn_ref, gain_ref, out_ref, normed_ref):
    layer_output = (mid_ref[...].astype(jnp.float32) + ffn_ref[...].astype(jnp.float32)).astype(
        out_ref.dtype
    )
    out_ref[...] = layer_output
    normed_ref[...] = (rms_rows(layer_output.astype(jnp.float32)) * gain_ref[...]).astype(
        normed_ref.dtype
    )


def finish_rows(residual_mid, ffn_own, gain):
    rows, width = residual_mid.shape
    vmem = pl.BlockSpec(memory_space=pltpu.VMEM)
    shape = jax.ShapeDtypeStruct((rows, width), jnp.bfloat16)
    return pl.pallas_call(
        output_kernel,
        out_shape=(shape, shape),
        in_specs=[vmem, vmem, vmem],
        out_specs=(vmem, vmem),
        cost_estimate=pl.CostEstimate(
            flops=6 * rows * width, bytes_accessed=8 * rows * width, transcendentals=rows
        ),
    )(residual_mid, ffn_own, gain.reshape(1, width))


def body(
    layer_input,
    q_in,
    k_in,
    v_in,
    segment_ids,
    lambda_parts,
    out_weight,
    ffn_gain,
    gate_weight,
    up_weight,
    down_weight,
    next_gain,
    qkv_weight,
    page_owner,
    page_slot,
):
    row_count = q_in.shape[0]
    feat_width = q_in.shape[1]
    head_dim = feat_width // (2 * HEADS)
    peer_count = lax.axis_size("tok")
    tok_place = lax.axis_index("tok")
    seg_row = segment_ids[0]
    first_row = tok_place * row_count
    query_places = first_row + jnp.arange(row_count)
    query_segs = lax.dynamic_slice_in_dim(seg_row, first_row, row_count)
    lambda_mix = lambda_value(lambda_parts)
    score_scale = 1.0 / math.sqrt(head_dim)
    query_split = q_in.reshape(row_count, HEADS, 2, head_dim)
    run_max = jnp.full((HEADS, 2, row_count), NEG_FILL, jnp.float32)
    back = -(-(MAX_SEG - 1) // row_count)
    own_kv = jnp.concatenate([k_in, v_in], axis=1)
    all_kv = lax.all_gather(own_kv, "tok", axis=0, tiled=True)
    residual_mid = window_attention(
        q_in, all_kv, query_segs, seg_row, first_row, lambda_mix, back, out_weight, layer_input
    )
    gathered = lax.all_gather(residual_mid, "req", axis=0, tiled=True)
    partial = ffn_partial(gathered, ffn_gain, gate_weight, up_weight, down_weight, 512)
    ffn_own = lax.psum_scatter(partial, "req", scatter_dimension=0, tiled=True)
    layer_output, next_normed = finish_rows(residual_mid, ffn_own, next_gain)
    projected_cols = project_rows(
        lax.all_gather(next_normed, "req", axis=0, tiled=True), qkv_weight, 256
    )
    n_req = lax.axis_size("req")
    col_w = projected_cols.shape[1]
    arrived = lax.all_to_all(
        projected_cols.reshape(n_req, row_count, col_w), "req", 0, 0, tiled=True
    )
    projected = jnp.transpose(arrived, (1, 0, 2)).reshape(row_count, n_req * col_w)
    q_next = projected[:, :feat_width]
    pages_dev = row_count // PAGE
    assert pages_dev == peer_count
    key_values = projected[:, feat_width:].reshape(pages_dev, PAGE, 2 * feat_width)
    owner_all = page_owner[0].reshape(peer_count, pages_dev)
    slot_all = page_slot[0].reshape(peer_count, pages_dev)
    numbers = jnp.arange(pages_dev, dtype=jnp.int32)
    my_owners = lax.dynamic_index_in_dim(owner_all, tok_place, 0, keepdims=False)
    send_order = jnp.sum(
        jnp.where(my_owners[None, :] == numbers[:, None], numbers[None, :], 0), axis=1
    )
    outgoing = key_values[send_order].reshape(peer_count, 1, PAGE, 2 * feat_width)
    incoming = lax.all_to_all(outgoing, "tok", split_axis=0, concat_axis=0, tiled=True)
    incoming = incoming.reshape(pages_dev, PAGE, 2 * feat_width)
    slot_list = jnp.sum(jnp.where(owner_all == tok_place, slot_all, 0), axis=1)
    source_of_slot = jnp.sum(
        jnp.where(slot_list[None, :] == numbers[:, None], numbers[None, :], 0), axis=1
    )
    page_cache = incoming[source_of_slot]
    return (layer_output, q_next, page_cache)


def solution(mesh):
    in_specs = (
        P(("req", "tok"), None),
        P(("req", "tok"), None),
        P(("req", "tok"), None),
        P(("req", "tok"), None),
        P("req", None),
        P(),
        P(),
        P(),
        P(None, "req"),
        P(None, "req"),
        P("req", None),
        P(),
        P(None, "req"),
        P("req", None),
        P("req", None),
    )
    out_specs = (P(("req", "tok"), None), P(("req", "tok"), None), P(("req", "tok"), None, None))
    return jax.shard_map(body, mesh=mesh, in_specs=in_specs, out_specs=out_specs, check_vma=False)
```

```python
import functools
import math

import jax
import jax.numpy as jnp
from jax import lax
from jax.experimental import pallas as pl
from jax.experimental.pallas import tpu as pltpu
from jax.sharding import PartitionSpec as P

HEADS = 8
PAGE = 8


NEG_FILL = -1e30
LAMBDA_INIT = 0.2
EPSILON = 1e-05
MAX_SEG = 1024


def rms_rows(values):
    return values * lax.rsqrt(jnp.mean(values * values, axis=-1, keepdims=True) + EPSILON)


def lambda_value(lambda_parts):
    first_term = jnp.exp(jnp.sum(lambda_parts[0] * lambda_parts[1]))
    second_term = jnp.exp(jnp.sum(lambda_parts[2] * lambda_parts[3]))
    return first_term - second_term + LAMBDA_INIT


def attention_kernel(
    back, head_dim, scalars_ref, lam_ref, q_ref, k_ref, v_ref, qseg_ref, kseg_ref, w_ref, base_ref, out_ref, total_ref
):
    rows = q_ref.shape[0]
    span = (back + 1) * rows
    start = pl.multiple_of(scalars_ref[0], rows)
    query_places = scalars_ref[1] + lax.broadcasted_iota(jnp.int32, (rows, span), 0)
    key_places = start + lax.broadcasted_iota(jnp.int32, (rows, span), 1)
    key_segs = kseg_ref[:, pl.ds(start, span)]
    visible = (key_segs == qseg_ref[...]) & (key_places <= query_places)
    score_scale = 1.0 / math.sqrt(head_dim)
    head_w = 2 * head_dim
    head_outs = []
    for head in range(q_ref.shape[1] // head_w):
        values = v_ref[pl.ds(start, span), head * head_w:(head + 1) * head_w]
        map_outputs = []
        for map_index in range(2):
            first = head * head_w + map_index * head_dim
            query_map = q_ref[:, first:first + head_dim]
            key_map = k_ref[pl.ds(start, span), first:first + head_dim]
            scores = (
                lax.dot_general(
                    query_map, key_map, (((1,), (1,)), ((), ())), preferred_element_type=jnp.float32
                )
                * score_scale
            )
            scores = jnp.where(visible, scores, NEG_FILL)
            row_max = jnp.max(scores, axis=1, keepdims=True)
            weights = jnp.exp(scores - row_max)
            totals = jnp.sum(weights, axis=1, keepdims=True)
            map_out = (
                jnp.dot(weights.astype(jnp.bfloat16), values, preferred_element_type=jnp.float32)
                / totals
            )
            map_outputs.append(map_out)
        difference = map_outputs[0] - lam_ref[0] * map_outputs[1]
        head_outs.append((rms_rows(difference) * (1.0 - LAMBDA_INIT)).astype(jnp.bfloat16))
    head_out = jnp.concatenate(head_outs, axis=1)
    step = pl.program_id(0)

    @pl.when(step == 0)
    def _():
        total_ref[...] = jnp.zeros_like(total_ref)

    total_ref[...] += jnp.dot(head_out, w_ref[...], preferred_element_type=jnp.float32)

    @pl.when(step == pl.num_programs(0) - 1)
    def _():
        out_ref[...] = (base_ref[...].astype(jnp.float32) + total_ref[...]).astype(out_ref.dtype)


def window_attention(q_in, all_kv, query_segs, seg_row, first_row, lambda_mix, back, out_weight, base):
    rows, width = q_in.shape
    keys = all_kv.shape[0]
    head_w = width // HEADS
    start = jnp.maximum(first_row - back * rows, 0)
    scalars = jnp.stack([start, first_row]).astype(jnp.int32)
    lam = jnp.reshape(lambda_mix, (1,)).astype(jnp.float32)
    span = (back + 1) * rows
    flops = HEADS * 2 * (2 * rows * span * (head_w // 2) + 2 * rows * span * head_w) + 2 * rows * width * width
    smem = pl.BlockSpec(memory_space=pltpu.SMEM)
    steps = HEADS // 2
    step_w = width // steps
    return pl.pallas_call(
        functools.partial(attention_kernel, back, head_w // 2),
        out_shape=jax.ShapeDtypeStruct((rows, width), jnp.bfloat16),
        grid=(steps,),
        in_specs=[
            smem,
            smem,
            pl.BlockSpec((rows, step_w), lambda h: (0, h)),
            pl.BlockSpec((keys, step_w), lambda h: (0, h)),
            pl.BlockSpec((keys, step_w), lambda h: (0, steps + h)),
            pl.BlockSpec((rows, 1), lambda h: (0, 0)),
            pl.BlockSpec((1, keys), lambda h: (0, 0)),
            pl.BlockSpec((step_w, width), lambda h: (h, 0)),
            pl.BlockSpec((rows, width), lambda h: (0, 0)),
        ],
        out_specs=pl.BlockSpec((rows, width), lambda h: (0, 0)),
        scratch_shapes=[pltpu.VMEM((rows, width), jnp.float32)],
        compiler_params=pltpu.CompilerParams(dimension_semantics=("arbitrary",)),
        cost_estimate=pl.CostEstimate(
            flops=flops,
            bytes_accessed=2 * keys * width * 2 + 3 * rows * width * 2 + width * width * 2,
            transcendentals=HEADS * 2 * rows * span,
        ),
    )(
        scalars,
        lam,
        q_in,
        all_kv,
        all_kv,
        query_segs.reshape(rows, 1),
        seg_row.reshape(1, keys),
        out_weight,
        base,
    )


def ffn_kernel(x_ref, gain_ref, gate_ref, up_ref, down_hbm, out_ref, down_ref, down_sem):
    step = pl.program_id(0)
    fetch = pltpu.make_async_copy(down_hbm, down_ref, down_sem)

    @pl.when(step == 0)
    def _():
        fetch.start()

    normed = (rms_rows(x_ref[...].astype(jnp.float32)) * gain_ref[...]).astype(jnp.bfloat16)
    contract = (((1,), (1,)), ((), ()))
    gate_proj = lax.dot_general(normed, gate_ref[...], contract, preferred_element_type=jnp.float32)
    up_proj = lax.dot_general(normed, up_ref[...], contract, preferred_element_type=jnp.float32)
    hidden = (gate_proj / (1.0 + jnp.exp(-gate_proj)) * up_proj).astype(jnp.bfloat16)

    @pl.when(step == 0)
    def _():
        fetch.wait()

    out_ref[...] = jnp.dot(hidden, down_ref[...], preferred_element_type=jnp.float32).astype(
        out_ref.dtype
    )


def ffn_partial(rows, gain, gate_weight, up_weight, down_weight, tile):
    count, width = rows.shape
    hidden_w = gate_weight.shape[1]
    full = lambda i: (0, 0)
    gate_t = gate_weight.T
    up_t = up_weight.T
    return pl.pallas_call(
        ffn_kernel,
        out_shape=jax.ShapeDtypeStruct((count, width), jnp.bfloat16),
        grid=(count // tile,),
        in_specs=[
            pl.BlockSpec((tile, width), lambda i: (i, 0)),
            pl.BlockSpec((1, width), full),
            pl.BlockSpec((hidden_w, width), full),
            pl.BlockSpec((hidden_w, width), full),
            pl.BlockSpec(memory_space=pl.ANY),
        ],
        out_specs=pl.BlockSpec((tile, width), lambda i: (i, 0)),
        scratch_shapes=[
            pltpu.VMEM((hidden_w, width), down_weight.dtype),
            pltpu.SemaphoreType.DMA(()),
        ],
        compiler_params=pltpu.CompilerParams(
            dimension_semantics=("arbitrary",), vmem_limit_bytes=48 * 1024 * 1024
        ),
        cost_estimate=pl.CostEstimate(
            flops=6 * count * width * hidden_w,
            bytes_accessed=3 * width * hidden_w * 2 + 2 * count * width * 2,
            transcendentals=count * hidden_w,
        ),
    )(rows, gain.reshape(1, width), gate_t, up_t, down_weight)


def project_kernel(x_ref, w_ref, out_ref):
    out_ref[...] = jnp.dot(x_ref[...], w_ref[...], preferred_element_type=jnp.float32).astype(
        out_ref.dtype
    )


def project_rows(rows, weight, tile):
    count, width = rows.shape
    cols = weight.shape[1]
    return pl.pallas_call(
        project_kernel,
        out_shape=jax.ShapeDtypeStruct((count, cols), jnp.bfloat16),
        grid=(count // tile,),
        in_specs=[
            pl.BlockSpec((tile, width), lambda i: (i, 0)),
            pl.BlockSpec((width, cols), lambda i: (0, 0)),
        ],
        out_specs=pl.BlockSpec((tile, cols), lambda i: (i, 0)),
        compiler_params=pltpu.CompilerParams(
            dimension_semantics=("arbitrary",), vmem_limit_bytes=48 * 1024 * 1024
        ),
        cost_estimate=pl.CostEstimate(
            flops=2 * count * width * cols,
            bytes_accessed=2 * (count * width + width * cols + count * cols),
            transcendentals=0,
        ),
    )(rows, weight)


def output_kernel(mid_ref, ffn_ref, gain_ref, out_ref, normed_ref):
    layer_output = (mid_ref[...].astype(jnp.float32) + ffn_ref[...].astype(jnp.float32)).astype(
        out_ref.dtype
    )
    out_ref[...] = layer_output
    normed_ref[...] = (rms_rows(layer_output.astype(jnp.float32)) * gain_ref[...]).astype(
        normed_ref.dtype
    )


def finish_rows(residual_mid, ffn_own, gain):
    rows, width = residual_mid.shape
    vmem = pl.BlockSpec(memory_space=pltpu.VMEM)
    shape = jax.ShapeDtypeStruct((rows, width), jnp.bfloat16)
    return pl.pallas_call(
        output_kernel,
        out_shape=(shape, shape),
        in_specs=[vmem, vmem, vmem],
        out_specs=(vmem, vmem),
        cost_estimate=pl.CostEstimate(
            flops=6 * rows * width, bytes_accessed=8 * rows * width, transcendentals=rows
        ),
    )(residual_mid, ffn_own, gain.reshape(1, width))


def body(
    layer_input,
    q_in,
    k_in,
    v_in,
    segment_ids,
    lambda_parts,
    out_weight,
    ffn_gain,
    gate_weight,
    up_weight,
    down_weight,
    next_gain,
    qkv_weight,
    page_owner,
    page_slot,
):
    row_count = q_in.shape[0]
    feat_width = q_in.shape[1]
    head_dim = feat_width // (2 * HEADS)
    peer_count = lax.axis_size("tok")
    tok_place = lax.axis_index("tok")
    seg_row = segment_ids[0]
    first_row = tok_place * row_count
    query_places = first_row + jnp.arange(row_count)
    query_segs = lax.dynamic_slice_in_dim(seg_row, first_row, row_count)
    lambda_mix = lambda_value(lambda_parts)
    score_scale = 1.0 / math.sqrt(head_dim)
    query_split = q_in.reshape(row_count, HEADS, 2, head_dim)
    run_max = jnp.full((HEADS, 2, row_count), NEG_FILL, jnp.float32)
    back = -(-(MAX_SEG - 1) // row_count)
    own_kv = jnp.concatenate([k_in, v_in], axis=1)
    all_kv = lax.all_gather(own_kv, "tok", axis=0, tiled=True)
    residual_mid = window_attention(
        q_in, all_kv, query_segs, seg_row, first_row, lambda_mix, back, out_weight, layer_input
    )
    gathered = lax.all_gather(residual_mid, "req", axis=0, tiled=True)
    partial = ffn_partial(gathered, ffn_gain, gate_weight, up_weight, down_weight, 512)
    ffn_own = lax.psum_scatter(partial, "req", scatter_dimension=0, tiled=True)
    layer_output, next_normed = finish_rows(residual_mid, ffn_own, next_gain)
    projected_cols = project_rows(
        lax.all_gather(next_normed, "req", axis=0, tiled=True), qkv_weight, 512
    )
    n_req = lax.axis_size("req")
    col_w = projected_cols.shape[1]
    arrived = lax.all_to_all(
        projected_cols.reshape(n_req, row_count, col_w), "req", 0, 0, tiled=True
    )
    projected = jnp.transpose(arrived, (1, 0, 2)).reshape(row_count, n_req * col_w)
    q_next = projected[:, :feat_width]
    pages_dev = row_count // PAGE
    assert pages_dev == peer_count
    key_values = projected[:, feat_width:].reshape(pages_dev, PAGE, 2 * feat_width)
    owner_all = page_owner[0].reshape(peer_count, pages_dev)
    slot_all = page_slot[0].reshape(peer_count, pages_dev)
    numbers = jnp.arange(pages_dev, dtype=jnp.int32)
    my_owners = lax.dynamic_index_in_dim(owner_all, tok_place, 0, keepdims=False)
    send_order = jnp.sum(
        jnp.where(my_owners[None, :] == numbers[:, None], numbers[None, :], 0), axis=1
    )
    outgoing = key_values[send_order].reshape(peer_count, 1, PAGE, 2 * feat_width)
    incoming = lax.all_to_all(outgoing, "tok", split_axis=0, concat_axis=0, tiled=True)
    incoming = incoming.reshape(pages_dev, PAGE, 2 * feat_width)
    slot_list = jnp.sum(jnp.where(owner_all == tok_place, slot_all, 0), axis=1)
    source_of_slot = jnp.sum(
        jnp.where(slot_list[None, :] == numbers[:, None], numbers[None, :], 0), axis=1
    )
    page_cache = incoming[source_of_slot]
    return (layer_output, q_next, page_cache)


def solution(mesh):
    in_specs = (
        P(("req", "tok"), None),
        P(("req", "tok"), None),
        P(("req", "tok"), None),
        P(("req", "tok"), None),
        P("req", None),
        P(),
        P(),
        P(),
        P(None, "req"),
        P(None, "req"),
        P("req", None),
        P(),
        P(None, "req"),
        P("req", None),
        P("req", None),
    )
    out_specs = (P(("req", "tok"), None), P(("req", "tok"), None), P(("req", "tok"), None, None))
    return jax.shard_map(body, mesh=mesh, in_specs=in_specs, out_specs=out_specs, check_vma=False)
```

```python
import functools
import math

import jax
import jax.numpy as jnp
from jax import lax
from jax.experimental import pallas as pl
from jax.experimental.pallas import tpu as pltpu
from jax.sharding import PartitionSpec as P

HEADS = 8
PAGE = 8


NEG_FILL = -1e30
LAMBDA_INIT = 0.2
EPSILON = 1e-05
MAX_SEG = 1024


def rms_rows(values):
    return values * lax.rsqrt(jnp.mean(values * values, axis=-1, keepdims=True) + EPSILON)


def lambda_value(lambda_parts):
    first_term = jnp.exp(jnp.sum(lambda_parts[0] * lambda_parts[1]))
    second_term = jnp.exp(jnp.sum(lambda_parts[2] * lambda_parts[3]))
    return first_term - second_term + LAMBDA_INIT


def attention_kernel(
    back, head_dim, scalars_ref, lam_ref, q_ref, k_ref, v_ref, qseg_ref, kseg_ref, w_ref, base_ref, out_ref, total_ref
):
    rows = q_ref.shape[0]
    span = (back + 1) * rows
    start = pl.multiple_of(scalars_ref[0], rows)
    query_places = scalars_ref[1] + lax.broadcasted_iota(jnp.int32, (rows, span), 0)
    key_places = start + lax.broadcasted_iota(jnp.int32, (rows, span), 1)
    key_segs = kseg_ref[:, pl.ds(start, span)]
    visible = (key_segs == qseg_ref[...]) & (key_places <= query_places)
    score_scale = 1.0 / math.sqrt(head_dim)
    head_w = 2 * head_dim
    head_outs = []
    for head in range(q_ref.shape[1] // head_w):
        values = v_ref[pl.ds(start, span), head * head_w:(head + 1) * head_w]
        map_outputs = []
        for map_index in range(2):
            first = head * head_w + map_index * head_dim
            query_map = q_ref[:, first:first + head_dim]
            key_map = k_ref[pl.ds(start, span), first:first + head_dim]
            scores = (
                lax.dot_general(
                    query_map, key_map, (((1,), (1,)), ((), ())), preferred_element_type=jnp.float32
                )
                * score_scale
            )
            scores = jnp.where(visible, scores, NEG_FILL)
            row_max = jnp.max(scores, axis=1, keepdims=True)
            weights = jnp.exp(scores - row_max)
            totals = jnp.sum(weights, axis=1, keepdims=True)
            map_out = (
                jnp.dot(weights.astype(jnp.bfloat16), values, preferred_element_type=jnp.float32)
                / totals
            )
            map_outputs.append(map_out)
        difference = map_outputs[0] - lam_ref[0] * map_outputs[1]
        head_outs.append((rms_rows(difference) * (1.0 - LAMBDA_INIT)).astype(jnp.bfloat16))
    head_out = jnp.concatenate(head_outs, axis=1)
    step = pl.program_id(0)

    @pl.when(step == 0)
    def _():
        total_ref[...] = jnp.zeros_like(total_ref)

    total_ref[...] += jnp.dot(head_out, w_ref[...], preferred_element_type=jnp.float32)

    @pl.when(step == pl.num_programs(0) - 1)
    def _():
        out_ref[...] = (base_ref[...].astype(jnp.float32) + total_ref[...]).astype(out_ref.dtype)


def window_attention(q_in, all_kv, query_segs, seg_row, first_row, lambda_mix, back, out_weight, base):
    rows, width = q_in.shape
    keys = all_kv.shape[0]
    head_w = width // HEADS
    start = jnp.maximum(first_row - back * rows, 0)
    scalars = jnp.stack([start, first_row]).astype(jnp.int32)
    lam = jnp.reshape(lambda_mix, (1,)).astype(jnp.float32)
    span = (back + 1) * rows
    flops = HEADS * 2 * (2 * rows * span * (head_w // 2) + 2 * rows * span * head_w) + 2 * rows * width * width
    smem = pl.BlockSpec(memory_space=pltpu.SMEM)
    steps = HEADS // 2
    step_w = width // steps
    return pl.pallas_call(
        functools.partial(attention_kernel, back, head_w // 2),
        out_shape=jax.ShapeDtypeStruct((rows, width), jnp.bfloat16),
        grid=(steps,),
        in_specs=[
            smem,
            smem,
            pl.BlockSpec((rows, step_w), lambda h: (0, h)),
            pl.BlockSpec((keys, step_w), lambda h: (0, h)),
            pl.BlockSpec((keys, step_w), lambda h: (0, steps + h)),
            pl.BlockSpec((rows, 1), lambda h: (0, 0)),
            pl.BlockSpec((1, keys), lambda h: (0, 0)),
            pl.BlockSpec((step_w, width), lambda h: (h, 0)),
            pl.BlockSpec((rows, width), lambda h: (0, 0)),
        ],
        out_specs=pl.BlockSpec((rows, width), lambda h: (0, 0)),
        scratch_shapes=[pltpu.VMEM((rows, width), jnp.float32)],
        compiler_params=pltpu.CompilerParams(dimension_semantics=("arbitrary",)),
        cost_estimate=pl.CostEstimate(
            flops=flops,
            bytes_accessed=2 * keys * width * 2 + 3 * rows * width * 2 + width * width * 2,
            transcendentals=HEADS * 2 * rows * span,
        ),
    )(
        scalars,
        lam,
        q_in,
        all_kv,
        all_kv,
        query_segs.reshape(rows, 1),
        seg_row.reshape(1, keys),
        out_weight,
        base,
    )


def ffn_kernel(x_ref, gain_ref, gate_ref, up_ref, down_hbm, out_ref, down_ref, down_sem):
    step = pl.program_id(0)
    fetch = pltpu.make_async_copy(down_hbm, down_ref, down_sem)

    @pl.when(step == 0)
    def _():
        fetch.start()

    normed = (rms_rows(x_ref[...].astype(jnp.float32)) * gain_ref[...]).astype(jnp.bfloat16)
    contract = (((1,), (1,)), ((), ()))
    gate_proj = lax.dot_general(normed, gate_ref[...], contract, preferred_element_type=jnp.float32)
    up_proj = lax.dot_general(normed, up_ref[...], contract, preferred_element_type=jnp.float32)
    hidden = (gate_proj / (1.0 + jnp.exp(-gate_proj)) * up_proj).astype(jnp.bfloat16)

    @pl.when(step == 0)
    def _():
        fetch.wait()

    out_ref[...] = jnp.dot(hidden, down_ref[...], preferred_element_type=jnp.float32).astype(
        out_ref.dtype
    )


def ffn_partial(rows, gain, gate_weight, up_weight, down_weight, tile):
    count, width = rows.shape
    hidden_w = gate_weight.shape[1]
    full = lambda i: (0, 0)
    gate_t = gate_weight.T
    up_t = up_weight.T
    return pl.pallas_call(
        ffn_kernel,
        out_shape=jax.ShapeDtypeStruct((count, width), jnp.bfloat16),
        grid=(count // tile,),
        in_specs=[
            pl.BlockSpec((tile, width), lambda i: (i, 0)),
            pl.BlockSpec((1, width), full),
            pl.BlockSpec((hidden_w, width), full),
            pl.BlockSpec((hidden_w, width), full),
            pl.BlockSpec(memory_space=pl.ANY),
        ],
        out_specs=pl.BlockSpec((tile, width), lambda i: (i, 0)),
        scratch_shapes=[
            pltpu.VMEM((hidden_w, width), down_weight.dtype),
            pltpu.SemaphoreType.DMA(()),
        ],
        compiler_params=pltpu.CompilerParams(
            dimension_semantics=("arbitrary",), vmem_limit_bytes=48 * 1024 * 1024
        ),
        cost_estimate=pl.CostEstimate(
            flops=6 * count * width * hidden_w,
            bytes_accessed=3 * width * hidden_w * 2 + 2 * count * width * 2,
            transcendentals=count * hidden_w,
        ),
    )(rows, gain.reshape(1, width), gate_t, up_t, down_weight)


def project_kernel(x_ref, w_ref, out_ref):
    out_ref[...] = jnp.dot(x_ref[...], w_ref[...], preferred_element_type=jnp.float32).astype(
        out_ref.dtype
    )


def project_rows(rows, weight, tile):
    count, width = rows.shape
    cols = weight.shape[1]
    return pl.pallas_call(
        project_kernel,
        out_shape=jax.ShapeDtypeStruct((count, cols), jnp.bfloat16),
        grid=(count // tile,),
        in_specs=[
            pl.BlockSpec((tile, width), lambda i: (i, 0)),
            pl.BlockSpec((width, cols), lambda i: (0, 0)),
        ],
        out_specs=pl.BlockSpec((tile, cols), lambda i: (i, 0)),
        compiler_params=pltpu.CompilerParams(
            dimension_semantics=("arbitrary",), vmem_limit_bytes=48 * 1024 * 1024
        ),
        cost_estimate=pl.CostEstimate(
            flops=2 * count * width * cols,
            bytes_accessed=2 * (count * width + width * cols + count * cols),
            transcendentals=0,
        ),
    )(rows, weight)


def output_kernel(mid_ref, ffn_ref, gain_ref, out_ref, normed_ref):
    layer_output = (mid_ref[...].astype(jnp.float32) + ffn_ref[...].astype(jnp.float32)).astype(
        out_ref.dtype
    )
    out_ref[...] = layer_output
    normed_ref[...] = (rms_rows(layer_output.astype(jnp.float32)) * gain_ref[...]).astype(
        normed_ref.dtype
    )


def finish_rows(residual_mid, ffn_own, gain):
    rows, width = residual_mid.shape
    vmem = pl.BlockSpec(memory_space=pltpu.VMEM)
    shape = jax.ShapeDtypeStruct((rows, width), jnp.bfloat16)
    return pl.pallas_call(
        output_kernel,
        out_shape=(shape, shape),
        in_specs=[vmem, vmem, vmem],
        out_specs=(vmem, vmem),
        cost_estimate=pl.CostEstimate(
            flops=6 * rows * width, bytes_accessed=8 * rows * width, transcendentals=rows
        ),
    )(residual_mid, ffn_own, gain.reshape(1, width))


def body(
    layer_input,
    q_in,
    k_in,
    v_in,
    segment_ids,
    lambda_parts,
    out_weight,
    ffn_gain,
    gate_weight,
    up_weight,
    down_weight,
    next_gain,
    qkv_weight,
    page_owner,
    page_slot,
):
    row_count = q_in.shape[0]
    feat_width = q_in.shape[1]
    head_dim = feat_width // (2 * HEADS)
    peer_count = lax.axis_size("tok")
    tok_place = lax.axis_index("tok")
    seg_row = segment_ids[0]
    first_row = tok_place * row_count
    query_places = first_row + jnp.arange(row_count)
    query_segs = lax.dynamic_slice_in_dim(seg_row, first_row, row_count)
    lambda_mix = lambda_value(lambda_parts)
    score_scale = 1.0 / math.sqrt(head_dim)
    query_split = q_in.reshape(row_count, HEADS, 2, head_dim)
    run_max = jnp.full((HEADS, 2, row_count), NEG_FILL, jnp.float32)
    back = -(-(MAX_SEG - 1) // row_count)
    own_kv = jnp.concatenate([k_in, v_in], axis=1)
    all_kv = lax.all_gather(own_kv, "tok", axis=0, tiled=True)
    residual_mid = window_attention(
        q_in, all_kv, query_segs, seg_row, first_row, lambda_mix, back, out_weight, layer_input
    )
    gathered = lax.all_gather(residual_mid, "req", axis=0, tiled=True)
    partial = ffn_partial(gathered, ffn_gain, gate_weight, up_weight, down_weight, 1024)
    ffn_own = lax.psum_scatter(partial, "req", scatter_dimension=0, tiled=True)
    layer_output, next_normed = finish_rows(residual_mid, ffn_own, next_gain)
    projected_cols = project_rows(
        lax.all_gather(next_normed, "req", axis=0, tiled=True), qkv_weight, 256
    )
    n_req = lax.axis_size("req")
    col_w = projected_cols.shape[1]
    arrived = lax.all_to_all(
        projected_cols.reshape(n_req, row_count, col_w), "req", 0, 0, tiled=True
    )
    projected = jnp.transpose(arrived, (1, 0, 2)).reshape(row_count, n_req * col_w)
    q_next = projected[:, :feat_width]
    pages_dev = row_count // PAGE
    assert pages_dev == peer_count
    key_values = projected[:, feat_width:].reshape(pages_dev, PAGE, 2 * feat_width)
    owner_all = page_owner[0].reshape(peer_count, pages_dev)
    slot_all = page_slot[0].reshape(peer_count, pages_dev)
    numbers = jnp.arange(pages_dev, dtype=jnp.int32)
    my_owners = lax.dynamic_index_in_dim(owner_all, tok_place, 0, keepdims=False)
    send_order = jnp.sum(
        jnp.where(my_owners[None, :] == numbers[:, None], numbers[None, :], 0), axis=1
    )
    outgoing = key_values[send_order].reshape(peer_count, 1, PAGE, 2 * feat_width)
    incoming = lax.all_to_all(outgoing, "tok", split_axis=0, concat_axis=0, tiled=True)
    incoming = incoming.reshape(pages_dev, PAGE, 2 * feat_width)
    slot_list = jnp.sum(jnp.where(owner_all == tok_place, slot_all, 0), axis=1)
    source_of_slot = jnp.sum(
        jnp.where(slot_list[None, :] == numbers[:, None], numbers[None, :], 0), axis=1
    )
    page_cache = incoming[source_of_slot]
    return (layer_output, q_next, page_cache)


def solution(mesh):
    in_specs = (
        P(("req", "tok"), None),
        P(("req", "tok"), None),
        P(("req", "tok"), None),
        P(("req", "tok"), None),
        P("req", None),
        P(),
        P(),
        P(),
        P(None, "req"),
        P(None, "req"),
        P("req", None),
        P(),
        P(None, "req"),
        P("req", None),
        P("req", None),
    )
    out_specs = (P(("req", "tok"), None), P(("req", "tok"), None), P(("req", "tok"), None, None))
    return jax.shard_map(body, mesh=mesh, in_specs=in_specs, out_specs=out_specs, check_vma=False)
```
